32 devices in a mesh: dp: 4 (over z), seq: 4 (over y, x), fsdp: 2 (over core).
Axes of the slice: x: 2, y: 2, z: 4, core: 2. Of those that a mesh axis runs over, the one named last changes fastest.
Arguments:
- tokens: bfloat16 [4, 4096, 2048], P(None, ('dp', 'seq', 'fsdp')), may hold values from -6 to 6
- cotangent: bfloat16 [4, 4096, 2048], P(None, ('dp', 'seq', 'fsdp')), may hold values from -6 to 6
- segments: int32 [4, 4096], P(None, ('dp', 'seq', 'fsdp')), may hold values from 0 to 3, as said below
- positions: int32 [4, 4096], P(None, ('dp', 'seq', 'fsdp')), may hold values from 0 to 1020, as said below
- w_query: bfloat16 [2048, 2048], P(('dp', 'seq', 'fsdp')), may hold values from -0.125 to 0.125
- w_key: bfloat16 [2048, 128], P(('dp', 'seq', 'fsdp')), may hold values from -0.125 to 0.125
- w_value: bfloat16 [2048, 128], P(('dp', 'seq', 'fsdp')), may hold values from -0.125 to 0.125
- w_out: bfloat16 [2048, 2048], P(('dp', 'seq', 'fsdp')), may hold values from -0.75 to 0.75
- w_gate: bfloat16 [2048, 5632], P(('dp', 'seq', 'fsdp')), may hold values from -0.125 to 0.125
- w_up: bfloat16 [2048, 5632], P(('dp', 'seq', 'fsdp')), may hold values from -0.125 to 0.125
- w_down: bfloat16 [5632, 2048], P(('dp', 'seq', 'fsdp')), may hold values from -0.078125 to 0.078125
- gain_attn: bfloat16 [2048], P(('dp', 'seq', 'fsdp')), may hold values from 0.5 to 1.5
- gain_mlp: bfloat16 [2048], P(('dp', 'seq', 'fsdp')), may hold values from 0.5 to 1.5
Outputs:
- layer_rows: bfloat16 [4, 4096, 2048], P(None, ('dp', 'seq', 'fsdp'))
- shared_keys: bfloat16 [4, 4096, 128], P(None, ('dp', 'seq', 'fsdp'))
- shared_values: bfloat16 [4, 4096, 128], P(None, ('dp', 'seq', 'fsdp'))
- grad_tokens: float32 [4, 4096, 2048], P(None, ('dp', 'seq', 'fsdp'))
- grad_query: float32 [2048, 2048], P(('dp', 'seq', 'fsdp'))
- grad_key: float32 [2048, 128], P(('dp', 'seq', 'fsdp'))
- grad_value: float32 [2048, 128], P(('dp', 'seq', 'fsdp'))
- grad_out: float32 [2048, 2048], P(('dp', 'seq', 'fsdp'))
- grad_gate: float32 [2048, 5632], P(('dp', 'seq', 'fsdp'))
- grad_up: float32 [2048, 5632], P(('dp', 'seq', 'fsdp'))
- grad_down: float32 [5632, 2048], P(('dp', 'seq', 'fsdp'))
- grad_gain_attn: float32 [2048], P(('dp', 'seq', 'fsdp'))
- grad_gain_mlp: float32 [2048], P(('dp', 'seq', 'fsdp'))
The draws below stay inside these ranges and needn't reach their ends.
Inputs may be any that keep to these rules, and one draw needn't show every extreme that they name: `segments`: in each sequence of 1024 consecutive tokens the ids start at 0, never fall, and number its 4 documents. `positions`: A token's place within its document: 0 at a document's first token, one more at each following token.
All inputs are finite; a program needn't handle non-finite values.
Results may differ from the reference program's by a relative error of at most 0.018.
Values may be sent and summed in bfloat16 or wider, within the bound.
A program may use at most 384 MiB of HBM per device.

```python
import math
import jax
import jax.numpy as jnp
from jax import lax

D = 2048
H = 16
HD = 128
FF = 5632
MICRO = 4
DOCS = 4
SEQS = 4
LENGTH = 1024
ROWS = 4096


def document_layout(key):
    base_key = jax.random.fold_in(key, 11)

    def one_sequence(seq_key, fixed_flag):
        shuffled = jax.random.permutation(seq_key, LENGTH - 1) + 1
        packed_cuts = jnp.arange(1, DOCS, dtype=jnp.int32)
        cut_points = jnp.where(fixed_flag, packed_cuts, shuffled[:DOCS - 1].astype(jnp.int32))
        places = jnp.arange(LENGTH, dtype=jnp.int32)
        starts = (places == 0) | jnp.any(places[:, None] == cut_points[None, :], axis=1)
        doc_ids = jnp.cumsum(starts.astype(jnp.int32)) - 1
        begins = lax.cummax(jnp.where(starts, places, 0), axis=0)
        return (doc_ids.astype(jnp.int32), (places - begins).astype(jnp.int32))
    seq_keys = jax.random.split(base_key, MICRO * SEQS)
    fixed_flags = jnp.arange(MICRO * SEQS, dtype=jnp.int32) == 0
    doc_ids, places = jax.vmap(one_sequence)(seq_keys, fixed_flags)
    return (doc_ids.reshape(MICRO, ROWS), places.reshape(MICRO, ROWS))


def draw_segments(key, part):
    return document_layout(key)[0]


def draw_positions(key, part):
    return document_layout(key)[1]


def block_scale(stream_key, dims, cuts, smallest, top_value):
    gain = 1.0
    for position, blocks in cuts:
        draws = jax.random.uniform(jax.random.fold_in(jax.random.fold_in(stream_key, 6), position), (blocks,), jnp.float32, smallest / len(cuts), top_value / len(cuts))
        gain = gain * jnp.repeat(jnp.exp(draws), dims[position] // blocks).reshape((-1,) + (1,) * (len(dims) - 1 - position))
    return gain


def scatter_about(key, shape, deviation, limit, cuts=(), kind=jnp.bfloat16):
    values = jax.random.normal(key, shape, jnp.float32) * deviation
    if len(cuts) > 0:
        values = block_scale(key, shape, cuts, -0.22, 0.18) * values
    return jnp.clip(values, min=-limit, max=limit).astype(kind)


def setup_inputs(seed: int = 0) -> dict:
    keys = jax.random.split(jax.random.key(seed), 14)
    return {
        "tokens": scatter_about(keys[0], (MICRO, ROWS, D), 1.0, 6.0, ((1, 32),)),
        "cotangent": scatter_about(keys[1], (MICRO, ROWS, D), 1.0, 6.0, ((1, 32),)),
        "segments": draw_segments(jax.random.fold_in(keys[13], 71), 0),
        "positions": draw_positions(jax.random.fold_in(keys[13], 71), 0),
        "w_query": scatter_about(keys[4], (D, D), D ** -0.5, 0.125, ((0, 32),)),
        "w_key": scatter_about(keys[5], (D, HD), D ** -0.5, 0.125, ((0, 32),)),
        "w_value": scatter_about(keys[6], (D, HD), D ** -0.5, 0.125, ((0, 32),)),
        "w_out": scatter_about(keys[7], (D, D), (D // 32) ** -0.5, 0.75, ((0, 32),)),
        "w_gate": scatter_about(keys[8], (D, FF), D ** -0.5, 0.125, ((0, 32),)),
        "w_up": scatter_about(keys[9], (D, FF), D ** -0.5, 0.125, ((0, 32),)),
        "w_down": scatter_about(keys[10], (FF, D), FF ** -0.5, 0.078125, ((0, 32),)),
        "gain_attn": jnp.clip(1.0 + 0.1 * jax.random.normal(keys[11], (D,), jnp.float32), 0.5, 1.5).astype(jnp.bfloat16),
        "gain_mlp": jnp.clip(1.0 + 0.1 * jax.random.normal(keys[12], (D,), jnp.float32), 0.5, 1.5).astype(jnp.bfloat16),
    }


@jax.custom_vjp
def low(v):
    return lax.optimization_barrier(v.astype(jnp.bfloat16)).astype(jnp.float32)

@jax.custom_vjp
def low_back(v):
    return v

def low_keep(v):
    return (low(v), None)

def low_pass(kept, grad):
    return (grad,)

def back_keep(v):
    return (v, None)

def back_low(kept, grad):
    return (low(grad),)
low.defvjp(low_keep, low_pass)
low_back.defvjp(back_keep, back_low)
EPSILON = 1e-05
MASKED = -1e+30

def matmul(left, right):
    return jnp.dot(left, right, precision=lax.Precision.HIGHEST, preferred_element_type=jnp.float32)

def rms_norm(vector):
    return vector * lax.rsqrt(lax.optimization_barrier(jnp.mean(vector * vector, axis=-1, keepdims=True)) + EPSILON)

def rope_tables(places, half_dim):
    frequency = jnp.exp(-math.log(10000.0) * jnp.arange(half_dim, dtype=jnp.float32) / half_dim)
    angles = places.astype(jnp.float32)[:, None] * frequency[None, :]
    return (jnp.cos(angles), jnp.sin(angles))

def rotate(vector, cosine, sine_part):
    half_dim = vector.shape[-1] // 2
    first_half = vector[..., :half_dim]
    second_half = vector[..., half_dim:]
    return jnp.concatenate([first_half * cosine - second_half * sine_part, second_half * cosine + first_half * sine_part], axis=-1)

def attend(sequence_item):
    queries, keys_seq, values_seq, documents = sequence_item
    score_scale = 1.0 / math.sqrt(HD)
    scores = low_back(jnp.einsum('qhd,kd->hqk', queries, keys_seq, precision=lax.Precision.HIGHEST) * score_scale)
    places = jnp.arange(queries.shape[0])
    allowed = (documents[:, None] == documents[None, :]) & (places[:, None] >= places[None, :])
    scores = jnp.where(allowed[None], scores, MASKED)
    soft_weights = low(jax.nn.softmax(scores, axis=-1))
    return jnp.einsum('hqk,kd->qhd', soft_weights, values_seq, precision=lax.Precision.HIGHEST)

def reference(tokens, cotangent, segments, positions, w_query, w_key, w_value, w_out, w_gate, w_up, w_down, gain_attn, gain_mlp):
    cosine, sine_part = rope_tables(positions.reshape(-1), HD // 2)
    doc_flat = segments.reshape(-1)

    def forward(rows_in, query_mat, key_mat, value_mat, out_mat, gate_mat, up_mat, down_mat, gain_one, gain_two):
        flat_rows = rows_in.reshape(-1, D)
        normed = low(rms_norm(flat_rows) * gain_one)
        queries = low(rotate(low_back(matmul(normed, query_mat)).reshape(-1, H, HD), cosine[:, None, :], sine_part[:, None, :]))
        keys_all = low(rotate(low_back(matmul(normed, key_mat)), cosine, sine_part))
        values_all = low(low_back(matmul(normed, value_mat)))
        seq_count = flat_rows.shape[0] // LENGTH
        attended = lax.map(jax.checkpoint(attend), (queries.reshape(seq_count, LENGTH, H, HD), keys_all.reshape(seq_count, LENGTH, HD), values_all.reshape(seq_count, LENGTH, HD), doc_flat.reshape(seq_count, LENGTH)))
        mixed = low(low_back(attended.reshape(-1, D)))
        middle = flat_rows + low_back(matmul(mixed, out_mat))
        normed_two = low(rms_norm(middle) * gain_two)
        gate_proj = low_back(matmul(normed_two, gate_mat))
        up_proj = low_back(matmul(normed_two, up_mat))
        hidden = low(jax.nn.silu(gate_proj) * up_proj)
        result = middle + low_back(matmul(hidden, down_mat))
        return (result.reshape(rows_in.shape), (keys_all, values_all))
    result, pullback, shared = jax.vjp(forward, tokens.astype(jnp.float32), w_query.astype(jnp.float32), w_key.astype(jnp.float32), w_value.astype(jnp.float32), w_out.astype(jnp.float32), w_gate.astype(jnp.float32), w_up.astype(jnp.float32), w_down.astype(jnp.float32), gain_attn.astype(jnp.float32), gain_mlp.astype(jnp.float32), has_aux=True)
    grads = pullback(cotangent.astype(jnp.float32))
    keys_out = shared[0].reshape(MICRO, ROWS, HD).astype(jnp.bfloat16)
    values_out = shared[1].reshape(MICRO, ROWS, HD).astype(jnp.bfloat16)
    return (result.astype(jnp.bfloat16), keys_out, values_out, grads[0], grads[1], grads[2], grads[3], grads[4], grads[5], grads[6], grads[7], grads[8], grads[9])
```

```python
import functools
import math

import jax
import jax.numpy as jnp
from jax import lax
from jax.experimental import pallas as pl
from jax.experimental.pallas import tpu as pltpu
from jax.sharding import PartitionSpec as P

EPSILON = 1e-05
MASKED = -1e30


def rope_tables(places, half_dim):
    frequency = jnp.exp(-math.log(10000.0) * jnp.arange(half_dim, dtype=jnp.float32) / half_dim)
    angles = places.astype(jnp.float32)[:, None] * frequency[None, :]
    return (jnp.cos(angles), jnp.sin(angles))


def rotate(vector, cosine, sine_part):
    half_dim = vector.shape[-1] // 2
    first_half = vector[..., :half_dim]
    second_half = vector[..., half_dim:]
    return jnp.concatenate(
        [
            first_half * cosine - second_half * sine_part,
            second_half * cosine + first_half * sine_part,
        ],
        axis=-1,
    )


def norm_back(grad_normed, normed, inverse):
    return inverse * (grad_normed - normed * jnp.mean(grad_normed * normed, axis=-1, keepdims=True))


def mask_scores(scores, query_place, query_segment, key_segment):
    key_place = jnp.arange(key_segment.shape[0], dtype=jnp.int32)
    allowed = (query_segment[:, None] == key_segment[None, :]) & (
        query_place[:, None] >= key_place[None, :]
    )
    return jnp.where(allowed[None], scores, MASKED)


def attend_micro(micro_item, query_place, block_rows, score_scale):
    queries, keys_seq, values_seq, query_segment, key_segment = micro_item
    query_rows, local_heads, head_dim = queries.shape
    blocks = query_rows // block_rows

    def one_block(block_item):
        block_query, block_place, block_segment = block_item
        scores = (
            jnp.einsum("qhd,kd->hqk", block_query, keys_seq, preferred_element_type=jnp.float32)
            * score_scale
        )
        scores = mask_scores(scores, block_place, block_segment, key_segment)
        row_max = jnp.max(scores, axis=-1, keepdims=True)
        log_total = row_max + jnp.log(jnp.sum(jnp.exp(scores - row_max), axis=-1, keepdims=True))
        soft_weights = jnp.exp(scores - log_total).astype(jnp.bfloat16)
        attended = jnp.einsum(
            "hqk,kd->qhd", soft_weights, values_seq, preferred_element_type=jnp.float32
        )
        return (attended.astype(jnp.bfloat16), log_total)

    return lax.map(
        one_block,
        (
            queries.reshape(blocks, block_rows, local_heads, head_dim),
            query_place.reshape(blocks, block_rows),
            query_segment.reshape(blocks, block_rows),
        ),
    )


def attend_back(micro_item, query_place, block_rows, score_scale):
    queries, keys_seq, values_seq, grad_attended, log_total, query_segment, key_segment = micro_item
    query_rows, local_heads, head_dim = queries.shape
    blocks = query_rows // block_rows

    def one_block(running, block_item):
        grad_keys, grad_values = running
        block_query, block_grad, block_total, block_place, block_segment = block_item
        scores = (
            jnp.einsum("qhd,kd->hqk", block_query, keys_seq, preferred_element_type=jnp.float32)
            * score_scale
        )
        scores = mask_scores(scores, block_place, block_segment, key_segment)
        soft_weights = jnp.exp(scores - block_total)
        grad_soft = jnp.einsum(
            "qhd,kd->hqk", block_grad, values_seq, preferred_element_type=jnp.float32
        )
        inner_sum = jnp.sum(soft_weights * grad_soft, axis=-1, keepdims=True)
        grad_scores = (soft_weights * (grad_soft - inner_sum)).astype(jnp.bfloat16)
        grad_queries = (
            jnp.einsum("hqk,kd->qhd", grad_scores, keys_seq, preferred_element_type=jnp.float32)
            * score_scale
        )
        grad_keys = (
            grad_keys
            + jnp.einsum(
                "hqk,qhd->kd", grad_scores, block_query, preferred_element_type=jnp.float32
            )
            * score_scale
        )
        grad_values = grad_values + jnp.einsum(
            "hqk,qhd->kd",
            soft_weights.astype(jnp.bfloat16),
            block_grad,
            preferred_element_type=jnp.float32,
        )
        return ((grad_keys, grad_values), grad_queries)

    zero_init = jnp.zeros(keys_seq.shape, jnp.float32)
    running, grad_queries = lax.scan(
        one_block,
        (zero_init, zero_init),
        (
            queries.reshape(blocks, block_rows, local_heads, head_dim),
            grad_attended.reshape(blocks, block_rows, local_heads, head_dim),
            log_total,
            query_place.reshape(blocks, block_rows),
            query_segment.reshape(blocks, block_rows),
        ),
    )
    return (grad_queries, running[0], running[1])


def body_general(
    tokens,
    cotangent,
    segments,
    positions,
    w_query,
    w_key,
    w_value,
    w_out,
    w_gate,
    w_up,
    w_down,
    gain_attn,
    gain_mlp,
):
    micro_count, tok_rows, model_width = tokens.shape
    head_dim = w_key.shape[1]
    head_count = model_width // head_dim
    seq_size = lax.axis_size("seq")
    pair_size = lax.axis_size("fsdp")
    local_heads = head_count // seq_size
    row_count = micro_count * tok_rows
    query_rows = seq_size * tok_rows
    block_rows = min(512, query_rows)
    score_scale = 1.0 / math.sqrt(head_dim)
    gathered = (
        lax.all_gather(w_query, ("dp", "seq", "fsdp"), axis=0, tiled=True),
        lax.all_gather(w_key, ("dp", "seq", "fsdp"), axis=0, tiled=True),
        lax.all_gather(w_value, ("dp", "seq", "fsdp"), axis=0, tiled=True),
        lax.all_gather(w_out, ("dp", "seq", "fsdp"), axis=0, tiled=True),
        lax.all_gather(w_gate, ("dp", "seq", "fsdp"), axis=0, tiled=True),
        lax.all_gather(w_up, ("dp", "seq", "fsdp"), axis=0, tiled=True),
        lax.all_gather(w_down, ("dp", "seq", "fsdp"), axis=0, tiled=True),
        lax.all_gather(gain_attn, ("dp", "seq", "fsdp"), axis=0, tiled=True),
        lax.all_gather(gain_mlp, ("dp", "seq", "fsdp"), axis=0, tiled=True),
    )
    query_mat, key_mat, value_mat, out_mat, gate_mat, up_mat, down_mat, gain_one, gain_two = (
        gathered
    )
    flat_rows = tokens.reshape(row_count, model_width).astype(jnp.float32)
    inverse_one = lax.rsqrt(jnp.mean(flat_rows * flat_rows, axis=-1, keepdims=True) + EPSILON)
    normed_one = flat_rows * inverse_one
    hidden_one = (normed_one * gain_one.astype(jnp.float32)).astype(jnp.bfloat16)
    cosine, sine_part = rope_tables(positions.reshape(row_count), head_dim // 2)
    query_lin = jnp.dot(hidden_one, query_mat, preferred_element_type=jnp.float32).reshape(
        row_count, head_count, head_dim
    )
    queries = rotate(query_lin, cosine[:, None, :], sine_part[:, None, :]).astype(jnp.bfloat16)
    keys_local = rotate(
        jnp.dot(hidden_one, key_mat, preferred_element_type=jnp.float32), cosine, sine_part
    ).astype(jnp.bfloat16)
    values_local = jnp.dot(hidden_one, value_mat, preferred_element_type=jnp.float32).astype(
        jnp.bfloat16
    )
    keys_local = keys_local.reshape(micro_count, tok_rows, head_dim)
    values_local = values_local.reshape(micro_count, tok_rows, head_dim)
    keys_seq, values_seq, segment_seq = (
        lax.all_gather(keys_local, ("seq", "fsdp"), axis=1, tiled=True),
        lax.all_gather(values_local, ("seq", "fsdp"), axis=1, tiled=True),
        lax.all_gather(segments.astype(jnp.bfloat16), ("seq", "fsdp"), axis=1, tiled=True),
    )
    key_segment = segment_seq.astype(jnp.int32)
    pair_index = lax.axis_index("fsdp")
    query_place = (
        (jnp.arange(seq_size, dtype=jnp.int32)[:, None] * pair_size + pair_index) * tok_rows
        + jnp.arange(tok_rows, dtype=jnp.int32)[None, :]
    ).reshape(query_rows)
    query_segment = lax.dynamic_index_in_dim(
        key_segment.reshape(micro_count, seq_size, pair_size, tok_rows),
        pair_index,
        axis=2,
        keepdims=False,
    ).reshape(micro_count, query_rows)
    head_queries = lax.all_to_all(
        queries.reshape(micro_count, tok_rows, model_width),
        "seq",
        split_axis=2,
        concat_axis=1,
        tiled=True,
    )
    head_queries = head_queries.reshape(micro_count, query_rows, local_heads, head_dim)

    def forward_micro(micro_item):
        return attend_micro(micro_item, query_place, block_rows, score_scale)

    attended, log_total = lax.map(
        forward_micro, (head_queries, keys_seq, values_seq, query_segment, key_segment)
    )
    mixed_rows = lax.all_to_all(
        attended.reshape(micro_count, query_rows, local_heads * head_dim),
        "seq",
        split_axis=1,
        concat_axis=2,
        tiled=True,
    )
    mixed_rows = mixed_rows.reshape(row_count, model_width)
    middle = flat_rows + jnp.dot(mixed_rows, out_mat, preferred_element_type=jnp.float32)
    inverse_two = lax.rsqrt(jnp.mean(middle * middle, axis=-1, keepdims=True) + EPSILON)
    normed_two = middle * inverse_two
    hidden_two = (normed_two * gain_two.astype(jnp.float32)).astype(jnp.bfloat16)
    gate_proj = jnp.dot(hidden_two, gate_mat, preferred_element_type=jnp.float32)
    up_proj = jnp.dot(hidden_two, up_mat, preferred_element_type=jnp.float32)
    gate_sigmoid = jax.nn.sigmoid(gate_proj)
    gate_silu = gate_proj * gate_sigmoid
    hidden_mlp = (gate_silu * up_proj).astype(jnp.bfloat16)
    result = middle + jnp.dot(hidden_mlp, down_mat, preferred_element_type=jnp.float32)
    back_weights = (
        lax.all_gather(w_query, ("dp", "seq", "fsdp"), axis=0, tiled=True),
        lax.all_gather(w_key, ("dp", "seq", "fsdp"), axis=0, tiled=True),
        lax.all_gather(w_value, ("dp", "seq", "fsdp"), axis=0, tiled=True),
        lax.all_gather(w_out, ("dp", "seq", "fsdp"), axis=0, tiled=True),
        lax.all_gather(w_gate, ("dp", "seq", "fsdp"), axis=0, tiled=True),
        lax.all_gather(w_up, ("dp", "seq", "fsdp"), axis=0, tiled=True),
        lax.all_gather(w_down, ("dp", "seq", "fsdp"), axis=0, tiled=True),
        lax.all_gather(gain_attn, ("dp", "seq", "fsdp"), axis=0, tiled=True),
        lax.all_gather(gain_mlp, ("dp", "seq", "fsdp"), axis=0, tiled=True),
    )
    query_mat, key_mat, value_mat, out_mat, gate_mat, up_mat, down_mat, gain_one, gain_two = (
        back_weights
    )
    grad_rows = cotangent.reshape(row_count, model_width).astype(jnp.float32)
    grad_branch = cotangent.reshape(row_count, model_width)
    grad_down_w = jnp.einsum(
        "nf,nd->fd", hidden_mlp, grad_branch, preferred_element_type=jnp.float32
    )
    grad_hidden = jnp.einsum("nd,fd->nf", grad_branch, down_mat, preferred_element_type=jnp.float32)
    grad_gate_pre = (
        grad_hidden * up_proj * gate_sigmoid * (1.0 + gate_proj * (1.0 - gate_sigmoid))
    ).astype(jnp.bfloat16)
    grad_up_pre = (grad_hidden * gate_silu).astype(jnp.bfloat16)
    grad_gate_w = jnp.einsum(
        "nd,nf->df", hidden_two, grad_gate_pre, preferred_element_type=jnp.float32
    )
    grad_up_w = jnp.einsum("nd,nf->df", hidden_two, grad_up_pre, preferred_element_type=jnp.float32)
    grad_hidden_two = jnp.einsum(
        "nf,df->nd", grad_gate_pre, gate_mat, preferred_element_type=jnp.float32
    ) + jnp.einsum("nf,df->nd", grad_up_pre, up_mat, preferred_element_type=jnp.float32)
    grad_gain_two = jnp.sum(grad_hidden_two * normed_two, axis=0)
    grad_middle = grad_rows + norm_back(
        grad_hidden_two * gain_two.astype(jnp.float32), normed_two, inverse_two
    )
    grad_proj = grad_middle.astype(jnp.bfloat16)
    grad_out_w = jnp.einsum("nd,ne->de", mixed_rows, grad_proj, preferred_element_type=jnp.float32)
    grad_mixed = jnp.einsum(
        "ne,de->nd", grad_proj, out_mat, preferred_element_type=jnp.float32
    ).astype(jnp.bfloat16)
    grad_heads = lax.all_to_all(
        grad_mixed.reshape(micro_count, tok_rows, model_width),
        "seq",
        split_axis=2,
        concat_axis=1,
        tiled=True,
    )
    grad_heads = grad_heads.reshape(micro_count, query_rows, local_heads, head_dim)

    def backward_micro(micro_item):
        return attend_back(micro_item, query_place, block_rows, score_scale)

    grad_head_queries, grad_keys_seq, grad_values_seq = lax.map(
        backward_micro,
        (head_queries, keys_seq, values_seq, grad_heads, log_total, query_segment, key_segment),
    )
    grad_query_rows = lax.all_to_all(
        grad_head_queries.reshape(micro_count, query_rows, local_heads * head_dim).astype(
            jnp.bfloat16
        ),
        "seq",
        split_axis=1,
        concat_axis=2,
        tiled=True,
    ).astype(jnp.float32)
    grad_keys_own, grad_values_own = (
        lax.psum_scatter(
            grad_keys_seq.astype(jnp.bfloat16), ("seq", "fsdp"), scatter_dimension=1, tiled=True
        ).astype(jnp.float32),
        lax.psum_scatter(
            grad_values_seq.astype(jnp.bfloat16), ("seq", "fsdp"), scatter_dimension=1, tiled=True
        ).astype(jnp.float32),
    )
    grad_query_lin = (
        rotate(
            grad_query_rows.reshape(row_count, head_count, head_dim),
            cosine[:, None, :],
            -sine_part[:, None, :],
        )
        .reshape(row_count, model_width)
        .astype(jnp.bfloat16)
    )
    grad_key_lin = rotate(grad_keys_own.reshape(row_count, head_dim), cosine, -sine_part).astype(
        jnp.bfloat16
    )
    grad_value_lin = grad_values_own.reshape(row_count, head_dim).astype(jnp.bfloat16)
    grad_query_w = jnp.einsum(
        "nd,ne->de", hidden_one, grad_query_lin, preferred_element_type=jnp.float32
    )
    grad_key_w = jnp.einsum(
        "nd,ne->de", hidden_one, grad_key_lin, preferred_element_type=jnp.float32
    )
    grad_value_w = jnp.einsum(
        "nd,ne->de", hidden_one, grad_value_lin, preferred_element_type=jnp.float32
    )
    grad_hidden_one = jnp.einsum(
        "ne,de->nd", grad_query_lin, query_mat, preferred_element_type=jnp.float32
    )
    grad_hidden_one = grad_hidden_one + jnp.einsum(
        "ne,de->nd", grad_key_lin, key_mat, preferred_element_type=jnp.float32
    )
    grad_hidden_one = grad_hidden_one + jnp.einsum(
        "ne,de->nd", grad_value_lin, value_mat, preferred_element_type=jnp.float32
    )
    grad_gain_one = jnp.sum(grad_hidden_one * normed_one, axis=0)
    grad_input = grad_middle + norm_back(
        grad_hidden_one * gain_one.astype(jnp.float32), normed_one, inverse_one
    )
    matrix_grads = (
        grad_query_w,
        grad_key_w,
        grad_value_w,
        grad_out_w,
        grad_gate_w,
        grad_up_w,
        grad_down_w,
    )
    shards = tuple(
        lax.psum_scatter(
            grad.astype(jnp.bfloat16), ("dp", "seq", "fsdp"), scatter_dimension=0, tiled=True
        ).astype(jnp.float32)
        for grad in matrix_grads
    ) + (
        lax.psum_scatter(grad_gain_one, ("dp", "seq", "fsdp"), scatter_dimension=0, tiled=True),
        lax.psum_scatter(grad_gain_two, ("dp", "seq", "fsdp"), scatter_dimension=0, tiled=True),
    )
    layer_rows = result.reshape(micro_count, tok_rows, model_width).astype(jnp.bfloat16)
    return (
        layer_rows,
        keys_local,
        values_local,
        grad_input.reshape(micro_count, tok_rows, model_width),
        shards[0],
        shards[1],
        shards[2],
        shards[3],
        shards[4],
        shards[5],
        shards[6],
        shards[7],
        shards[8],
    )


BF16 = jnp.bfloat16
F32 = jnp.float32


def dot32(left, right, contract):
    return lax.dot_general(left, right, ((contract[0], contract[1]), ((), ())), preferred_element_type=F32)


def turn(vector, cosine, sine):
    return vector * cosine + pltpu.roll(vector, vector.shape[-1] // 2, 1) * sine


def stack_heads(ref, start, rows, heads, head_dim):
    return jnp.concatenate(
        [ref[pl.ds(start, rows), pl.ds(h * head_dim, head_dim)] for h in range(heads)], axis=0
    )


def masked_block(stacked, keys, query_place, query_segment, key_segment, heads, score_scale):
    rows, extent = query_place.shape[0], keys.shape[0]
    key_place = lax.broadcasted_iota(jnp.int32, (rows, extent), 1)
    allowed = (query_place >= key_place) & (query_segment == key_segment)
    bias = jnp.where(allowed, 0.0, MASKED).astype(F32)
    scores = dot32(stacked, keys, ((1,), (1,))) * score_scale
    scores = (scores.reshape(heads, rows, extent) + bias[None]).reshape(heads * rows, extent)
    row_max = jnp.max(scores, axis=-1, keepdims=True)
    weights = jnp.exp(scores - row_max)
    total = jnp.sum(weights, axis=-1, keepdims=True)
    return weights * (1.0 / total)


def attend_kernel(
    plan,
    query_lin_ref,
    keys_ref,
    values_ref,
    place_ref,
    segment_ref,
    key_segment_ref,
    cosine_ref,
    sine_ref,
    attended_ref,
    queries_ref,
):
    blocks, rows, pair, heads, head_dim, score_scale = plan
    for block in range(blocks):
        start = block * rows
        extent = (block + 1) * pair * rows
        cosine, sine = cosine_ref[pl.ds(start, rows), :], sine_ref[pl.ds(start, rows), :]
        turned = []
        for h in range(heads):
            part = query_lin_ref[pl.ds(start, rows), pl.ds(h * head_dim, head_dim)]
            part = turn(part, cosine, sine).astype(BF16)
            queries_ref[pl.ds(start, rows), pl.ds(h * head_dim, head_dim)] = part
            turned.append(part)
        stacked = jnp.concatenate(turned, axis=0)
        soft = masked_block(
            stacked,
            keys_ref[pl.ds(0, extent), :],
            place_ref[pl.ds(start, rows), :],
            segment_ref[pl.ds(start, rows), :],
            key_segment_ref[:, pl.ds(0, extent)],
            heads,
            score_scale,
        ).astype(BF16)
        mixed = dot32(soft, values_ref[pl.ds(0, extent), :], ((1,), (0,))).astype(BF16)
        for h in range(heads):
            attended_ref[pl.ds(start, rows), pl.ds(h * head_dim, head_dim)] = mixed[
                h * rows : (h + 1) * rows
            ]


def attend_back_kernel(
    plan,
    queries_ref,
    grad_ref,
    keys_ref,
    values_ref,
    place_ref,
    segment_ref,
    key_segment_ref,
    cosine_ref,
    sine_ref,
    grad_lin_ref,
    grad_keys_ref,
    grad_values_ref,
):
    blocks, rows, pair, heads, head_dim, score_scale = plan

    @pl.when(pl.program_id(0) == 0)
    def _():
        grad_keys_ref[...] = jnp.zeros_like(grad_keys_ref)
        grad_values_ref[...] = jnp.zeros_like(grad_values_ref)

    for block in range(blocks):
        start = block * rows
        extent = (block + 1) * pair * rows
        stacked = stack_heads(queries_ref, start, rows, heads, head_dim)
        grads = stack_heads(grad_ref, start, rows, heads, head_dim)
        keys = keys_ref[pl.ds(0, extent), :]
        values = values_ref[pl.ds(0, extent), :]
        soft = masked_block(
            stacked,
            keys,
            place_ref[pl.ds(start, rows), :],
            segment_ref[pl.ds(start, rows), :],
            key_segment_ref[:, pl.ds(0, extent)],
            heads,
            score_scale,
        )
        grad_soft = dot32(grads, values, ((1,), (1,)))
        inner = jnp.sum(soft * grad_soft, axis=-1, keepdims=True)
        grad_scores = (soft * (grad_soft - inner)).astype(BF16)
        grad_values_ref[pl.ds(0, extent), :] += dot32(soft.astype(BF16), grads, ((0,), (0,)))
        grad_keys_ref[pl.ds(0, extent), :] += (
            dot32(grad_scores, stacked, ((0,), (0,))) * score_scale
        )
        grad_queries = dot32(grad_scores, keys, ((1,), (0,))) * score_scale
        cosine, sine = cosine_ref[pl.ds(start, rows), :], sine_ref[pl.ds(start, rows), :]
        for h in range(heads):
            part = turn(grad_queries[h * rows : (h + 1) * rows], cosine, -sine)
            grad_lin_ref[pl.ds(start, rows), pl.ds(h * head_dim, head_dim)] = part.astype(BF16)


def whole(shape):
    return pl.BlockSpec(shape, lambda g: (0,) * len(shape))


def attention_call(kernel, plan, groups, wide, narrow, outs, name, flops):
    rows = wide[0].shape[0]
    group = wide[0].shape[1] // groups
    column = pl.BlockSpec((rows, group), lambda g: (0, g))
    return pl.pallas_call(
        functools.partial(kernel, plan),
        grid=(groups,),
        in_specs=[column] * len(wide) + [whole(a.shape) for a in narrow],
        out_specs=[column if a.shape[0] == rows else whole(a.shape) for a in outs],
        out_shape=outs,
        compiler_params=pltpu.CompilerParams(vmem_limit_bytes=48 * 1024 * 1024),
        cost_estimate=pl.CostEstimate(
            flops=flops, bytes_accessed=6 * rows * wide[0].shape[1], transcendentals=flops // 512
        ),
        name=name,
    )(*wide, *narrow)


def gather(value, axes, dim):
    return lax.all_gather(value, axes, axis=dim, tiled=True)


def scatter_sum(value, axes, dim):
    return lax.psum_scatter(value, axes, scatter_dimension=dim, tiled=True)


def send_plane(value, step):
    return lax.ppermute(value, "seq", [(i, i ^ step) for i in range(4)])


def send_line(value, step):
    size = lax.axis_size("dp")
    return lax.ppermute(value, "dp", [(i, (i + step) % size) for i in range(size)])


def send_core(value):
    return lax.ppermute(value, "fsdp", [(0, 1), (1, 0)])


def block_of(value, index, dim=0):
    return lax.dynamic_index_in_dim(value, index, axis=dim, keepdims=False)


def put_block(value, block, index, dim=0):
    return lax.dynamic_update_index_in_dim(value, block, index, axis=dim)


def swap_blocks(value, own):
    out = value
    for step in (1, 2, 3):
        other = own ^ step
        out = put_block(out, send_plane(block_of(value, other), step), other)
    return out


def gather_plane(value):
    half = value.shape[-1] // 2
    by_x, by_y = send_plane(value, 1), send_plane(value, 2)
    far = jnp.concatenate(
        [send_plane(by_x[..., :half], 2), send_plane(by_y[..., half:], 1)], axis=-1
    )
    return jnp.concatenate([value, by_x, by_y, far], axis=0)


def scatter_plane(value):
    half = value.shape[-1] // 2
    left, right = value[..., :half], value[..., half:]
    got = send_plane(jnp.stack([left[1], left[3]]), 1).astype(F32)
    passed = send_plane((left[2].astype(F32) + got[1]).astype(BF16), 2).astype(F32)
    left = left[0].astype(F32) + got[0] + passed
    got = send_plane(right[2:], 2).astype(F32)
    passed = send_plane((right[1].astype(F32) + got[1]).astype(BF16), 1).astype(F32)
    right = right[0].astype(F32) + got[0] + passed
    return jnp.concatenate([left, right], axis=-1)


def gather_line(value, plane):
    size = lax.axis_size("dp")
    out = jnp.zeros((size,) + value.shape, value.dtype)
    out = put_block(out, value, plane)
    for step in range(1, size):
        out = put_block(out, send_line(value, step), (plane + size - step) % size)
    return out


def scatter_line(value, plane):
    size = lax.axis_size("dp")
    total = block_of(value, plane).astype(F32)
    for step in range(1, size):
        total = total + send_line(block_of(value, (plane + step) % size), step).astype(F32)
    return total


def gather_core(value, core, dim):
    other = send_core(value)
    first = jnp.where(core == 0, value, other)
    second = jnp.where(core == 0, other, value)
    return jnp.stack([first, second], axis=dim)


def scatter_core(value, core, dim):
    other = send_core(block_of(value, 1 - core, dim))
    return (block_of(value, core, dim).astype(F32) + other.astype(F32)).astype(BF16)


def scatter_every(value, plane, own, core):
    planes, chips, pair, shard, columns = value.shape
    value = scatter_core(value, core, 2)
    blocks = jnp.stack([block_of(value, own ^ step, 1) for step in range(chips)])
    value = scatter_plane(blocks).astype(BF16)
    return scatter_line(value, plane)


def body_plane(
    tokens,
    cotangent,
    segments,
    positions,
    w_query,
    w_key,
    w_value,
    w_out,
    w_gate,
    w_up,
    w_down,
    gain_attn,
    gain_mlp,
):
    micro, tile, width = tokens.shape
    head_dim = w_key.shape[1]
    head_count = width // head_dim
    planes = lax.axis_size("dp")
    chips = lax.axis_size("seq")
    pair = lax.axis_size("fsdp")
    plane = lax.axis_index("dp")
    own = lax.axis_index("seq")
    core = lax.axis_index("fsdp")
    rows = micro * tile
    hidden = w_gate.shape[1]
    shard = w_query.shape[0]
    own_hidden = hidden // chips
    piece = own_hidden // planes
    qkv = width + 2 * head_dim
    score_scale = 1.0 / math.sqrt(head_dim)
    every = ("dp", "seq", "fsdp")

    gains = jnp.stack([gain_attn, gain_mlp], axis=1)
    gains = jnp.pad(gains, ((0, 0), (0, head_dim - 2)))
    w_qkv = gather(jnp.concatenate([w_query, w_key, w_value, gains], axis=1), every, 0)
    out_mat = gather(w_out, every, 0)
    gate_up = jnp.stack([w_gate, w_up], axis=1).reshape(shard, 2, planes, chips, piece)
    gate_up = gate_up.transpose(3, 0, 1, 2, 4).reshape(chips, shard, 2 * own_hidden)
    w_qkv, gate_up, w_down = lax.optimization_barrier((w_qkv, gate_up, w_down))
    gate_up = swap_blocks(gate_up, own)
    gate_up = gather_core(gate_up, core, 1).reshape(pair, -1, 2 * own_hidden)
    gate_up_half = gather_line(block_of(gate_up, core), plane)
    gate_up = gather_core(gate_up_half, core, 1).reshape(width, 2 * own_hidden)
    down_mat = gather_core(gather_line(w_down, plane), core, 1).reshape(own_hidden, width)
    grads_in = gather(cotangent, "seq", 1).reshape(chips, rows, width)
    grads_in = jnp.concatenate([block_of(grads_in, own ^ step) for step in range(chips)])

    gain_one, gain_two = w_qkv[:, qkv].astype(F32), w_qkv[:, qkv + 1].astype(F32)
    w_qkv = w_qkv[:, :qkv]

    x_rows = swap_blocks(tokens, own).reshape(rows, width).astype(F32)
    marks = swap_blocks(jnp.stack([segments, positions], axis=1), own)
    segment_own, place_doc = marks[:, 0], marks[:, 1].reshape(rows)
    key_segment = gather_core(segment_own, core, 1).reshape(1, rows * pair)
    query_place = (
        (jnp.arange(chips, dtype=jnp.int32)[:, None] * pair + core) * tile
        + jnp.arange(tile, dtype=jnp.int32)[None, :]
    ).reshape(rows, 1)
    query_segment = segment_own.reshape(rows, 1)
    cosine, sine = rope_tables(place_doc, head_dim // 2)
    cosine = jnp.concatenate([cosine, cosine], axis=1)
    sine = jnp.concatenate([-sine, sine], axis=1)

    inverse_one = lax.rsqrt(jnp.mean(x_rows * x_rows, axis=-1, keepdims=True) + EPSILON)
    normed_one = x_rows * inverse_one
    hidden_one = (normed_one * gain_one).astype(BF16)
    lin = jnp.dot(hidden_one, w_qkv, preferred_element_type=F32)
    query_lin, key_lin, value_lin = (
        lin[:, :width],
        lin[:, width : width + head_dim],
        lin[:, width + head_dim :],
    )
    keys_own = (key_lin * cosine + jnp.roll(key_lin, head_dim // 2, axis=1) * sine).astype(BF16)
    values_own = value_lin.astype(BF16)
    kv_own = jnp.concatenate([keys_own, values_own], axis=1).reshape(chips, tile, 2 * head_dim)
    kv = gather_core(kv_own, core, 1).reshape(rows * pair, 2 * head_dim)
    keys, values = kv[:, :head_dim], kv[:, head_dim:]
    kv_home = swap_blocks(kv_own, own)
    groups = max(1, head_count // 4)
    heads = head_count // groups
    plan = (chips, tile, pair, heads, head_dim, score_scale)
    pairs_seen = tile * tile * pair * chips * (chips + 1) // 2 * head_count * head_dim
    narrow = (keys, values, query_place, query_segment, key_segment, cosine, sine)
    attended, queries = attention_call(
        attend_kernel,
        plan,
        groups,
        (query_lin,),
        narrow,
        [jax.ShapeDtypeStruct((rows, width), BF16)] * 2,
        "attend",
        4 * pairs_seen,
    )
    middle = x_rows + jnp.dot(attended, out_mat, preferred_element_type=F32)
    inverse_two = lax.rsqrt(jnp.mean(middle * middle, axis=-1, keepdims=True) + EPSILON)
    normed_two = middle * inverse_two
    hidden_two = (normed_two * gain_two).astype(BF16)

    plane_two = gather_plane(hidden_two)
    gate_up_lin = jnp.dot(plane_two, gate_up, preferred_element_type=F32)
    gate_proj, up_proj = gate_up_lin[:, :own_hidden], gate_up_lin[:, own_hidden:]
    gate_sigmoid = jax.nn.sigmoid(gate_proj)
    gate_silu = gate_proj * gate_sigmoid
    hidden_mlp = (gate_silu * up_proj).astype(BF16)
    partial_out = jnp.dot(hidden_mlp, down_mat, preferred_element_type=F32).astype(BF16)
    result = middle + scatter_plane(partial_out.reshape(chips, rows, width))
    layer_rows = swap_blocks(result.astype(BF16).reshape(chips, tile, width), own)

    grad_hidden = dot32(grads_in, down_mat, ((1,), (1,)))
    grad_gate_pre = (
        grad_hidden * up_proj * gate_sigmoid * (1.0 + gate_proj * (1.0 - gate_sigmoid))
    ).astype(BF16)
    grad_up_pre = (grad_hidden * gate_silu).astype(BF16)
    grad_pre = jnp.concatenate([grad_gate_pre, grad_up_pre], axis=1)
    partial_two = dot32(grad_pre, gate_up, ((1,), (1,))).astype(BF16)
    grad_hidden_two = scatter_plane(partial_two.reshape(chips, rows, width))
    grad_gate_up = dot32(plane_two, grad_pre, ((0,), (0,))).astype(BF16)
    grad_down = dot32(hidden_mlp, grads_in, ((0,), (0,))).astype(BF16)

    grad_down = scatter_core(grad_down.reshape(planes, pair, -1, width), core, 1)
    grad_down = scatter_line(grad_down, plane)
    grad_gate_up = scatter_core(
        grad_gate_up.reshape(planes, chips, pair, shard, 2 * own_hidden), core, 2
    )
    grad_gate_up = scatter_line(grad_gate_up, plane).astype(BF16)
    grad_gate_up = swap_blocks(grad_gate_up, own).reshape(chips, shard, 2, planes, piece)
    grad_gate_up = grad_gate_up.transpose(2, 1, 3, 0, 4).reshape(2, shard, hidden).astype(F32)

    grad_gain_two = jnp.sum(grad_hidden_two * normed_two, axis=0)
    grad_rows = grads_in[:rows].astype(F32)
    grad_middle = grad_rows + norm_back(grad_hidden_two * gain_two, normed_two, inverse_two)
    grad_proj = grad_middle.astype(BF16)
    grad_mixed = dot32(grad_proj, out_mat, ((1,), (1,))).astype(BF16)
    grad_query_lin, grad_keys, grad_values = attention_call(
        attend_back_kernel,
        plan,
        groups,
        (queries, grad_mixed),
        narrow,
        [
            jax.ShapeDtypeStruct((rows, width), BF16),
            jax.ShapeDtypeStruct((rows * pair, head_dim), F32),
            jax.ShapeDtypeStruct((rows * pair, head_dim), F32),
        ],
        "attend_back",
        10 * pairs_seen,
    )
    grad_kv = jnp.concatenate([grad_keys, grad_values], axis=1)
    grad_kv = grad_kv.reshape(chips, pair, tile, 2 * head_dim)
    grad_kv = block_of(grad_kv, core, 1) + send_core(block_of(grad_kv, 1 - core, 1))
    grad_kv = grad_kv.reshape(rows, 2 * head_dim)
    grad_keys = grad_kv[:, :head_dim]
    grad_keys = grad_keys * cosine - jnp.roll(grad_keys, head_dim // 2, axis=1) * sine
    grad_lin = jnp.concatenate(
        [grad_query_lin, grad_keys.astype(BF16), grad_kv[:, head_dim:].astype(BF16)], axis=1
    )
    grad_out = dot32(attended, grad_proj, ((0,), (0,))).astype(BF16)
    grad_hidden_one = dot32(grad_lin, w_qkv, ((1,), (1,)))
    grad_gain_one = jnp.sum(grad_hidden_one * normed_one, axis=0)
    grad_input = grad_middle + norm_back(grad_hidden_one * gain_one, normed_one, inverse_one)
    grad_input = swap_blocks(grad_input.astype(BF16).reshape(chips, tile, width), own)
    grad_out = scatter_every(grad_out.reshape(planes, chips, pair, shard, width), plane, own, core)
    grad_gains = jnp.pad(
        jnp.stack([grad_gain_one, grad_gain_two], axis=1), ((0, 0), (0, head_dim - 2))
    )
    grad_qkv = dot32(hidden_one, grad_lin, ((0,), (0,)))
    grad_qkv = jnp.concatenate([grad_qkv, grad_gains], axis=1).astype(BF16)
    grad_qkv = grad_qkv.reshape(planes, chips, pair, shard, qkv + head_dim)
    grad_qkv = scatter_every(grad_qkv, plane, own, core)
    return (
        layer_rows,
        kv_home[..., :head_dim],
        kv_home[..., head_dim:],
        grad_input.astype(F32),
        grad_qkv[:, :width],
        grad_qkv[:, width : width + head_dim],
        grad_qkv[:, width + head_dim : qkv],
        grad_out,
        grad_gate_up[0],
        grad_gate_up[1],
        grad_down,
        grad_qkv[:, qkv],
        grad_qkv[:, qkv + 1],
    )


def body(tokens, *rest):
    if tokens.shape[0] == lax.axis_size("seq") == 4 and lax.axis_size("fsdp") == 2:
        return body_plane(tokens, *rest)
    return body_general(tokens, *rest)


def solution(mesh):
    in_specs = (
        P(None, ("dp", "seq", "fsdp"), None),
        P(None, ("dp", "seq", "fsdp"), None),
        P(None, ("dp", "seq", "fsdp")),
        P(None, ("dp", "seq", "fsdp")),
        P(("dp", "seq", "fsdp"), None),
        P(("dp", "seq", "fsdp"), None),
        P(("dp", "seq", "fsdp"), None),
        P(("dp", "seq", "fsdp"), None),
        P(("dp", "seq", "fsdp"), None),
        P(("dp", "seq", "fsdp"), None),
        P(("dp", "seq", "fsdp"), None),
        P(("dp", "seq", "fsdp")),
        P(("dp", "seq", "fsdp")),
    )
    out_specs = (
        P(None, ("dp", "seq", "fsdp"), None),
        P(None, ("dp", "seq", "fsdp"), None),
        P(None, ("dp", "seq", "fsdp"), None),
        P(None, ("dp", "seq", "fsdp"), None),
        P(("dp", "seq", "fsdp"), None),
        P(("dp", "seq", "fsdp"), None),
        P(("dp", "seq", "fsdp"), None),
        P(("dp", "seq", "fsdp"), None),
        P(("dp", "seq", "fsdp"), None),
        P(("dp", "seq", "fsdp"), None),
        P(("dp", "seq", "fsdp"), None),
        P(("dp", "seq", "fsdp")),
        P(("dp", "seq", "fsdp")),
    )
    return jax.shard_map(body, mesh=mesh, in_specs=in_specs, out_specs=out_specs, check_vma=False)
```

```python
import functools
import math

import jax
import jax.numpy as jnp
from jax import lax
from jax.experimental import pallas as pl
from jax.experimental.pallas import tpu as pltpu
from jax.sharding import PartitionSpec as P

EPSILON = 1e-05
MASKED = -1e30


def rope_tables(places, half_dim):
    frequency = jnp.exp(-math.log(10000.0) * jnp.arange(half_dim, dtype=jnp.float32) / half_dim)
    angles = places.astype(jnp.float32)[:, None] * frequency[None, :]
    return (jnp.cos(angles), jnp.sin(angles))


def rotate(vector, cosine, sine_part):
    half_dim = vector.shape[-1] // 2
    first_half = vector[..., :half_dim]
    second_half = vector[..., half_dim:]
    return jnp.concatenate(
        [
            first_half * cosine - second_half * sine_part,
            second_half * cosine + first_half * sine_part,
        ],
        axis=-1,
    )


def norm_back(grad_normed, normed, inverse):
    return inverse * (grad_normed - normed * jnp.mean(grad_normed * normed, axis=-1, keepdims=True))


def mask_scores(scores, query_place, query_segment, key_segment):
    key_place = jnp.arange(key_segment.shape[0], dtype=jnp.int32)
    allowed = (query_segment[:, None] == key_segment[None, :]) & (
        query_place[:, None] >= key_place[None, :]
    )
    return jnp.where(allowed[None], scores, MASKED)


def attend_micro(micro_item, query_place, block_rows, score_scale):
    queries, keys_seq, values_seq, query_segment, key_segment = micro_item
    query_rows, local_heads, head_dim = queries.shape
    blocks = query_rows // block_rows

    def one_block(block_item):
        block_query, block_place, block_segment = block_item
        scores = (
            jnp.einsum("qhd,kd->hqk", block_query, keys_seq, preferred_element_type=jnp.float32)
            * score_scale
        )
        scores = mask_scores(scores, block_place, block_segment, key_segment)
        row_max = jnp.max(scores, axis=-1, keepdims=True)
        log_total = row_max + jnp.log(jnp.sum(jnp.exp(scores - row_max), axis=-1, keepdims=True))
        soft_weights = jnp.exp(scores - log_total).astype(jnp.bfloat16)
        attended = jnp.einsum(
            "hqk,kd->qhd", soft_weights, values_seq, preferred_element_type=jnp.float32
        )
        return (attended.astype(jnp.bfloat16), log_total)

    return lax.map(
        one_block,
        (
            queries.reshape(blocks, block_rows, local_heads, head_dim),
            query_place.reshape(blocks, block_rows),
            query_segment.reshape(blocks, block_rows),
        ),
    )


def attend_back(micro_item, query_place, block_rows, score_scale):
    queries, keys_seq, values_seq, grad_attended, log_total, query_segment, key_segment = micro_item
    query_rows, local_heads, head_dim = queries.shape
    blocks = query_rows // block_rows

    def one_block(running, block_item):
        grad_keys, grad_values = running
        block_query, block_grad, block_total, block_place, block_segment = block_item
        scores = (
            jnp.einsum("qhd,kd->hqk", block_query, keys_seq, preferred_element_type=jnp.float32)
            * score_scale
        )
        scores = mask_scores(scores, block_place, block_segment, key_segment)
        soft_weights = jnp.exp(scores - block_total)
        grad_soft = jnp.einsum(
            "qhd,kd->hqk", block_grad, values_seq, preferred_element_type=jnp.float32
        )
        inner_sum = jnp.sum(soft_weights * grad_soft, axis=-1, keepdims=True)
        grad_scores = (soft_weights * (grad_soft - inner_sum)).astype(jnp.bfloat16)
        grad_queries = (
            jnp.einsum("hqk,kd->qhd", grad_scores, keys_seq, preferred_element_type=jnp.float32)
            * score_scale
        )
        grad_keys = (
            grad_keys
            + jnp.einsum(
                "hqk,qhd->kd", grad_scores, block_query, preferred_element_type=jnp.float32
            )
            * score_scale
        )
        grad_values = grad_values + jnp.einsum(
            "hqk,qhd->kd",
            soft_weights.astype(jnp.bfloat16),
            block_grad,
            preferred_element_type=jnp.float32,
        )
        return ((grad_keys, grad_values), grad_queries)

    zero_init = jnp.zeros(keys_seq.shape, jnp.float32)
    running, grad_queries = lax.scan(
        one_block,
        (zero_init, zero_init),
        (
            queries.reshape(blocks, block_rows, local_heads, head_dim),
            grad_attended.reshape(blocks, block_rows, local_heads, head_dim),
            log_total,
            query_place.reshape(blocks, block_rows),
            query_segment.reshape(blocks, block_rows),
        ),
    )
    return (grad_queries, running[0], running[1])


def body_general(
    tokens,
    cotangent,
    segments,
    positions,
    w_query,
    w_key,
    w_value,
    w_out,
    w_gate,
    w_up,
    w_down,
    gain_attn,
    gain_mlp,
):
    micro_count, tok_rows, model_width = tokens.shape
    head_dim = w_key.shape[1]
    head_count = model_width // head_dim
    seq_size = lax.axis_size("seq")
    pair_size = lax.axis_size("fsdp")
    local_heads = head_count // seq_size
    row_count = micro_count * tok_rows
    query_rows = seq_size * tok_rows
    block_rows = min(512, query_rows)
    score_scale = 1.0 / math.sqrt(head_dim)
    gathered = (
        lax.all_gather(w_query, ("dp", "seq", "fsdp"), axis=0, tiled=True),
        lax.all_gather(w_key, ("dp", "seq", "fsdp"), axis=0, tiled=True),
        lax.all_gather(w_value, ("dp", "seq", "fsdp"), axis=0, tiled=True),
        lax.all_gather(w_out, ("dp", "seq", "fsdp"), axis=0, tiled=True),
        lax.all_gather(w_gate, ("dp", "seq", "fsdp"), axis=0, tiled=True),
        lax.all_gather(w_up, ("dp", "seq", "fsdp"), axis=0, tiled=True),
        lax.all_gather(w_down, ("dp", "seq", "fsdp"), axis=0, tiled=True),
        lax.all_gather(gain_attn, ("dp", "seq", "fsdp"), axis=0, tiled=True),
        lax.all_gather(gain_mlp, ("dp", "seq", "fsdp"), axis=0, tiled=True),
    )
    query_mat, key_mat, value_mat, out_mat, gate_mat, up_mat, down_mat, gain_one, gain_two = (
        gathered
    )
    flat_rows = tokens.reshape(row_count, model_width).astype(jnp.float32)
    inverse_one = lax.rsqrt(jnp.mean(flat_rows * flat_rows, axis=-1, keepdims=True) + EPSILON)
    normed_one = flat_rows * inverse_one
    hidden_one = (normed_one * gain_one.astype(jnp.float32)).astype(jnp.bfloat16)
    cosine, sine_part = rope_tables(positions.reshape(row_count), head_dim // 2)
    query_lin = jnp.dot(hidden_one, query_mat, preferred_element_type=jnp.float32).reshape(
        row_count, head_count, head_dim
    )
    queries = rotate(query_lin, cosine[:, None, :], sine_part[:, None, :]).astype(jnp.bfloat16)
    keys_local = rotate(
        jnp.dot(hidden_one, key_mat, preferred_element_type=jnp.float32), cosine, sine_part
    ).astype(jnp.bfloat16)
    values_local = jnp.dot(hidden_one, value_mat, preferred_element_type=jnp.float32).astype(
        jnp.bfloat16
    )
    keys_local = keys_local.reshape(micro_count, tok_rows, head_dim)
    values_local = values_local.reshape(micro_count, tok_rows, head_dim)
    keys_seq, values_seq, segment_seq = (
        lax.all_gather(keys_local, ("seq", "fsdp"), axis=1, tiled=True),
        lax.all_gather(values_local, ("seq", "fsdp"), axis=1, tiled=True),
        lax.all_gather(segments.astype(jnp.bfloat16), ("seq", "fsdp"), axis=1, tiled=True),
    )
    key_segment = segment_seq.astype(jnp.int32)
    pair_index = lax.axis_index("fsdp")
    query_place = (
        (jnp.arange(seq_size, dtype=jnp.int32)[:, None] * pair_size + pair_index) * tok_rows
        + jnp.arange(tok_rows, dtype=jnp.int32)[None, :]
    ).reshape(query_rows)
    query_segment = lax.dynamic_index_in_dim(
        key_segment.reshape(micro_count, seq_size, pair_size, tok_rows),
        pair_index,
        axis=2,
        keepdims=False,
    ).reshape(micro_count, query_rows)
    head_queries = lax.all_to_all(
        queries.reshape(micro_count, tok_rows, model_width),
        "seq",
        split_axis=2,
        concat_axis=1,
        tiled=True,
    )
    head_queries = head_queries.reshape(micro_count, query_rows, local_heads, head_dim)

    def forward_micro(micro_item):
        return attend_micro(micro_item, query_place, block_rows, score_scale)

    attended, log_total = lax.map(
        forward_micro, (head_queries, keys_seq, values_seq, query_segment, key_segment)
    )
    mixed_rows = lax.all_to_all(
        attended.reshape(micro_count, query_rows, local_heads * head_dim),
        "seq",
        split_axis=1,
        concat_axis=2,
        tiled=True,
    )
    mixed_rows = mixed_rows.reshape(row_count, model_width)
    middle = flat_rows + jnp.dot(mixed_rows, out_mat, preferred_element_type=jnp.float32)
    inverse_two = lax.rsqrt(jnp.mean(middle * middle, axis=-1, keepdims=True) + EPSILON)
    normed_two = middle * inverse_two
    hidden_two = (normed_two * gain_two.astype(jnp.float32)).astype(jnp.bfloat16)
    gate_proj = jnp.dot(hidden_two, gate_mat, preferred_element_type=jnp.float32)
    up_proj = jnp.dot(hidden_two, up_mat, preferred_element_type=jnp.float32)
    gate_sigmoid = jax.nn.sigmoid(gate_proj)
    gate_silu = gate_proj * gate_sigmoid
    hidden_mlp = (gate_silu * up_proj).astype(jnp.bfloat16)
    result = middle + jnp.dot(hidden_mlp, down_mat, preferred_element_type=jnp.float32)
    back_weights = (
        lax.all_gather(w_query, ("dp", "seq", "fsdp"), axis=0, tiled=True),
        lax.all_gather(w_key, ("dp", "seq", "fsdp"), axis=0, tiled=True),
        lax.all_gather(w_value, ("dp", "seq", "fsdp"), axis=0, tiled=True),
        lax.all_gather(w_out, ("dp", "seq", "fsdp"), axis=0, tiled=True),
        lax.all_gather(w_gate, ("dp", "seq", "fsdp"), axis=0, tiled=True),
        lax.all_gather(w_up, ("dp", "seq", "fsdp"), axis=0, tiled=True),
        lax.all_gather(w_down, ("dp", "seq", "fsdp"), axis=0, tiled=True),
        lax.all_gather(gain_attn, ("dp", "seq", "fsdp"), axis=0, tiled=True),
        lax.all_gather(gain_mlp, ("dp", "seq", "fsdp"), axis=0, tiled=True),
    )
    query_mat, key_mat, value_mat, out_mat, gate_mat, up_mat, down_mat, gain_one, gain_two = (
        back_weights
    )
    grad_rows = cotangent.reshape(row_count, model_width).astype(jnp.float32)
    grad_branch = cotangent.reshape(row_count, model_width)
    grad_down_w = jnp.einsum(
        "nf,nd->fd", hidden_mlp, grad_branch, preferred_element_type=jnp.float32
    )
    grad_hidden = jnp.einsum("nd,fd->nf", grad_branch, down_mat, preferred_element_type=jnp.float32)
    grad_gate_pre = (
        grad_hidden * up_proj * gate_sigmoid * (1.0 + gate_proj * (1.0 - gate_sigmoid))
    ).astype(jnp.bfloat16)
    grad_up_pre = (grad_hidden * gate_silu).astype(jnp.bfloat16)
    grad_gate_w = jnp.einsum(
        "nd,nf->df", hidden_two, grad_gate_pre, preferred_element_type=jnp.float32
    )
    grad_up_w = jnp.einsum("nd,nf->df", hidden_two, grad_up_pre, preferred_element_type=jnp.float32)
    grad_hidden_two = jnp.einsum(
        "nf,df->nd", grad_gate_pre, gate_mat, preferred_element_type=jnp.float32
    ) + jnp.einsum("nf,df->nd", grad_up_pre, up_mat, preferred_element_type=jnp.float32)
    grad_gain_two = jnp.sum(grad_hidden_two * normed_two, axis=0)
    grad_middle = grad_rows + norm_back(
        grad_hidden_two * gain_two.astype(jnp.float32), normed_two, inverse_two
    )
    grad_proj = grad_middle.astype(jnp.bfloat16)
    grad_out_w = jnp.einsum("nd,ne->de", mixed_rows, grad_proj, preferred_element_type=jnp.float32)
    grad_mixed = jnp.einsum(
        "ne,de->nd", grad_proj, out_mat, preferred_element_type=jnp.float32
    ).astype(jnp.bfloat16)
    grad_heads = lax.all_to_all(
        grad_mixed.reshape(micro_count, tok_rows, model_width),
        "seq",
        split_axis=2,
        concat_axis=1,
        tiled=True,
    )
    grad_heads = grad_heads.reshape(micro_count, query_rows, local_heads, head_dim)

    def backward_micro(micro_item):
        return attend_back(micro_item, query_place, block_rows, score_scale)

    grad_head_queries, grad_keys_seq, grad_values_seq = lax.map(
        backward_micro,
        (head_queries, keys_seq, values_seq, grad_heads, log_total, query_segment, key_segment),
    )
    grad_query_rows = lax.all_to_all(
        grad_head_queries.reshape(micro_count, query_rows, local_heads * head_dim).astype(
            jnp.bfloat16
        ),
        "seq",
        split_axis=1,
        concat_axis=2,
        tiled=True,
    ).astype(jnp.float32)
    grad_keys_own, grad_values_own = (
        lax.psum_scatter(
            grad_keys_seq.astype(jnp.bfloat16), ("seq", "fsdp"), scatter_dimension=1, tiled=True
        ).astype(jnp.float32),
        lax.psum_scatter(
            grad_values_seq.astype(jnp.bfloat16), ("seq", "fsdp"), scatter_dimension=1, tiled=True
        ).astype(jnp.float32),
    )
    grad_query_lin = (
        rotate(
            grad_query_rows.reshape(row_count, head_count, head_dim),
            cosine[:, None, :],
            -sine_part[:, None, :],
        )
        .reshape(row_count, model_width)
        .astype(jnp.bfloat16)
    )
    grad_key_lin = rotate(grad_keys_own.reshape(row_count, head_dim), cosine, -sine_part).astype(
        jnp.bfloat16
    )
    grad_value_lin = grad_values_own.reshape(row_count, head_dim).astype(jnp.bfloat16)
    grad_query_w = jnp.einsum(
        "nd,ne->de", hidden_one, grad_query_lin, preferred_element_type=jnp.float32
    )
    grad_key_w = jnp.einsum(
        "nd,ne->de", hidden_one, grad_key_lin, preferred_element_type=jnp.float32
    )
    grad_value_w = jnp.einsum(
        "nd,ne->de", hidden_one, grad_value_lin, preferred_element_type=jnp.float32
    )
    grad_hidden_one = jnp.einsum(
        "ne,de->nd", grad_query_lin, query_mat, preferred_element_type=jnp.float32
    )
    grad_hidden_one = grad_hidden_one + jnp.einsum(
        "ne,de->nd", grad_key_lin, key_mat, preferred_element_type=jnp.float32
    )
    grad_hidden_one = grad_hidden_one + jnp.einsum(
        "ne,de->nd", grad_value_lin, value_mat, preferred_element_type=jnp.float32
    )
    grad_gain_one = jnp.sum(grad_hidden_one * normed_one, axis=0)
    grad_input = grad_middle + norm_back(
        grad_hidden_one * gain_one.astype(jnp.float32), normed_one, inverse_one
    )
    matrix_grads = (
        grad_query_w,
        grad_key_w,
        grad_value_w,
        grad_out_w,
        grad_gate_w,
        grad_up_w,
        grad_down_w,
    )
    shards = tuple(
        lax.psum_scatter(
            grad.astype(jnp.bfloat16), ("dp", "seq", "fsdp"), scatter_dimension=0, tiled=True
        ).astype(jnp.float32)
        for grad in matrix_grads
    ) + (
        lax.psum_scatter(grad_gain_one, ("dp", "seq", "fsdp"), scatter_dimension=0, tiled=True),
        lax.psum_scatter(grad_gain_two, ("dp", "seq", "fsdp"), scatter_dimension=0, tiled=True),
    )
    layer_rows = result.reshape(micro_count, tok_rows, model_width).astype(jnp.bfloat16)
    return (
        layer_rows,
        keys_local,
        values_local,
        grad_input.reshape(micro_count, tok_rows, model_width),
        shards[0],
        shards[1],
        shards[2],
        shards[3],
        shards[4],
        shards[5],
        shards[6],
        shards[7],
        shards[8],
    )


BF16 = jnp.bfloat16
F32 = jnp.float32
MESH = pl.DeviceIdType.MESH
GROUPS = 64


def dot32(left, right, contract):
    return lax.dot_general(left, right, ((contract[0], contract[1]), ((), ())), preferred_element_type=F32)


def turn(vector, cosine, sine):
    return vector * cosine + pltpu.roll(vector, vector.shape[-1] // 2, 1) * sine


def stack_heads(ref, start, rows, heads, head_dim):
    return jnp.concatenate(
        [ref[pl.ds(start, rows), pl.ds(h * head_dim, head_dim)] for h in range(heads)], axis=0
    )


def masked_block(stacked, keys, query_place, query_segment, key_segment, heads, score_scale):
    rows, extent = query_place.shape[0], keys.shape[0]
    key_place = lax.broadcasted_iota(jnp.int32, (rows, extent), 1)
    allowed = (query_place >= key_place) & (query_segment == key_segment)
    bias = jnp.where(allowed, 0.0, MASKED).astype(F32)
    scores = dot32(stacked, keys, ((1,), (1,))) * score_scale
    scores = (scores.reshape(heads, rows, extent) + bias[None]).reshape(heads * rows, extent)
    row_max = jnp.max(scores, axis=-1, keepdims=True)
    weights = jnp.exp(scores - row_max)
    total = jnp.sum(weights, axis=-1, keepdims=True)
    return weights * (1.0 / total)


def attend_back_kernel(
    plan,
    queries_ref,
    grad_ref,
    keys_ref,
    values_ref,
    place_ref,
    segment_ref,
    key_segment_ref,
    cosine_ref,
    sine_ref,
    grad_lin_ref,
    grad_keys_ref,
    grad_values_ref,
):
    blocks, rows, pair, heads, head_dim, score_scale = plan

    @pl.when(pl.program_id(0) == 0)
    def _():
        grad_keys_ref[...] = jnp.zeros_like(grad_keys_ref)
        grad_values_ref[...] = jnp.zeros_like(grad_values_ref)

    for block in range(blocks):
        start = block * rows
        extent = (block + 1) * pair * rows
        stacked = stack_heads(queries_ref, start, rows, heads, head_dim)
        grads = stack_heads(grad_ref, start, rows, heads, head_dim)
        keys = keys_ref[pl.ds(0, extent), :]
        values = values_ref[pl.ds(0, extent), :]
        soft = masked_block(
            stacked,
            keys,
            place_ref[pl.ds(start, rows), :],
            segment_ref[pl.ds(start, rows), :],
            key_segment_ref[:, pl.ds(0, extent)],
            heads,
            score_scale,
        )
        grad_soft = dot32(grads, values, ((1,), (1,)))
        inner = jnp.sum(soft * grad_soft, axis=-1, keepdims=True)
        grad_scores = (soft * (grad_soft - inner)).astype(BF16)
        grad_values_ref[pl.ds(0, extent), :] += dot32(soft.astype(BF16), grads, ((0,), (0,)))
        grad_keys_ref[pl.ds(0, extent), :] += (
            dot32(grad_scores, stacked, ((0,), (0,))) * score_scale
        )
        grad_queries = dot32(grad_scores, keys, ((1,), (0,))) * score_scale
        cosine, sine = cosine_ref[pl.ds(start, rows), :], sine_ref[pl.ds(start, rows), :]
        for h in range(heads):
            part = turn(grad_queries[h * rows : (h + 1) * rows], cosine, -sine)
            grad_lin_ref[pl.ds(start, rows), pl.ds(h * head_dim, head_dim)] = part.astype(BF16)


def whole(shape):
    return pl.BlockSpec(shape, lambda g: (0,) * len(shape))


def attention_call(kernel, plan, groups, wide, narrow, outs, name, flops):
    rows = wide[0].shape[0]
    group = wide[0].shape[1] // groups
    column = pl.BlockSpec((rows, group), lambda g: (0, g))
    return pl.pallas_call(
        functools.partial(kernel, plan),
        grid=(groups,),
        in_specs=[column] * len(wide) + [whole(a.shape) for a in narrow],
        out_specs=[column if a.shape[0] == rows else whole(a.shape) for a in outs],
        out_shape=outs,
        compiler_params=pltpu.CompilerParams(vmem_limit_bytes=48 * 1024 * 1024),
        cost_estimate=pl.CostEstimate(
            flops=flops, bytes_accessed=6 * rows * wide[0].shape[1], transcendentals=flops // 512
        ),
        name=name,
    )(*wide, *narrow)


def gather(value, axes, dim):
    return lax.all_gather(value, axes, axis=dim, tiled=True)


def scatter_sum(value, axes, dim):
    return lax.psum_scatter(value, axes, scatter_dimension=dim, tiled=True)


def send_plane(value, step):
    return lax.ppermute(value, "seq", [(i, i ^ step) for i in range(4)])


def send_line(value, step):
    size = lax.axis_size("dp")
    return lax.ppermute(value, "dp", [(i, (i + step) % size) for i in range(size)])


def send_core(value):
    return lax.ppermute(value, "fsdp", [(0, 1), (1, 0)])


def block_of(value, index, dim=0):
    return lax.dynamic_index_in_dim(value, index, axis=dim, keepdims=False)


def put_block(value, block, index, dim=0):
    return lax.dynamic_update_index_in_dim(value, block, index, axis=dim)


def swap_blocks(value, own):
    out = value
    for step in (1, 2, 3):
        other = own ^ step
        out = put_block(out, send_plane(block_of(value, other), step), other)
    return out


def scatter_plane(value):
    half = value.shape[-1] // 2
    left, right = value[..., :half], value[..., half:]
    got = send_plane(jnp.stack([left[1], left[3]]), 1).astype(F32)
    passed = send_plane((left[2].astype(F32) + got[1]).astype(BF16), 2).astype(F32)
    left = left[0].astype(F32) + got[0] + passed
    got = send_plane(right[2:], 2).astype(F32)
    passed = send_plane((right[1].astype(F32) + got[1]).astype(BF16), 1).astype(F32)
    right = right[0].astype(F32) + got[0] + passed
    return jnp.concatenate([left, right], axis=-1)


def scatter_line(value, plane):
    size = lax.axis_size("dp")
    total = block_of(value, plane).astype(F32)
    for step in range(1, size):
        total = total + send_line(block_of(value, (plane + step) % size), step).astype(F32)
    return total


def scatter_core(value, core, dim):
    other = send_core(block_of(value, 1 - core, dim))
    return (block_of(value, core, dim).astype(F32) + other.astype(F32)).astype(BF16)


def scatter_every(value, plane, own, core):
    planes, chips, pair, shard, columns = value.shape
    value = scatter_core(value, core, 2)
    blocks = jnp.stack([block_of(value, own ^ step, 1) for step in range(chips)])
    value = scatter_plane(blocks).astype(BF16)
    return scatter_line(value, plane)


def by_step(blocks, own):
    return jnp.stack([block_of(blocks, own ^ step) for step in range(4)])


class Post:
    def __init__(self, send_sem, recv_sem):
        self.plane=lax.axis_index("dp"); self.own=lax.axis_index("seq"); self.core=lax.axis_index("fsdp")
        self.planes=lax.axis_size("dp")
        x=lax.rem(self.own,2); y=lax.div(self.own,2)
        self.by_x=self.own+1-2*x; self.by_y=self.own+2-4*y; self.far=3-self.own
        z,s,c=self.plane,self.own,self.core
        self.to_x=(z,self.by_x,c); self.to_y=(z,self.by_y,c); self.to_far=(z,self.far,c)
        self.to_core=(z,s,1-c)
        self.to_up=(lax.rem(z+1,self.planes),s,c); self.to_down=(lax.rem(z+self.planes-1,self.planes),s,c)
        self.has_up=z<self.planes-1; self.has_down=z>0
        self.send_sem, self.recv_sem = send_sem, recv_sem
        self.sent=[]
        self.steps={0:[(z,())]}
        for k in range(1,self.planes):
            self.steps[k]=[(jnp.clip(z-k,0,self.planes-1),(z-k>=0,)),(jnp.clip(z+k,0,self.planes-1),(z+k<=self.planes-1,))]
        self.groups={}
    def group(self, name):
        return self.groups.setdefault(name, len(self.groups))
    def barrier(self):
        bar=pltpu.get_barrier_semaphore()
        for t in (self.to_x,self.to_y,self.to_far,self.to_core):
            pl.semaphore_signal(bar,inc=1,device_id=t,device_id_type=MESH)
        for chip in (self.by_x,self.by_y,self.far):
            pl.semaphore_signal(bar,inc=1,device_id=(self.plane,chip,1-self.core),device_id_type=MESH)
        @pl.when(self.has_up)
        def _(): pl.semaphore_signal(bar,inc=1,device_id=self.to_up,device_id_type=MESH)
        @pl.when(self.has_down)
        def _(): pl.semaphore_signal(bar,inc=1,device_id=self.to_down,device_id_type=MESH)
        pl.semaphore_wait(bar,7+self.has_up.astype(jnp.int32)+self.has_down.astype(jnp.int32))
    def copy(self, src, dst, name, index, target, arrive=None):
        return pltpu.make_async_remote_copy(src_ref=src,dst_ref=dst,
            send_sem=self.send_sem.at[self.group(name),index],
            recv_sem=self.recv_sem.at[self.group(arrive or name),index],
            device_id=target,device_id_type=MESH)
    def send(self, src, dst, name, index, target, arrive=None, when=()):
        def go(): self.copy(src,dst,name,index,target,arrive).start()
        if when:
            cond=functools.reduce(jnp.logical_and,when)
            pl.when(cond)(go)
        else: go()
        self.sent.append((when,lambda: self.copy(src,dst,name,index,target,arrive).wait_send()))
    def wait(self, ref, name, index):
        self.copy(ref,ref,name,index,self.to_core).wait_recv()
    def finish(self):
        for when,w in self.sent:
            if when: pl.when(functools.reduce(jnp.logical_and,when))(w)
            else: w()

class Line:
    def __init__(self, post, name, unit, own_source):
        self.p, self.name, self.unit, self.src = post, name, unit, own_source
    def start(self):
        p=self.p
        p.send(self.src,self.unit(p.plane),self.name+"_up",p.plane,p.to_up,self.name,(p.has_up,))
        p.send(self.src,self.unit(p.plane),self.name+"_down",p.plane,p.to_down,self.name,(p.has_down,))
    def hop(self, k, then=None):
        p=self.p
        for sign,(at,(here,)) in zip((-1,1),p.steps[k]):
            on=p.has_up if sign<0 else p.has_down
            target=p.to_up if sign<0 else p.to_down
            ref=self.unit(at)
            @pl.when(here)
            def _(ref=ref,at=at): p.wait(ref,self.name,at)
            if k<p.planes-1:
                p.send(ref,ref,self.name+("_up" if sign<0 else "_down"),at,target,self.name,(here,on))
            if then: then(at,here)

class Spread:
    def __init__(self, post, name, unit, low, high):
        self.p,self.name,self.unit,self.low,self.high=post,name,unit,low,high
    def start(self, index, source, when=()):
        p=self.p
        dst=self.unit(index,p.own)
        p.send(source,dst,self.name+"_x",index,p.to_x,None,when)
        p.send(source,dst,self.name+"_y",index,p.to_y,None,when)
    def relay(self, index, when=()):
        p=self.p
        def go(f):
            if when: pl.when(functools.reduce(jnp.logical_and,when))(f)
            else: f()
        go(lambda: p.wait(self.unit(index,p.by_x),self.name+"_x",index))
        ref=self.low(index,p.by_x)
        p.send(ref,ref,self.name+"_l",index,p.to_y,None,when)
        go(lambda: p.wait(self.unit(index,p.by_y),self.name+"_y",index))
        ref=self.high(index,p.by_y)
        p.send(ref,ref,self.name+"_h",index,p.to_x,None,when)
    def arrive(self, index, when=()):
        p=self.p
        def go():
            p.wait(self.low(index,p.far),self.name+"_l",index)
            p.wait(self.high(index,p.far),self.name+"_h",index)
        if when: pl.when(functools.reduce(jnp.logical_and,when))(go)
        else: go()


def dot2(l, r, ca, cb):
    return dot32(l, r, ((ca,), (cb,)))


def front_kernel(plan,tok,cot,marks,wq_in,wo_in,gu_in,wd_in,freq,
    x_out,marks_out,wq_out,wo_out,gu,wd,E,two,middle_out,h1_out,q_out,att_out,kv_out,home,cos_out,sin_out,
    send_sem,recv_sem,local_sem,b_cot,b_gu,b_wd,
    x_v,marks_v,wq_v,wo_v,h1_v,lin_v,q_v,att_v,kv_v,mid_v,two_v,cos_v,sin_v,gain_v):
    tile,width,head_dim,group=plan
    scale=head_dim**-0.5
    p=Post(send_sem,recv_sem)
    z,s,c=p.plane,p.own,p.core
    chips=4
    rows=chips*tile
    groups=width//group; heads=group//head_dim
    qkv=width+2*head_dim
    count=[0]
    outs_=[]
    def local(src,dst):
        cp=pltpu.make_async_copy(src,dst,local_sem.at[count[0]]); count[0]+=1
        cp.start(); return cp
    def out(src,dst):
        outs_.append(local(src,dst))
    loads=[local(tok.at[s],x_v.at[s]),local(marks.at[s],marks_v.at[c,s]),local(wq_in,wq_v.at[z,s,c]),local(wo_in,wo_v.at[z,s,c])]
    late=[local(cot,b_cot),local(gu_in.at[s],b_gu),local(wd_in,b_wd)]
    p.barrier()
    def attention_weight(name, arr, src):
        n=arr.shape[3]//2
        spread=Spread(p,name,lambda a,b: arr.at[a,b,c],lambda a,b: arr.at[a,b,c,pl.ds(0,n)],lambda a,b: arr.at[a,b,c,pl.ds(n,n)])
        line=Line(p,name+"_z",lambda a: arr.at[a,s,c],src)
        return spread,line
    q_spread,q_line=attention_weight("wq",wq_v,wq_in)
    o_spread,o_line=attention_weight("wo",wo_v,wo_in)
    def each(k, f):
        for at,when in p.steps[k]: f(at,when)
    def to_sibling(name, arr, a, when):
        ref=arr.at[a,:,c]
        p.send(ref,ref,name+"_c",a,p.to_core,None,when)
    others=((p.to_x,p.by_x),(p.to_y,p.by_y),(p.to_far,p.far))
    def swap(src,dst_of,name):
        for i,(t,o) in enumerate(others):
            p.send(src.at[o],dst_of(s),name,i,t)
    def swapped(dst_of,name):
        for i,(t,o) in enumerate(others):
            p.wait(dst_of(o),name,i)
    q_line.start()
    swap(tok,lambda b: x_v.at[b],"tok")
    q_spread.start(z,wq_in)
    for i,(t,o) in enumerate(others):
        p.send(marks.at[o],marks_v.at[c,s],"mk",i,t)
        p.send(marks.at[o],marks_v.at[c,s],"mk2",i,(z,o,1-c))
    p.send(marks.at[s],marks_v.at[c,s],"mk2",3,p.to_core)
    fwd=lambda a,here: q_spread.start(a,wq_v.at[a,s,c],(here,))
    wd_line=Line(p,"wd_z",lambda a: wd.at[a,c],wd_in)
    gu_line=Line(p,"gu_z",lambda a: gu.at[a,:,c],gu.at[z,:,c])
    q_line.hop(1,fwd)
    wd_line.start()
    q_line.hop(2,fwd)
    q_line.hop(3,fwd)
    swap(gu_in,lambda b: gu.at[z,b,c],"gu")
    for cp in loads+late: cp.wait()
    out(b_cot,E.at[:,s]); out(b_gu,gu.at[z,s,c]); own_gu=outs_[-1]; out(b_wd,wd.at[z,c]); own_wd=outs_[-1]
    for k in range(4): each(k,lambda a,w: q_spread.relay(a,w))
    o_line.start(); o_spread.start(z,wo_in)
    def each_q(a,w):
        q_spread.arrive(a,w); to_sibling("wq",wq_v,a,w)
    for k in range(4): each(k,each_q)
    swapped(lambda b: x_v.at[b],"tok")
    for i,(t,o) in enumerate(others):
        p.wait(marks_v.at[c,o],"mk",i); p.wait(marks_v.at[1-c,o],"mk2",i)
    p.wait(marks_v.at[1-c,s],"mk2",3)
    swapped(lambda b: gu.at[z,b,c],"gu")
    own_gu.wait(); outs_[:]=[o for o in outs_ if o is not own_gu]
    gu_line.start(); to_sibling("gu",gu,z,())
    for a in range(4): p.wait(wq_v.at[a,:,1-c],"wq_c",a)
    out(x_v,x_out); out(marks_v,marks_out); out(wq_v,wq_out)
    ofwd=lambda a,here: o_spread.start(a,wo_v.at[a,s,c],(here,))
    gufwd=lambda a,here: to_sibling("gu",gu,a,(here,))
    e_parts=[]
    for i in range(2):
        def sub(lo,n,i=i): return lambda _,b: E.at[pl.ds(2*i+lo,n),b]
        e_parts.append(Spread(p,"E%d"%i,sub(0,2),sub(0,1),sub(1,1)))
    def e_start(i):
        for t,nm in ((p.to_x,"_x"),(p.to_y,"_y")):
            p.send(cot.at[pl.ds(2*i,2)],E.at[pl.ds(2*i,2),s],"E%d"%i+nm,0,t)
    for i in range(width//head_dim):
        a,b=divmod(i,4)
        block=wq_v[a,b,:,:,pl.ds(qkv,head_dim)].reshape(head_dim,head_dim).astype(F32)
        gain_v[:,pl.ds(i*head_dim,head_dim)]=jnp.transpose(block)[0:8]
    def norm_block(b,carry):
        x=x_v[b].astype(F32)
        inv=lax.rsqrt(jnp.mean(x*x,axis=-1,keepdims=True)+EPSILON)
        h1_v[pl.ds(b*tile,tile),:]=(x*inv*gain_v[0:1,:]).astype(BF16)
        return carry
    lax.fori_loop(0,chips,norm_block,0)
    lane=lax.broadcasted_iota(jnp.int32,(1,head_dim),1)
    sign=jnp.where(lane<head_dim//2,-1.0,1.0).astype(F32)
    seg_cols=[]
    for b in range(chips):
        m=jnp.transpose(marks_v[c,b].astype(F32))
        angle=m[:,1:2]*freq[...]
        cos_v[pl.ds(b*tile,tile),:]=jnp.cos(angle); sin_v[pl.ds(b*tile,tile),:]=jnp.sin(angle)*sign
        seg_cols.append(m[:,0:1])
    key_seg=jnp.concatenate([marks_v[k%2,k//2,0:1,:] for k in range(2*chips)],axis=1).astype(F32)
    o_line.hop(1,ofwd)
    w=wq_v[:,:,:,:,pl.ds(width,2*head_dim)].reshape(width,2*head_dim)
    kv=dot2(h1_v[...],w,1,0)
    kv=jnp.concatenate([turn(kv[:,:head_dim],cos_v[...],sin_v[...]),kv[:,head_dim:]],axis=1).astype(BF16)
    kv_v[:,pl.ds(c,1)]=kv.reshape(chips,1,tile,2*head_dim)
    p.send(kv_v.at[:,c],kv_v.at[:,c],"kv",0,p.to_core)
    swap(kv_v.at[:,c],lambda b: home.at[b],"home")
    out(kv_v.at[s,c],home.at[s]); out(h1_v,h1_out); out(cos_v,cos_out); out(sin_v,sin_out)
    steps={0:[lambda: o_line.hop(2,ofwd)],
           1:[lambda: p.wait(kv_v.at[:,1-c],"kv",0), lambda: o_line.hop(3,ofwd)],
           2:[lambda: wd_line.hop(1), lambda: each(0,lambda a,w: o_spread.relay(a,w)), lambda: each(1,lambda a,w: o_spread.relay(a,w))],
           3:[lambda: each(2,lambda a,w: o_spread.relay(a,w)), lambda: each(3,lambda a,w: o_spread.relay(a,w)),lambda: gu_line.hop(1,gufwd)],
           4:[lambda: wd_line.hop(2), lambda: e_start(0)]}
    def lin_group(g,carry):
        w=wq_v[:,:,:,:,pl.ds(pl.multiple_of(g*group,group),group)].reshape(width,group)
        lin_v[...]=dot2(h1_v[...],w,1,0)
        for b in range(chips):
            cos,sin=cos_v[pl.ds(b*tile,tile),:],sin_v[pl.ds(b*tile,tile),:]
            for h in range(heads):
                part=lin_v[pl.ds(b*tile,tile),pl.ds(h*head_dim,head_dim)]
                q_v[pl.ds(b*tile,tile),pl.ds(pl.multiple_of(g*group+h*head_dim,head_dim),head_dim)]=turn(part,cos,sin).astype(BF16)
        return carry
    for f in steps[0]: f()
    lax.fori_loop(0,groups,lin_group,0)
    for f in steps[1]: f()
    out(kv_v,kv_out); out(q_v,q_out)
    def attend_group(g,carry):
        for b in range(chips):
            extent=(b+1)*2*tile
            at=lambda h: pl.ds(pl.multiple_of(g*group+h*head_dim,head_dim),head_dim)
            q=jnp.concatenate([q_v[pl.ds(b*tile,tile),at(h)] for h in range(heads)],axis=0)
            kvs=kv_v[pl.ds(0,b+1)].reshape(extent,2*head_dim)
            place=(2*b+c)*tile+lax.broadcasted_iota(jnp.int32,(tile,extent),0)
            seen=lax.broadcasted_iota(jnp.int32,(tile,extent),1)
            allowed=(place>=seen)&(seg_cols[b]==key_seg[:,:extent])
            bias=jnp.where(allowed,0.0,MASKED).astype(F32)
            sc=dot2(q,kvs[:,:head_dim],1,1)*scale
            sc=(sc.reshape(heads,tile,extent)+bias[None]).reshape(heads*tile,extent)
            top=jnp.max(sc,axis=-1,keepdims=True)
            e=jnp.exp(sc-top)
            soft=(e*(1.0/jnp.sum(e,axis=-1,keepdims=True))).astype(BF16)
            mixed=dot2(soft,kvs[:,head_dim:],1,0).astype(BF16)
            for h in range(heads):
                att_v[pl.ds(b*tile,tile),at(h)]=mixed[h*tile:(h+1)*tile]
        for i in (2,3):
            @pl.when(g==i-1)
            def _(i=i):
                for f in steps[i]: f()
        return carry
    lax.fori_loop(0,groups,attend_group,0)
    out(att_v,att_out)
    def each_o(a,w):
        o_spread.arrive(a,w); to_sibling("wo",wo_v,a,w)
    for k in range(4): each(k,each_o)
    for f in steps[4]: f()
    for a in range(4): p.wait(wo_v.at[a,:,1-c],"wo_c",a)
    out(wo_v,wo_out)
    def project(g,carry):
        at=pl.ds(pl.multiple_of(g*group,group),group)
        w=wo_v[:,:,:,:,at].reshape(width,group)
        lin_v[...]=dot2(att_v[...],w,1,0)
        for b in range(chips):
            mid_v[pl.ds(b*tile,tile),at]=x_v[b,:,at].astype(F32)+lin_v[pl.ds(b*tile,tile),:]
        return carry
    lax.fori_loop(0,groups,project,0)
    out(mid_v,middle_out)
    def norm_two(b,carry):
        at=pl.ds(pl.multiple_of(b*tile,tile),tile)
        m=mid_v[at,:]
        inv=lax.rsqrt(jnp.mean(m*m,axis=-1,keepdims=True)+EPSILON)
        two_v[at,:]=(m*inv*gain_v[1:2,:]).astype(BF16)
        return carry
    lax.fori_loop(0,chips,norm_two,0)
    half=rows//2
    two_spread=Spread(p,"two",lambda _,b: two.at[b],lambda _,b: two.at[b,pl.ds(0,half)],lambda _,b: two.at[b,pl.ds(half,half)])
    two_spread.start(0,two_v)
    out(two_v,two.at[s])
    e_start(1)
    wd_line.hop(3)
    gu_line.hop(2,gufwd)
    e_parts[0].relay(0)
    own_wd.wait(); outs_[:]=[o for o in outs_ if o is not own_wd]
    p.send(wd.at[:,c],wd.at[:,c],"wd_c",0,p.to_core)
    gu_line.hop(3,gufwd)
    two_spread.relay(0)
    e_parts[0].arrive(0)
    e_parts[1].relay(0)
    two_spread.arrive(0)
    e_parts[1].arrive(0)
    p.wait(wd.at[:,1-c],"wd_c",0)
    for a in range(4): p.wait(gu.at[a,:,1-c],"gu_c",a)
    swapped(lambda b: home.at[b],"home")
    for cp in outs_: cp.wait()
    p.finish()
    assert len(p.groups)<=GROUPS, len(p.groups)

def front(tok,cot,marks,wq_in,wo_in,gu_in,wd_in):
    Z,S,C=lax.axis_size("dp"),lax.axis_size("seq"),lax.axis_size("fsdp")
    sd=jax.ShapeDtypeStruct
    micro,tile,width=tok.shape
    rows=micro*tile
    head_dim=128
    group=512
    half=head_dim//2
    freq=jnp.exp(-jnp.log(jnp.float32(10000.0))*jnp.arange(half,dtype=F32)/half)
    freq=jnp.concatenate([freq,freq])[None]
    outs=[sd((S,tile,width),BF16),sd((C,)+marks.shape,jnp.int32),sd((Z,S,C)+wq_in.shape,BF16),sd((Z,S,C)+wo_in.shape,BF16),
          sd((Z,S,C)+gu_in.shape[1:],BF16),sd((Z,C)+wd_in.shape,BF16),sd((S,)+cot.shape,BF16),
          sd((S,rows,width),BF16),sd((rows,width),F32),sd((rows,width),BF16),sd((rows,width),BF16),sd((rows,width),BF16),
          sd((S,C,tile,2*head_dim),BF16),sd((S,tile,2*head_dim),BF16),sd((rows,head_dim),F32),sd((rows,head_dim),F32)]
    anyspec=pl.BlockSpec(memory_space=pl.ANY)
    V=pltpu.VMEM
    return pl.pallas_call(functools.partial(front_kernel,(tile,width,head_dim,group)),out_shape=outs,
        in_specs=[anyspec]*7+[pl.BlockSpec(memory_space=V)],out_specs=[anyspec]*len(outs),
        scratch_shapes=[pltpu.SemaphoreType.DMA((GROUPS,4)),pltpu.SemaphoreType.DMA((GROUPS,4)),pltpu.SemaphoreType.DMA((32,)),
          V(cot.shape,BF16),V(gu_in.shape[1:],BF16),V(wd_in.shape,BF16),
          V((S,tile,width),BF16),V((C,)+marks.shape,jnp.int32),V((Z,S,C)+wq_in.shape,BF16),V((Z,S,C)+wo_in.shape,BF16),
          V((rows,width),BF16),V((rows,group),F32),V((rows,width),BF16),V((rows,width),BF16),V((S,C,tile,2*head_dim),BF16),
          V((rows,width),F32),V((rows,width),BF16),V((rows,head_dim),F32),V((rows,head_dim),F32),V((8,width),F32)],
        compiler_params=pltpu.CompilerParams(collective_id=1,has_side_effects=True,vmem_limit_bytes=60*1024*1024),name="front")(tok,cot,marks,wq_in,wo_in,gu_in,wd_in,freq)


def body_plane(
    tokens,
    cotangent,
    segments,
    positions,
    w_query,
    w_key,
    w_value,
    w_out,
    w_gate,
    w_up,
    w_down,
    gain_attn,
    gain_mlp,
):
    micro, tile, width = tokens.shape
    head_dim = w_key.shape[1]
    head_count = width // head_dim
    planes = lax.axis_size("dp")
    chips = lax.axis_size("seq")
    pair = lax.axis_size("fsdp")
    plane = lax.axis_index("dp")
    own = lax.axis_index("seq")
    core = lax.axis_index("fsdp")
    rows = micro * tile
    hidden = w_gate.shape[1]
    shard = w_query.shape[0]
    own_hidden = hidden // chips
    piece = own_hidden // planes
    qkv = width + 2 * head_dim
    score_scale = 1.0 / math.sqrt(head_dim)

    gains = jnp.stack([gain_attn, gain_mlp], axis=1)
    gains = jnp.pad(gains, ((0, 0), (0, head_dim - 2)))
    w_in = jnp.concatenate([w_query, w_key, w_value, gains], axis=1)
    gate_up = jnp.stack([w_gate, w_up], axis=1).reshape(shard, 2, planes, chips, piece)
    gate_up = gate_up.transpose(3, 0, 1, 2, 4).reshape(chips, shard, 2 * own_hidden)
    marks = jnp.pad(jnp.stack([segments, positions], axis=1), ((0, 0), (0, 6), (0, 0)))
    (
        x_rows,
        marks,
        w_qkv,
        out_mat,
        gate_up,
        down_mat,
        grads_in,
        plane_two,
        middle,
        hidden_one,
        queries,
        attended,
        kv,
        kv_home,
        cosine,
        sine,
    ) = front(tokens, cotangent, marks, w_in, w_out, gate_up, w_down)
    x_rows = x_rows.reshape(rows, width).astype(F32)
    w_qkv = w_qkv.reshape(width, qkv + head_dim)
    gain_one, gain_two = w_qkv[:, qkv].astype(F32), w_qkv[:, qkv + 1].astype(F32)
    out_mat = out_mat.reshape(width, width)
    gate_up = gate_up.reshape(width, 2 * own_hidden)
    down_mat = down_mat.reshape(own_hidden, width)
    grads_in = grads_in.reshape(chips * rows, width)
    plane_two = plane_two.reshape(chips * rows, width)
    kv = kv.reshape(rows * pair, 2 * head_dim)
    keys, values = kv[:, :head_dim], kv[:, head_dim:]
    query_segment = block_of(marks, core)[:, 0].reshape(rows, 1)
    key_segment = marks[:, :, 0].transpose(1, 0, 2).reshape(1, rows * pair)
    query_place = (
        (jnp.arange(chips, dtype=jnp.int32)[:, None] * pair + core) * tile
        + jnp.arange(tile, dtype=jnp.int32)[None, :]
    ).reshape(rows, 1)
    groups = max(1, head_count // 4)
    heads = head_count // groups
    plan = (chips, tile, pair, heads, head_dim, score_scale)
    pairs_seen = tile * tile * pair * chips * (chips + 1) // 2 * head_count * head_dim
    narrow = (keys, values, query_place, query_segment, key_segment, cosine, sine)
    inverse_one = lax.rsqrt(jnp.mean(x_rows * x_rows, axis=-1, keepdims=True) + EPSILON)
    normed_one = x_rows * inverse_one
    inverse_two = lax.rsqrt(jnp.mean(middle * middle, axis=-1, keepdims=True) + EPSILON)
    normed_two = middle * inverse_two

    gate_up_lin = jnp.dot(plane_two, gate_up, preferred_element_type=F32)
    gate_proj, up_proj = gate_up_lin[:, :own_hidden], gate_up_lin[:, own_hidden:]
    gate_sigmoid = jax.nn.sigmoid(gate_proj)
    gate_silu = gate_proj * gate_sigmoid
    hidden_mlp = (gate_silu * up_proj).astype(BF16)
    partial_out = jnp.dot(hidden_mlp, down_mat, preferred_element_type=F32).astype(BF16)
    result = middle + scatter_plane(by_step(partial_out.reshape(chips, rows, width), own))
    layer_rows = swap_blocks(result.astype(BF16).reshape(chips, tile, width), own)

    grad_hidden = dot32(grads_in, down_mat, ((1,), (1,)))
    grad_gate_pre = (
        grad_hidden * up_proj * gate_sigmoid * (1.0 + gate_proj * (1.0 - gate_sigmoid))
    ).astype(BF16)
    grad_up_pre = (grad_hidden * gate_silu).astype(BF16)
    grad_pre = jnp.concatenate([grad_gate_pre, grad_up_pre], axis=1)
    partial_two = dot32(grad_pre, gate_up, ((1,), (1,))).astype(BF16)
    grad_hidden_two = scatter_plane(by_step(partial_two.reshape(chips, rows, width), own))
    grad_gate_up = dot32(plane_two, grad_pre, ((0,), (0,))).astype(BF16)
    grad_down = dot32(hidden_mlp, grads_in, ((0,), (0,))).astype(BF16)

    grad_down = scatter_core(grad_down.reshape(planes, pair, -1, width), core, 1)
    grad_down = scatter_line(grad_down, plane)
    grad_gate_up = scatter_core(
        grad_gate_up.reshape(planes, chips, pair, shard, 2 * own_hidden), core, 2
    )
    grad_gate_up = scatter_line(grad_gate_up, plane).astype(BF16)
    grad_gate_up = swap_blocks(grad_gate_up, own).reshape(chips, shard, 2, planes, piece)
    grad_gate_up = grad_gate_up.transpose(2, 1, 3, 0, 4).reshape(2, shard, hidden).astype(F32)

    grad_gain_two = jnp.sum(grad_hidden_two * normed_two, axis=0)
    grad_rows = lax.dynamic_slice_in_dim(grads_in, own * rows, rows, axis=0).astype(F32)
    grad_middle = grad_rows + norm_back(grad_hidden_two * gain_two, normed_two, inverse_two)
    grad_proj = grad_middle.astype(BF16)
    grad_mixed = dot32(grad_proj, out_mat, ((1,), (1,))).astype(BF16)
    grad_query_lin, grad_keys, grad_values = attention_call(
        attend_back_kernel,
        plan,
        groups,
        (queries, grad_mixed),
        narrow,
        [
            jax.ShapeDtypeStruct((rows, width), BF16),
            jax.ShapeDtypeStruct((rows * pair, head_dim), F32),
            jax.ShapeDtypeStruct((rows * pair, head_dim), F32),
        ],
        "attend_back",
        10 * pairs_seen,
    )
    grad_kv = jnp.concatenate([grad_keys, grad_values], axis=1)
    grad_kv = grad_kv.reshape(chips, pair, tile, 2 * head_dim)
    grad_kv = block_of(grad_kv, core, 1) + send_core(block_of(grad_kv, 1 - core, 1))
    grad_kv = grad_kv.reshape(rows, 2 * head_dim)
    grad_keys = grad_kv[:, :head_dim]
    grad_keys = grad_keys * cosine - jnp.roll(grad_keys, head_dim // 2, axis=1) * sine
    grad_lin = jnp.concatenate(
        [grad_query_lin, grad_keys.astype(BF16), grad_kv[:, head_dim:].astype(BF16)], axis=1
    )
    grad_out = dot32(attended, grad_proj, ((0,), (0,))).astype(BF16)
    grad_hidden_one = dot32(grad_lin, w_qkv[:, :qkv], ((1,), (1,)))
    grad_gain_one = jnp.sum(grad_hidden_one * normed_one, axis=0)
    grad_input = grad_middle + norm_back(grad_hidden_one * gain_one, normed_one, inverse_one)
    grad_input = swap_blocks(grad_input.astype(BF16).reshape(chips, tile, width), own)
    grad_out = scatter_every(grad_out.reshape(planes, chips, pair, shard, width), plane, own, core)
    grad_gains = jnp.pad(
        jnp.stack([grad_gain_one, grad_gain_two], axis=1), ((0, 0), (0, head_dim - 2))
    )
    grad_qkv = dot32(hidden_one, grad_lin, ((0,), (0,)))
    grad_qkv = jnp.concatenate([grad_qkv, grad_gains], axis=1).astype(BF16)
    grad_qkv = grad_qkv.reshape(planes, chips, pair, shard, qkv + head_dim)
    grad_qkv = scatter_every(grad_qkv, plane, own, core)
    return (
        layer_rows,
        kv_home[..., :head_dim],
        kv_home[..., head_dim:],
        grad_input.astype(F32),
        grad_qkv[:, :width],
        grad_qkv[:, width : width + head_dim],
        grad_qkv[:, width + head_dim : qkv],
        grad_out,
        grad_gate_up[0],
        grad_gate_up[1],
        grad_down,
        grad_qkv[:, qkv],
        grad_qkv[:, qkv + 1],
    )


def body(tokens, *rest):
    if tokens.shape[0] == lax.axis_size("seq") == 4 and lax.axis_size("fsdp") == 2:
        return body_plane(tokens, *rest)
    return body_general(tokens, *rest)


def solution(mesh):
    in_specs = (
        P(None, ("dp", "seq", "fsdp"), None),
        P(None, ("dp", "seq", "fsdp"), None),
        P(None, ("dp", "seq", "fsdp")),
        P(None, ("dp", "seq", "fsdp")),
        P(("dp", "seq", "fsdp"), None),
        P(("dp", "seq", "fsdp"), None),
        P(("dp", "seq", "fsdp"), None),
        P(("dp", "seq", "fsdp"), None),
        P(("dp", "seq", "fsdp"), None),
        P(("dp", "seq", "fsdp"), None),
        P(("dp", "seq", "fsdp"), None),
        P(("dp", "seq", "fsdp")),
        P(("dp", "seq", "fsdp")),
    )
    out_specs = (
        P(None, ("dp", "seq", "fsdp"), None),
        P(None, ("dp", "seq", "fsdp"), None),
        P(None, ("dp", "seq", "fsdp"), None),
        P(None, ("dp", "seq", "fsdp"), None),
        P(("dp", "seq", "fsdp"), None),
        P(("dp", "seq", "fsdp"), None),
        P(("dp", "seq", "fsdp"), None),
        P(("dp", "seq", "fsdp"), None),
        P(("dp", "seq", "fsdp"), None),
        P(("dp", "seq", "fsdp"), None),
        P(("dp", "seq", "fsdp"), None),
        P(("dp", "seq", "fsdp")),
        P(("dp", "seq", "fsdp")),
    )
    return jax.shard_map(body, mesh=mesh, in_specs=in_specs, out_specs=out_specs, check_vma=False)
```

```python
import functools
import math

import jax
import jax.numpy as jnp
from jax import lax
from jax.experimental import pallas as pl
from jax.experimental.pallas import tpu as pltpu
from jax.sharding import PartitionSpec as P

EPSILON = 1e-05
MASKED = -1e30


def rope_tables(places, half_dim):
    frequency = jnp.exp(-math.log(10000.0) * jnp.arange(half_dim, dtype=jnp.float32) / half_dim)
    angles = places.astype(jnp.float32)[:, None] * frequency[None, :]
    return (jnp.cos(angles), jnp.sin(angles))


def rotate(vector, cosine, sine_part):
    half_dim = vector.shape[-1] // 2
    first_half = vector[..., :half_dim]
    second_half = vector[..., half_dim:]
    return jnp.concatenate(
        [
            first_half * cosine - second_half * sine_part,
            second_half * cosine + first_half * sine_part,
        ],
        axis=-1,
    )


def norm_back(grad_normed, normed, inverse):
    return inverse * (grad_normed - normed * jnp.mean(grad_normed * normed, axis=-1, keepdims=True))


def mask_scores(scores, query_place, query_segment, key_segment):
    key_place = jnp.arange(key_segment.shape[0], dtype=jnp.int32)
    allowed = (query_segment[:, None] == key_segment[None, :]) & (
        query_place[:, None] >= key_place[None, :]
    )
    return jnp.where(allowed[None], scores, MASKED)


def attend_micro(micro_item, query_place, block_rows, score_scale):
    queries, keys_seq, values_seq, query_segment, key_segment = micro_item
    query_rows, local_heads, head_dim = queries.shape
    blocks = query_rows // block_rows

    def one_block(block_item):
        block_query, block_place, block_segment = block_item
        scores = (
            jnp.einsum("qhd,kd->hqk", block_query, keys_seq, preferred_element_type=jnp.float32)
            * score_scale
        )
        scores = mask_scores(scores, block_place, block_segment, key_segment)
        row_max = jnp.max(scores, axis=-1, keepdims=True)
        log_total = row_max + jnp.log(jnp.sum(jnp.exp(scores - row_max), axis=-1, keepdims=True))
        soft_weights = jnp.exp(scores - log_total).astype(jnp.bfloat16)
        attended = jnp.einsum(
            "hqk,kd->qhd", soft_weights, values_seq, preferred_element_type=jnp.float32
        )
        return (attended.astype(jnp.bfloat16), log_total)

    return lax.map(
        one_block,
        (
            queries.reshape(blocks, block_rows, local_heads, head_dim),
            query_place.reshape(blocks, block_rows),
            query_segment.reshape(blocks, block_rows),
        ),
    )


def attend_back(micro_item, query_place, block_rows, score_scale):
    queries, keys_seq, values_seq, grad_attended, log_total, query_segment, key_segment = micro_item
    query_rows, local_heads, head_dim = queries.shape
    blocks = query_rows // block_rows

    def one_block(running, block_item):
        grad_keys, grad_values = running
        block_query, block_grad, block_total, block_place, block_segment = block_item
        scores = (
            jnp.einsum("qhd,kd->hqk", block_query, keys_seq, preferred_element_type=jnp.float32)
            * score_scale
        )
        scores = mask_scores(scores, block_place, block_segment, key_segment)
        soft_weights = jnp.exp(scores - block_total)
        grad_soft = jnp.einsum(
            "qhd,kd->hqk", block_grad, values_seq, preferred_element_type=jnp.float32
        )
        inner_sum = jnp.sum(soft_weights * grad_soft, axis=-1, keepdims=True)
        grad_scores = (soft_weights * (grad_soft - inner_sum)).astype(jnp.bfloat16)
        grad_queries = (
            jnp.einsum("hqk,kd->qhd", grad_scores, keys_seq, preferred_element_type=jnp.float32)
            * score_scale
        )
        grad_keys = (
            grad_keys
            + jnp.einsum(
                "hqk,qhd->kd", grad_scores, block_query, preferred_element_type=jnp.float32
            )
            * score_scale
        )
        grad_values = grad_values + jnp.einsum(
            "hqk,qhd->kd",
            soft_weights.astype(jnp.bfloat16),
            block_grad,
            preferred_element_type=jnp.float32,
        )
        return ((grad_keys, grad_values), grad_queries)

    zero_init = jnp.zeros(keys_seq.shape, jnp.float32)
    running, grad_queries = lax.scan(
        one_block,
        (zero_init, zero_init),
        (
            queries.reshape(blocks, block_rows, local_heads, head_dim),
            grad_attended.reshape(blocks, block_rows, local_heads, head_dim),
            log_total,
            query_place.reshape(blocks, block_rows),
            query_segment.reshape(blocks, block_rows),
        ),
    )
    return (grad_queries, running[0], running[1])


def body_general(
    tokens,
    cotangent,
    segments,
    positions,
    w_query,
    w_key,
    w_value,
    w_out,
    w_gate,
    w_up,
    w_down,
    gain_attn,
    gain_mlp,
):
    micro_count, tok_rows, model_width = tokens.shape
    head_dim = w_key.shape[1]
    head_count = model_width // head_dim
    seq_size = lax.axis_size("seq")
    pair_size = lax.axis_size("fsdp")
    local_heads = head_count // seq_size
    row_count = micro_count * tok_rows
    query_rows = seq_size * tok_rows
    block_rows = min(512, query_rows)
    score_scale = 1.0 / math.sqrt(head_dim)
    gathered = (
        lax.all_gather(w_query, ("dp", "seq", "fsdp"), axis=0, tiled=True),
        lax.all_gather(w_key, ("dp", "seq", "fsdp"), axis=0, tiled=True),
        lax.all_gather(w_value, ("dp", "seq", "fsdp"), axis=0, tiled=True),
        lax.all_gather(w_out, ("dp", "seq", "fsdp"), axis=0, tiled=True),
        lax.all_gather(w_gate, ("dp", "seq", "fsdp"), axis=0, tiled=True),
        lax.all_gather(w_up, ("dp", "seq", "fsdp"), axis=0, tiled=True),
        lax.all_gather(w_down, ("dp", "seq", "fsdp"), axis=0, tiled=True),
        lax.all_gather(gain_attn, ("dp", "seq", "fsdp"), axis=0, tiled=True),
        lax.all_gather(gain_mlp, ("dp", "seq", "fsdp"), axis=0, tiled=True),
    )
    query_mat, key_mat, value_mat, out_mat, gate_mat, up_mat, down_mat, gain_one, gain_two = (
        gathered
    )
    flat_rows = tokens.reshape(row_count, model_width).astype(jnp.float32)
    inverse_one = lax.rsqrt(jnp.mean(flat_rows * flat_rows, axis=-1, keepdims=True) + EPSILON)
    normed_one = flat_rows * inverse_one
    hidden_one = (normed_one * gain_one.astype(jnp.float32)).astype(jnp.bfloat16)
    cosine, sine_part = rope_tables(positions.reshape(row_count), head_dim // 2)
    query_lin = jnp.dot(hidden_one, query_mat, preferred_element_type=jnp.float32).reshape(
        row_count, head_count, head_dim
    )
    queries = rotate(query_lin, cosine[:, None, :], sine_part[:, None, :]).astype(jnp.bfloat16)
    keys_local = rotate(
        jnp.dot(hidden_one, key_mat, preferred_element_type=jnp.float32), cosine, sine_part
    ).astype(jnp.bfloat16)
    values_local = jnp.dot(hidden_one, value_mat, preferred_element_type=jnp.float32).astype(
        jnp.bfloat16
    )
    keys_local = keys_local.reshape(micro_count, tok_rows, head_dim)
    values_local = values_local.reshape(micro_count, tok_rows, head_dim)
    keys_seq, values_seq, segment_seq = (
        lax.all_gather(keys_local, ("seq", "fsdp"), axis=1, tiled=True),
        lax.all_gather(values_local, ("seq", "fsdp"), axis=1, tiled=True),
        lax.all_gather(segments.astype(jnp.bfloat16), ("seq", "fsdp"), axis=1, tiled=True),
    )
    key_segment = segment_seq.astype(jnp.int32)
    pair_index = lax.axis_index("fsdp")
    query_place = (
        (jnp.arange(seq_size, dtype=jnp.int32)[:, None] * pair_size + pair_index) * tok_rows
        + jnp.arange(tok_rows, dtype=jnp.int32)[None, :]
    ).reshape(query_rows)
    query_segment = lax.dynamic_index_in_dim(
        key_segment.reshape(micro_count, seq_size, pair_size, tok_rows),
        pair_index,
        axis=2,
        keepdims=False,
    ).reshape(micro_count, query_rows)
    head_queries = lax.all_to_all(
        queries.reshape(micro_count, tok_rows, model_width),
        "seq",
        split_axis=2,
        concat_axis=1,
        tiled=True,
    )
    head_queries = head_queries.reshape(micro_count, query_rows, local_heads, head_dim)

    def forward_micro(micro_item):
        return attend_micro(micro_item, query_place, block_rows, score_scale)

    attended, log_total = lax.map(
        forward_micro, (head_queries, keys_seq, values_seq, query_segment, key_segment)
    )
    mixed_rows = lax.all_to_all(
        attended.reshape(micro_count, query_rows, local_heads * head_dim),
        "seq",
        split_axis=1,
        concat_axis=2,
        tiled=True,
    )
    mixed_rows = mixed_rows.reshape(row_count, model_width)
    middle = flat_rows + jnp.dot(mixed_rows, out_mat, preferred_element_type=jnp.float32)
    inverse_two = lax.rsqrt(jnp.mean(middle * middle, axis=-1, keepdims=True) + EPSILON)
    normed_two = middle * inverse_two
    hidden_two = (normed_two * gain_two.astype(jnp.float32)).astype(jnp.bfloat16)
    gate_proj = jnp.dot(hidden_two, gate_mat, preferred_element_type=jnp.float32)
    up_proj = jnp.dot(hidden_two, up_mat, preferred_element_type=jnp.float32)
    gate_sigmoid = jax.nn.sigmoid(gate_proj)
    gate_silu = gate_proj * gate_sigmoid
    hidden_mlp = (gate_silu * up_proj).astype(jnp.bfloat16)
    result = middle + jnp.dot(hidden_mlp, down_mat, preferred_element_type=jnp.float32)
    back_weights = (
        lax.all_gather(w_query, ("dp", "seq", "fsdp"), axis=0, tiled=True),
        lax.all_gather(w_key, ("dp", "seq", "fsdp"), axis=0, tiled=True),
        lax.all_gather(w_value, ("dp", "seq", "fsdp"), axis=0, tiled=True),
        lax.all_gather(w_out, ("dp", "seq", "fsdp"), axis=0, tiled=True),
        lax.all_gather(w_gate, ("dp", "seq", "fsdp"), axis=0, tiled=True),
        lax.all_gather(w_up, ("dp", "seq", "fsdp"), axis=0, tiled=True),
        lax.all_gather(w_down, ("dp", "seq", "fsdp"), axis=0, tiled=True),
        lax.all_gather(gain_attn, ("dp", "seq", "fsdp"), axis=0, tiled=True),
        lax.all_gather(gain_mlp, ("dp", "seq", "fsdp"), axis=0, tiled=True),
    )
    query_mat, key_mat, value_mat, out_mat, gate_mat, up_mat, down_mat, gain_one, gain_two = (
        back_weights
    )
    grad_rows = cotangent.reshape(row_count, model_width).astype(jnp.float32)
    grad_branch = cotangent.reshape(row_count, model_width)
    grad_down_w = jnp.einsum(
        "nf,nd->fd", hidden_mlp, grad_branch, preferred_element_type=jnp.float32
    )
    grad_hidden = jnp.einsum("nd,fd->nf", grad_branch, down_mat, preferred_element_type=jnp.float32)
    grad_gate_pre = (
        grad_hidden * up_proj * gate_sigmoid * (1.0 + gate_proj * (1.0 - gate_sigmoid))
    ).astype(jnp.bfloat16)
    grad_up_pre = (grad_hidden * gate_silu).astype(jnp.bfloat16)
    grad_gate_w = jnp.einsum(
        "nd,nf->df", hidden_two, grad_gate_pre, preferred_element_type=jnp.float32
    )
    grad_up_w = jnp.einsum("nd,nf->df", hidden_two, grad_up_pre, preferred_element_type=jnp.float32)
    grad_hidden_two = jnp.einsum(
        "nf,df->nd", grad_gate_pre, gate_mat, preferred_element_type=jnp.float32
    ) + jnp.einsum("nf,df->nd", grad_up_pre, up_mat, preferred_element_type=jnp.float32)
    grad_gain_two = jnp.sum(grad_hidden_two * normed_two, axis=0)
    grad_middle = grad_rows + norm_back(
        grad_hidden_two * gain_two.astype(jnp.float32), normed_two, inverse_two
    )
    grad_proj = grad_middle.astype(jnp.bfloat16)
    grad_out_w = jnp.einsum("nd,ne->de", mixed_rows, grad_proj, preferred_element_type=jnp.float32)
    grad_mixed = jnp.einsum(
        "ne,de->nd", grad_proj, out_mat, preferred_element_type=jnp.float32
    ).astype(jnp.bfloat16)
    grad_heads = lax.all_to_all(
        grad_mixed.reshape(micro_count, tok_rows, model_width),
        "seq",
        split_axis=2,
        concat_axis=1,
        tiled=True,
    )
    grad_heads = grad_heads.reshape(micro_count, query_rows, local_heads, head_dim)

    def backward_micro(micro_item):
        return attend_back(micro_item, query_place, block_rows, score_scale)

    grad_head_queries, grad_keys_seq, grad_values_seq = lax.map(
        backward_micro,
        (head_queries, keys_seq, values_seq, grad_heads, log_total, query_segment, key_segment),
    )
    grad_query_rows = lax.all_to_all(
        grad_head_queries.reshape(micro_count, query_rows, local_heads * head_dim).astype(
            jnp.bfloat16
        ),
        "seq",
        split_axis=1,
        concat_axis=2,
        tiled=True,
    ).astype(jnp.float32)
    grad_keys_own, grad_values_own = (
        lax.psum_scatter(
            grad_keys_seq.astype(jnp.bfloat16), ("seq", "fsdp"), scatter_dimension=1, tiled=True
        ).astype(jnp.float32),
        lax.psum_scatter(
            grad_values_seq.astype(jnp.bfloat16), ("seq", "fsdp"), scatter_dimension=1, tiled=True
        ).astype(jnp.float32),
    )
    grad_query_lin = (
        rotate(
            grad_query_rows.reshape(row_count, head_count, head_dim),
            cosine[:, None, :],
            -sine_part[:, None, :],
        )
        .reshape(row_count, model_width)
        .astype(jnp.bfloat16)
    )
    grad_key_lin = rotate(grad_keys_own.reshape(row_count, head_dim), cosine, -sine_part).astype(
        jnp.bfloat16
    )
    grad_value_lin = grad_values_own.reshape(row_count, head_dim).astype(jnp.bfloat16)
    grad_query_w = jnp.einsum(
        "nd,ne->de", hidden_one, grad_query_lin, preferred_element_type=jnp.float32
    )
    grad_key_w = jnp.einsum(
        "nd,ne->de", hidden_one, grad_key_lin, preferred_element_type=jnp.float32
    )
    grad_value_w = jnp.einsum(
        "nd,ne->de", hidden_one, grad_value_lin, preferred_element_type=jnp.float32
    )
    grad_hidden_one = jnp.einsum(
        "ne,de->nd", grad_query_lin, query_mat, preferred_element_type=jnp.float32
    )
    grad_hidden_one = grad_hidden_one + jnp.einsum(
        "ne,de->nd", grad_key_lin, key_mat, preferred_element_type=jnp.float32
    )
    grad_hidden_one = grad_hidden_one + jnp.einsum(
        "ne,de->nd", grad_value_lin, value_mat, preferred_element_type=jnp.float32
    )
    grad_gain_one = jnp.sum(grad_hidden_one * normed_one, axis=0)
    grad_input = grad_middle + norm_back(
        grad_hidden_one * gain_one.astype(jnp.float32), normed_one, inverse_one
    )
    matrix_grads = (
        grad_query_w,
        grad_key_w,
        grad_value_w,
        grad_out_w,
        grad_gate_w,
        grad_up_w,
        grad_down_w,
    )
    shards = tuple(
        lax.psum_scatter(
            grad.astype(jnp.bfloat16), ("dp", "seq", "fsdp"), scatter_dimension=0, tiled=True
        ).astype(jnp.float32)
        for grad in matrix_grads
    ) + (
        lax.psum_scatter(grad_gain_one, ("dp", "seq", "fsdp"), scatter_dimension=0, tiled=True),
        lax.psum_scatter(grad_gain_two, ("dp", "seq", "fsdp"), scatter_dimension=0, tiled=True),
    )
    layer_rows = result.reshape(micro_count, tok_rows, model_width).astype(jnp.bfloat16)
    return (
        layer_rows,
        keys_local,
        values_local,
        grad_input.reshape(micro_count, tok_rows, model_width),
        shards[0],
        shards[1],
        shards[2],
        shards[3],
        shards[4],
        shards[5],
        shards[6],
        shards[7],
        shards[8],
    )


BF16 = jnp.bfloat16
F32 = jnp.float32
MESH = pl.DeviceIdType.MESH
GROUPS = 64


def dot32(left, right, contract):
    return lax.dot_general(left, right, ((contract[0], contract[1]), ((), ())), preferred_element_type=F32)


def turn(vector, cosine, sine):
    return vector * cosine + pltpu.roll(vector, vector.shape[-1] // 2, 1) * sine


def scatter_sum(value, axes, dim):
    return lax.psum_scatter(value, axes, scatter_dimension=dim, tiled=True)


def send_plane(value, step):
    return lax.ppermute(value, "seq", [(i, i ^ step) for i in range(4)])


def send_core(value):
    return lax.ppermute(value, "fsdp", [(0, 1), (1, 0)])


def block_of(value, index, dim=0):
    return lax.dynamic_index_in_dim(value, index, axis=dim, keepdims=False)


def put_block(value, block, index, dim=0):
    return lax.dynamic_update_index_in_dim(value, block, index, axis=dim)


def swap_blocks(value, own):
    out = value
    for step in (1, 2, 3):
        other = own ^ step
        out = put_block(out, send_plane(block_of(value, other), step), other)
    return out


def scatter_core(value, core, dim):
    other = send_core(block_of(value, 1 - core, dim))
    return (block_of(value, core, dim).astype(F32) + other.astype(F32)).astype(BF16)


class Post:
    def __init__(self, send_sem, recv_sem):
        self.plane=lax.axis_index("dp"); self.own=lax.axis_index("seq"); self.core=lax.axis_index("fsdp")
        self.planes=lax.axis_size("dp")
        x=lax.rem(self.own,2); y=lax.div(self.own,2)
        self.by_x=self.own+1-2*x; self.by_y=self.own+2-4*y; self.far=3-self.own
        z,s,c=self.plane,self.own,self.core
        self.to_x=(z,self.by_x,c); self.to_y=(z,self.by_y,c); self.to_far=(z,self.far,c)
        self.to_core=(z,s,1-c)
        self.to_up=(lax.rem(z+1,self.planes),s,c); self.to_down=(lax.rem(z+self.planes-1,self.planes),s,c)
        self.has_up=z<self.planes-1; self.has_down=z>0
        self.send_sem, self.recv_sem = send_sem, recv_sem
        self.sent=[]
        self.steps={0:[(z,())]}
        for k in range(1,self.planes):
            self.steps[k]=[(jnp.clip(z-k,0,self.planes-1),(z-k>=0,)),(jnp.clip(z+k,0,self.planes-1),(z+k<=self.planes-1,))]
        self.groups={}
    def group(self, name):
        return self.groups.setdefault(name, len(self.groups))
    def barrier(self):
        bar=pltpu.get_barrier_semaphore()
        for t in (self.to_x,self.to_y,self.to_far,self.to_core):
            pl.semaphore_signal(bar,inc=1,device_id=t,device_id_type=MESH)
        for chip in (self.by_x,self.by_y,self.far):
            pl.semaphore_signal(bar,inc=1,device_id=(self.plane,chip,1-self.core),device_id_type=MESH)
        @pl.when(self.has_up)
        def _(): pl.semaphore_signal(bar,inc=1,device_id=self.to_up,device_id_type=MESH)
        @pl.when(self.has_down)
        def _(): pl.semaphore_signal(bar,inc=1,device_id=self.to_down,device_id_type=MESH)
        pl.semaphore_wait(bar,7+self.has_up.astype(jnp.int32)+self.has_down.astype(jnp.int32))
    def copy(self, src, dst, name, index, target, arrive=None):
        return pltpu.make_async_remote_copy(src_ref=src,dst_ref=dst,
            send_sem=self.send_sem.at[self.group(name),index],
            recv_sem=self.recv_sem.at[self.group(arrive or name),index],
            device_id=target,device_id_type=MESH)
    def send(self, src, dst, name, index, target, arrive=None, when=()):
        def go(): self.copy(src,dst,name,index,target,arrive).start()
        if when:
            cond=functools.reduce(jnp.logical_and,when)
            pl.when(cond)(go)
        else: go()
        self.sent.append((when,lambda: self.copy(src,dst,name,index,target,arrive).wait_send()))
    def wait(self, ref, name, index):
        self.copy(ref,ref,name,index,self.to_core).wait_recv()
    def finish(self):
        for when,w in self.sent:
            if when: pl.when(functools.reduce(jnp.logical_and,when))(w)
            else: w()

class Line:
    def __init__(self, post, name, unit, own_source):
        self.p, self.name, self.unit, self.src = post, name, unit, own_source
    def start(self):
        p=self.p
        p.send(self.src,self.unit(p.plane),self.name+"_up",p.plane,p.to_up,self.name,(p.has_up,))
        p.send(self.src,self.unit(p.plane),self.name+"_down",p.plane,p.to_down,self.name,(p.has_down,))
    def hop(self, k, then=None):
        p=self.p
        for sign,(at,(here,)) in zip((-1,1),p.steps[k]):
            on=p.has_up if sign<0 else p.has_down
            target=p.to_up if sign<0 else p.to_down
            ref=self.unit(at)
            @pl.when(here)
            def _(ref=ref,at=at): p.wait(ref,self.name,at)
            if k<p.planes-1:
                p.send(ref,ref,self.name+("_up" if sign<0 else "_down"),at,target,self.name,(here,on))
            if then: then(at,here)

class Spread:
    def __init__(self, post, name, unit, low, high):
        self.p,self.name,self.unit,self.low,self.high=post,name,unit,low,high
    def start(self, index, source, when=()):
        p=self.p
        dst=self.unit(index,p.own)
        p.send(source,dst,self.name+"_x",index,p.to_x,None,when)
        p.send(source,dst,self.name+"_y",index,p.to_y,None,when)
    def relay(self, index, when=()):
        p=self.p
        def go(f):
            if when: pl.when(functools.reduce(jnp.logical_and,when))(f)
            else: f()
        go(lambda: p.wait(self.unit(index,p.by_x),self.name+"_x",index))
        ref=self.low(index,p.by_x)
        p.send(ref,ref,self.name+"_l",index,p.to_y,None,when)
        go(lambda: p.wait(self.unit(index,p.by_y),self.name+"_y",index))
        ref=self.high(index,p.by_y)
        p.send(ref,ref,self.name+"_h",index,p.to_x,None,when)
    def arrive(self, index, when=()):
        p=self.p
        def go():
            p.wait(self.low(index,p.far),self.name+"_l",index)
            p.wait(self.high(index,p.far),self.name+"_h",index)
        if when: pl.when(functools.reduce(jnp.logical_and,when))(go)
        else: go()


def dot2(l, r, ca, cb):
    return dot32(l, r, ((ca,), (cb,)))


def front_kernel(plan,tok,cot,marks,wq_in,wo_in,gu_in,wd_in,freq,
    x_out,marks_out,wq_out,wo_out,gu,wd,E,two,middle_out,h1_out,q_out,att_out,kv_out,home,cos_out,sin_out,
    send_sem,recv_sem,local_sem,b_cot,b_gu,b_wd,
    x_v,marks_v,wq_v,wo_v,h1_v,lin_v,q_v,att_v,kv_v,mid_v,two_v,cos_v,sin_v,gain_v):
    tile,width,head_dim,group=plan
    scale=head_dim**-0.5
    p=Post(send_sem,recv_sem)
    z,s,c=p.plane,p.own,p.core
    chips=4
    rows=chips*tile
    groups=width//group; heads=group//head_dim
    qkv=width+2*head_dim
    count=[0]
    outs_=[]
    def local(src,dst):
        cp=pltpu.make_async_copy(src,dst,local_sem.at[count[0]]); count[0]+=1
        cp.start(); return cp
    def out(src,dst):
        outs_.append(local(src,dst))
    loads=[local(tok.at[s],x_v.at[s]),local(marks.at[s],marks_v.at[c,s]),local(wq_in,wq_v.at[z,s,c]),local(wo_in,wo_v.at[z,s,c])]
    late=[local(cot,b_cot),local(gu_in.at[s],b_gu),local(wd_in,b_wd)]
    p.barrier()
    def attention_weight(name, arr, src):
        n=arr.shape[3]//2
        spread=Spread(p,name,lambda a,b: arr.at[a,b,c],lambda a,b: arr.at[a,b,c,pl.ds(0,n)],lambda a,b: arr.at[a,b,c,pl.ds(n,n)])
        line=Line(p,name+"_z",lambda a: arr.at[a,s,c],src)
        return spread,line
    q_spread,q_line=attention_weight("wq",wq_v,wq_in)
    o_spread,o_line=attention_weight("wo",wo_v,wo_in)
    def each(k, f):
        for at,when in p.steps[k]: f(at,when)
    def to_sibling(name, arr, a, when):
        ref=arr.at[a,:,c]
        p.send(ref,ref,name+"_c",a,p.to_core,None,when)
    others=((p.to_x,p.by_x),(p.to_y,p.by_y),(p.to_far,p.far))
    def swap(src,dst_of,name):
        for i,(t,o) in enumerate(others):
            p.send(src.at[o],dst_of(s),name,i,t)
    def swapped(dst_of,name):
        for i,(t,o) in enumerate(others):
            p.wait(dst_of(o),name,i)
    q_line.start()
    swap(tok,lambda b: x_v.at[b],"tok")
    q_spread.start(z,wq_in)
    for i,(t,o) in enumerate(others):
        p.send(marks.at[o],marks_v.at[c,s],"mk",i,t)
        p.send(marks.at[o],marks_v.at[c,s],"mk2",i,(z,o,1-c))
    p.send(marks.at[s],marks_v.at[c,s],"mk2",3,p.to_core)
    fwd=lambda a,here: q_spread.start(a,wq_v.at[a,s,c],(here,))
    wd_line=Line(p,"wd_z",lambda a: wd.at[a,c],wd_in)
    gu_line=Line(p,"gu_z",lambda a: gu.at[a,:,c],gu.at[z,:,c])
    q_line.hop(1,fwd)
    wd_line.start()
    q_line.hop(2,fwd)
    q_line.hop(3,fwd)
    swap(gu_in,lambda b: gu.at[z,b,c],"gu")
    for cp in loads+late: cp.wait()
    out(b_cot,E.at[:,s]); out(b_gu,gu.at[z,s,c]); own_gu=outs_[-1]; out(b_wd,wd.at[z,c]); own_wd=outs_[-1]
    for k in range(4): each(k,lambda a,w: q_spread.relay(a,w))
    o_line.start(); o_spread.start(z,wo_in)
    def each_q(a,w):
        q_spread.arrive(a,w); to_sibling("wq",wq_v,a,w)
    for k in range(4): each(k,each_q)
    swapped(lambda b: x_v.at[b],"tok")
    for i,(t,o) in enumerate(others):
        p.wait(marks_v.at[c,o],"mk",i); p.wait(marks_v.at[1-c,o],"mk2",i)
    p.wait(marks_v.at[1-c,s],"mk2",3)
    swapped(lambda b: gu.at[z,b,c],"gu")
    own_gu.wait(); outs_[:]=[o for o in outs_ if o is not own_gu]
    gu_line.start(); to_sibling("gu",gu,z,())
    for a in range(4): p.wait(wq_v.at[a,:,1-c],"wq_c",a)
    out(x_v,x_out); out(marks_v,marks_out); out(wq_v,wq_out)
    ofwd=lambda a,here: o_spread.start(a,wo_v.at[a,s,c],(here,))
    gufwd=lambda a,here: to_sibling("gu",gu,a,(here,))
    e_parts=[]
    for i in range(2):
        def sub(lo,n,i=i): return lambda _,b: E.at[pl.ds(2*i+lo,n),b]
        e_parts.append(Spread(p,"E%d"%i,sub(0,2),sub(0,1),sub(1,1)))
    def e_start(i):
        for t,nm in ((p.to_x,"_x"),(p.to_y,"_y")):
            p.send(cot.at[pl.ds(2*i,2)],E.at[pl.ds(2*i,2),s],"E%d"%i+nm,0,t)
    for i in range(width//head_dim):
        a,b=divmod(i,4)
        block=wq_v[a,b,:,:,pl.ds(qkv,head_dim)].reshape(head_dim,head_dim).astype(F32)
        gain_v[:,pl.ds(i*head_dim,head_dim)]=jnp.transpose(block)[0:8]
    def norm_block(b,carry):
        x=x_v[b].astype(F32)
        inv=lax.rsqrt(jnp.mean(x*x,axis=-1,keepdims=True)+EPSILON)
        h1_v[pl.ds(b*tile,tile),:]=(x*inv*gain_v[0:1,:]).astype(BF16)
        return carry
    lax.fori_loop(0,chips,norm_block,0)
    lane=lax.broadcasted_iota(jnp.int32,(1,head_dim),1)
    sign=jnp.where(lane<head_dim//2,-1.0,1.0).astype(F32)
    seg_cols=[]
    for b in range(chips):
        m=jnp.transpose(marks_v[c,b].astype(F32))
        angle=m[:,1:2]*freq[...]
        cos_v[pl.ds(b*tile,tile),:]=jnp.cos(angle); sin_v[pl.ds(b*tile,tile),:]=jnp.sin(angle)*sign
        seg_cols.append(m[:,0:1])
    key_seg=jnp.concatenate([marks_v[k%2,k//2,0:1,:] for k in range(2*chips)],axis=1).astype(F32)
    o_line.hop(1,ofwd)
    w=wq_v[:,:,:,:,pl.ds(width,2*head_dim)].reshape(width,2*head_dim)
    kv=dot2(h1_v[...],w,1,0)
    kv=jnp.concatenate([turn(kv[:,:head_dim],cos_v[...],sin_v[...]),kv[:,head_dim:]],axis=1).astype(BF16)
    kv_v[:,pl.ds(c,1)]=kv.reshape(chips,1,tile,2*head_dim)
    p.send(kv_v.at[:,c],kv_v.at[:,c],"kv",0,p.to_core)
    swap(kv_v.at[:,c],lambda b: home.at[b],"home")
    out(kv_v.at[s,c],home.at[s]); out(h1_v,h1_out); out(cos_v,cos_out); out(sin_v,sin_out)
    steps={0:[lambda: o_line.hop(2,ofwd)],
           1:[lambda: p.wait(kv_v.at[:,1-c],"kv",0), lambda: o_line.hop(3,ofwd)],
           2:[lambda: wd_line.hop(1), lambda: each(0,lambda a,w: o_spread.relay(a,w)), lambda: each(1,lambda a,w: o_spread.relay(a,w))],
           3:[lambda: each(2,lambda a,w: o_spread.relay(a,w)), lambda: each(3,lambda a,w: o_spread.relay(a,w)),lambda: gu_line.hop(1,gufwd)],
           4:[lambda: wd_line.hop(2), lambda: e_start(0)]}
    def lin_group(g,carry):
        w=wq_v[:,:,:,:,pl.ds(pl.multiple_of(g*group,group),group)].reshape(width,group)
        lin_v[...]=dot2(h1_v[...],w,1,0)
        for b in range(chips):
            cos,sin=cos_v[pl.ds(b*tile,tile),:],sin_v[pl.ds(b*tile,tile),:]
            for h in range(heads):
                part=lin_v[pl.ds(b*tile,tile),pl.ds(h*head_dim,head_dim)]
                q_v[pl.ds(b*tile,tile),pl.ds(pl.multiple_of(g*group+h*head_dim,head_dim),head_dim)]=turn(part,cos,sin).astype(BF16)
        return carry
    for f in steps[0]: f()
    lax.fori_loop(0,groups,lin_group,0)
    for f in steps[1]: f()
    out(kv_v,kv_out); out(q_v,q_out)
    def attend_group(g,carry):
        for b in range(chips):
            extent=(b+1)*2*tile
            at=lambda h: pl.ds(pl.multiple_of(g*group+h*head_dim,head_dim),head_dim)
            q=jnp.concatenate([q_v[pl.ds(b*tile,tile),at(h)] for h in range(heads)],axis=0)
            kvs=kv_v[pl.ds(0,b+1)].reshape(extent,2*head_dim)
            place=(2*b+c)*tile+lax.broadcasted_iota(jnp.int32,(tile,extent),0)
            seen=lax.broadcasted_iota(jnp.int32,(tile,extent),1)
            allowed=(place>=seen)&(seg_cols[b]==key_seg[:,:extent])
            bias=jnp.where(allowed,0.0,MASKED).astype(F32)
            sc=dot2(q,kvs[:,:head_dim],1,1)*scale
            sc=(sc.reshape(heads,tile,extent)+bias[None]).reshape(heads*tile,extent)
            top=jnp.max(sc,axis=-1,keepdims=True)
            e=jnp.exp(sc-top)
            soft=(e*(1.0/jnp.sum(e,axis=-1,keepdims=True))).astype(BF16)
            mixed=dot2(soft,kvs[:,head_dim:],1,0).astype(BF16)
            for h in range(heads):
                att_v[pl.ds(b*tile,tile),at(h)]=mixed[h*tile:(h+1)*tile]
        for i in (2,3):
            @pl.when(g==i-1)
            def _(i=i):
                for f in steps[i]: f()
        return carry
    lax.fori_loop(0,groups,attend_group,0)
    out(att_v,att_out)
    def each_o(a,w):
        o_spread.arrive(a,w); to_sibling("wo",wo_v,a,w)
    for k in range(4): each(k,each_o)
    for f in steps[4]: f()
    for a in range(4): p.wait(wo_v.at[a,:,1-c],"wo_c",a)
    out(wo_v,wo_out)
    def project(g,carry):
        at=pl.ds(pl.multiple_of(g*group,group),group)
        w=wo_v[:,:,:,:,at].reshape(width,group)
        lin_v[...]=dot2(att_v[...],w,1,0)
        for b in range(chips):
            mid_v[pl.ds(b*tile,tile),at]=x_v[b,:,at].astype(F32)+lin_v[pl.ds(b*tile,tile),:]
        return carry
    lax.fori_loop(0,groups,project,0)
    out(mid_v,middle_out)
    def norm_two(b,carry):
        at=pl.ds(pl.multiple_of(b*tile,tile),tile)
        m=mid_v[at,:]
        inv=lax.rsqrt(jnp.mean(m*m,axis=-1,keepdims=True)+EPSILON)
        two_v[at,:]=(m*inv*gain_v[1:2,:]).astype(BF16)
        return carry
    lax.fori_loop(0,chips,norm_two,0)
    half=rows//2
    two_spread=Spread(p,"two",lambda _,b: two.at[b],lambda _,b: two.at[b,pl.ds(0,half)],lambda _,b: two.at[b,pl.ds(half,half)])
    two_spread.start(0,two_v)
    out(two_v,two.at[s])
    e_start(1)
    wd_line.hop(3)
    gu_line.hop(2,gufwd)
    e_parts[0].relay(0)
    own_wd.wait(); outs_[:]=[o for o in outs_ if o is not own_wd]
    p.send(wd.at[:,c],wd.at[:,c],"wd_c",0,p.to_core)
    gu_line.hop(3,gufwd)
    two_spread.relay(0)
    e_parts[0].arrive(0)
    e_parts[1].relay(0)
    two_spread.arrive(0)
    e_parts[1].arrive(0)
    p.wait(wd.at[:,1-c],"wd_c",0)
    for a in range(4): p.wait(gu.at[a,:,1-c],"gu_c",a)
    swapped(lambda b: home.at[b],"home")
    for cp in outs_: cp.wait()
    p.finish()
    assert len(p.groups)<=GROUPS, len(p.groups)

def front(tok,cot,marks,wq_in,wo_in,gu_in,wd_in):
    Z,S,C=lax.axis_size("dp"),lax.axis_size("seq"),lax.axis_size("fsdp")
    sd=jax.ShapeDtypeStruct
    micro,tile,width=tok.shape
    rows=micro*tile
    head_dim=128
    group=512
    half=head_dim//2
    freq=jnp.exp(-jnp.log(jnp.float32(10000.0))*jnp.arange(half,dtype=F32)/half)
    freq=jnp.concatenate([freq,freq])[None]
    outs=[sd((S,tile,width),BF16),sd((C,)+marks.shape,jnp.int32),sd((Z,S,C)+wq_in.shape,BF16),sd((Z,S,C)+wo_in.shape,BF16),
          sd((Z,S,C)+gu_in.shape[1:],BF16),sd((Z,C)+wd_in.shape,BF16),sd((S,)+cot.shape,BF16),
          sd((S,rows,width),BF16),sd((rows,width),F32),sd((rows,width),BF16),sd((rows,width),BF16),sd((rows,width),BF16),
          sd((S,C,tile,2*head_dim),BF16),sd((S,tile,2*head_dim),BF16),sd((rows,head_dim),F32),sd((rows,head_dim),F32)]
    anyspec=pl.BlockSpec(memory_space=pl.ANY)
    V=pltpu.VMEM
    return pl.pallas_call(functools.partial(front_kernel,(tile,width,head_dim,group)),out_shape=outs,
        in_specs=[anyspec]*7+[pl.BlockSpec(memory_space=V)],out_specs=[anyspec]*len(outs),
        scratch_shapes=[pltpu.SemaphoreType.DMA((GROUPS,4)),pltpu.SemaphoreType.DMA((GROUPS,4)),pltpu.SemaphoreType.DMA((32,)),
          V(cot.shape,BF16),V(gu_in.shape[1:],BF16),V(wd_in.shape,BF16),
          V((S,tile,width),BF16),V((C,)+marks.shape,jnp.int32),V((Z,S,C)+wq_in.shape,BF16),V((Z,S,C)+wo_in.shape,BF16),
          V((rows,width),BF16),V((rows,group),F32),V((rows,width),BF16),V((rows,width),BF16),V((S,C,tile,2*head_dim),BF16),
          V((rows,width),F32),V((rows,width),BF16),V((rows,head_dim),F32),V((rows,head_dim),F32),V((8,width),F32)],
        compiler_params=pltpu.CompilerParams(collective_id=1,has_side_effects=True,vmem_limit_bytes=60*1024*1024),name="front")(tok,cot,marks,wq_in,wo_in,gu_in,wd_in,freq)


def back_kernel(
    plan,
    gh2,
    grads_in,
    middle,
    x_in,
    wq,
    wo,
    h1t_in,
    q_in,
    att_t_in,
    kv_in,
    cos_in,
    sin_in,
    marks_in,
    gain_v,
    home,
    gq_out,
    gkv_out,
    go_out,
    send_sem,
    recv_sem,
    local_sem,
    mid_v,
    gh1_v,
    x_v,
    proj_v,
    h1t_v,
    q_v,
    att_t_v,
    kv_v,
    cos_v,
    sin_v,
    marks_v,
    wo_b,
    wq_b,
    wk_v,
    mix_v,
    lin_v,
    kvacc,
    kvx,
    gains_acc,
    sq,
    so,
    rq,
    ro,
    tq,
    to,
    pq,
    po,
    uq,
    uo,
    zq,
    zo,
    skv,
    rkv,
    tkv,
    pkv,
    ukv,
    zkv,
    gl_v,
):
    tile, width, head_dim, group = plan
    scale = head_dim**-0.5
    chips, planes = 4, 4
    rows = chips * tile
    groups = width // group
    heads = group // head_dim
    shard = sq.shape[3]
    p = Post(send_sem, recv_sem)
    z, s, c = p.plane, p.own, p.core
    others = ((p.to_x, p.by_x), (p.to_y, p.by_y), (p.to_far, p.far))
    lines = [lax.rem(z + k, planes) for k in range(1, planes)]
    bar = pltpu.get_barrier_semaphore()

    def load(src, dst, index):
        return pltpu.make_async_copy(src, dst, local_sem.at[index])

    first = [
        load(gh2, q_v, 0),
        load(middle, mid_v, 1),
        load(grads_in.at[s], x_v, 2),
    ]
    second = [
        load(h1t_in, h1t_v, 3),
        load(att_t_in, att_t_v, 5),
        load(kv_in, kv_v, 6),
        load(cos_in, cos_v, 7),
        load(sin_in, sin_v, 8),
        load(marks_in, marks_v, 9),
        load(wq.at[:, :, :, :, pl.ds(width, 2 * head_dim)], wk_v, 10),
    ]
    tokens_again = load(x_in, x_v, 11)

    def fetch(g):
        at = pl.ds(pl.multiple_of(g * group, group), group)
        slot = lax.rem(g, 2)
        return (
            load(wo.at[g], wo_b.at[slot], 12 + slot),
            load(wq.at[:, :, :, :, at], wq_b.at[slot], 14 + slot),
        )

    for cp in first + second:
        cp.start()
    for cp in fetch(0):
        cp.start()
    for target in [t for t, _ in others] + [p.to_core] + [(a, s, c) for a in lines]:
        pl.semaphore_signal(bar, inc=1, device_id=target, device_id_type=MESH)
    pl.semaphore_wait(bar, 7)

    def stage_a(g):
        slot = lax.rem(g, 2)
        return (
            p.copy(sq.at[:, :, 1 - c], rq.at[slot], "aq", g, p.to_core),
            p.copy(so.at[:, 1 - c], ro.at[slot], "ao", g, p.to_core),
        )

    def stage_b(g):
        slot = lax.rem(g, 2)
        copies = []
        for i, (target, other) in enumerate(others):
            copies.append(p.copy(tq.at[slot, :, other], pq.at[g, i], "bq%d" % i, g, target))
            copies.append(p.copy(to.at[slot, other], po.at[g, i], "bo%d" % i, g, target))
        return copies

    def stage_c(g):
        slot = lax.rem(g, 2)
        return [
            p.copy(uq.at[slot, a], zq.at[g, k], "cq%d" % k, g, (a, s, c))
            for k, a in enumerate(lines)
        ]

    def stage_c_out(g, k):
        return p.copy(uo.at[lax.rem(g, 2)], zo.at[k], "co", k, (g, s, c))

    def wide(value):
        return value.astype(F32)

    def do_b(g):
        slot = lax.rem(g, 2)
        for cp in stage_a(g):
            cp.wait_recv()

        @pl.when(g >= 2)
        def _():
            for cp in stage_b(g - 2):
                cp.wait_send()

        def one(a, carry):
            tq[slot, a] = (wide(sq[a, :, c]) + wide(rq[slot, a])).astype(BF16)
            to[slot, a] = (wide(so[a, c]) + wide(ro[slot, a])).astype(BF16)
            return carry

        lax.fori_loop(0, planes, one, 0)
        for cp in stage_b(g):
            cp.start()

    def do_c(g):
        slot = lax.rem(g, 2)
        for cp in stage_b(g):
            cp.wait_recv()
        total = wide(tq[slot, :, s])
        mixed = wide(to[slot, s])
        for i in range(3):
            total = total + wide(pq[g, i])
            mixed = mixed + wide(po[g, i])
        uq[slot] = total.astype(BF16)
        uo[slot] = mixed.astype(BF16)
        for cp in stage_c(g):
            cp.start()
        for k in range(1, planes):

            @pl.when(lax.rem(g + planes - z, planes) == k)
            def _(k=k):
                stage_c_out(g, k - 1).start()

    def do_d(g):
        slot = lax.rem(g, 2)
        total = wide(uq[slot, z])
        for k, cp in enumerate(stage_c(g)):
            cp.wait_recv()
            total = total + wide(zq[g, k])
        gq_out[:, pl.ds(pl.multiple_of(g * group, group), group)] = total

        @pl.when(z == g)
        def _():
            mixed = wide(uo[slot])
            for k in range(planes - 1):
                stage_c_out(g, k).wait_recv()
                mixed = mixed + wide(zo[k])
            go_out[...] = mixed

        for k in range(1, planes):

            @pl.when(lax.rem(g + planes - z, planes) == k)
            def _(k=k):
                stage_c_out(g, k - 1).wait_send()

        for cp in stage_c(g):
            cp.wait_send()

    for cp in first:
        cp.wait()
    gains_acc[...] = jnp.zeros_like(gains_acc)

    def norm_two(b, carry):
        at = pl.ds(pl.multiple_of(b * tile, tile), tile)
        m = mid_v[at, :]
        inv = lax.rsqrt(jnp.mean(m * m, axis=-1, keepdims=True) + EPSILON)
        normed = m * inv
        grad = wide(q_v[at, :])
        gains_acc[1:2, :] += jnp.sum(grad * normed, axis=0, keepdims=True)
        grad = grad * gain_v[1:2, :]
        grad = wide(x_v[b]) + inv * (grad - normed * jnp.mean(grad * normed, axis=-1, keepdims=True))
        mid_v[at, :] = grad
        proj_v[at, :] = grad.astype(BF16)
        gh1_v[at, :] = jnp.zeros_like(grad)
        return carry

    lax.fori_loop(0, chips, norm_two, 0)
    tokens_again.start()
    queries = load(q_in, q_v, 4)
    queries.start()
    for cp in second + [queries]:
        cp.wait()
    kvacc[...] = jnp.zeros_like(kvacc)
    seg_cols = [jnp.transpose(marks_v[c, b].astype(F32))[:, 0:1] for b in range(chips)]
    key_seg = jnp.concatenate(
        [marks_v[k % 2, k // 2, 0:1, :] for k in range(2 * chips)], axis=1
    ).astype(F32)

    def one_group(g, carry):
        slot = lax.rem(g, 2)
        column = pl.multiple_of(g * group, group)
        for cp in fetch(g):
            cp.wait()

        @pl.when(g + 1 < groups)
        def _():
            for cp in fetch(g + 1):
                cp.start()

        w = wo_b[slot].reshape(group, width)
        mix_v[...] = dot2(proj_v[...], w, 1, 1).astype(BF16)
        for b in range(chips):
            extent = (b + 1) * 2 * tile
            at = pl.ds(b * tile, tile)
            kvs = kv_v[pl.ds(0, b + 1)].reshape(extent, 2 * head_dim)
            keys, values = kvs[:, :head_dim], kvs[:, head_dim:]
            place = (2 * b + c) * tile + lax.broadcasted_iota(jnp.int32, (tile, extent), 0)
            seen = lax.broadcasted_iota(jnp.int32, (tile, extent), 1)
            allowed = (place >= seen) & (seg_cols[b] == key_seg[:, :extent])
            bias = jnp.where(allowed, 0.0, MASKED).astype(F32)
            cosine, sine = cos_v[at, :], sin_v[at, :]
            for first_head in range(0, heads, 2):
                span = range(first_head, first_head + 2)
                q = jnp.concatenate(
                    [q_v[at, pl.ds(pl.multiple_of(column + h * head_dim, head_dim), head_dim)] for h in span],
                    axis=0,
                )
                grads = jnp.concatenate(
                    [mix_v[at, pl.ds(h * head_dim, head_dim)] for h in span], axis=0
                )
                scores = dot2(q, keys, 1, 1) * scale
                scores = (scores.reshape(2, tile, extent) + bias[None]).reshape(2 * tile, extent)
                top = jnp.max(scores, axis=-1, keepdims=True)
                soft = jnp.exp(scores - top)
                soft = soft * (1.0 / jnp.sum(soft, axis=-1, keepdims=True))
                grad_soft = dot2(grads, values, 1, 1)
                inner = jnp.sum(soft * grad_soft, axis=-1, keepdims=True)
                grad_scores = (soft * (grad_soft - inner)).astype(BF16)
                both = jnp.concatenate(
                    [dot2(grad_scores, q, 0, 0) * scale, dot2(soft.astype(BF16), grads, 0, 0)],
                    axis=1,
                )
                kvacc[pl.ds(0, b + 1)] += both.reshape(b + 1, 2, tile, 2 * head_dim)
                grad_q = dot2(grad_scores, keys, 1, 0) * scale
                for i, h in enumerate(span):
                    part = turn(grad_q[i * tile : (i + 1) * tile], cosine, -sine)
                    lin_v[at, pl.ds(h * head_dim, head_dim)] = part.astype(BF16)

        @pl.when(g >= 1)
        def _():
            do_b(g - 1)
            for cp in stage_a(g - 1):
                cp.wait_send()

        left = att_t_v[pl.ds(column, group), :]

        def weights(n, carry):
            at = pl.ds(pl.multiple_of(n * group, group), group)
            part = dot2(h1t_v[at, :], lin_v[...], 1, 0)
            sq[n] = part.astype(BF16).reshape(chips, 2, shard, group)
            part = dot2(left, proj_v[:, at], 1, 0)
            so[:, :, :, at] = part.astype(BF16).reshape(chips, 2, shard, group)
            return carry

        lax.fori_loop(0, planes, weights, 0)
        for cp in stage_a(g):
            cp.start()

        def inputs(n, carry):
            at = pl.ds(pl.multiple_of(n * group, group), group)
            gh1_v[:, at] += dot2(lin_v[...], wq_b[slot, n].reshape(group, group), 1, 1)
            return carry

        lax.fori_loop(0, planes, inputs, 0)

        @pl.when(g >= 2)
        def _():
            do_c(g - 2)

        @pl.when(g >= 3)
        def _():
            do_d(g - 3)

        return carry

    lax.fori_loop(0, groups, one_group, 0)

    to_other = p.copy(kvacc.at[:, 1 - c], kvx, "kx", 0, p.to_core)
    to_other.start()
    do_b(groups - 1)
    to_other.wait_recv()
    for b in range(chips):
        at = pl.ds(b * tile, tile)
        part = kvacc[b, c] + kvx[b]
        turned = turn(part[:, :head_dim], cos_v[at, :], -sin_v[at, :])
        gl_v[at, :] = jnp.concatenate([turned, part[:, head_dim:]], axis=1).astype(BF16)

    def last_inputs(n, carry):
        at = pl.ds(pl.multiple_of(n * group, group), group)
        gh1_v[:, at] += dot2(gl_v[...], wk_v[n].reshape(group, 2 * head_dim), 1, 1)
        part = dot2(h1t_v[at, :], gl_v[...], 1, 0).astype(BF16)
        skv[n, :, :, :, pl.ds(0, 2 * head_dim)] = part.reshape(chips, 2, shard, 2 * head_dim)
        return carry

    lax.fori_loop(0, planes, last_inputs, 0)
    tokens_again.wait()

    def norm_one(b, carry):
        at = pl.ds(pl.multiple_of(b * tile, tile), tile)
        x = wide(x_v[b])
        inv = lax.rsqrt(jnp.mean(x * x, axis=-1, keepdims=True) + EPSILON)
        normed = x * inv
        grad = gh1_v[at, :]
        gains_acc[0:1, :] += jnp.sum(grad * normed, axis=0, keepdims=True)
        grad = grad * gain_v[0:1, :]
        grad = mid_v[at, :] + inv * (
            grad - normed * jnp.mean(grad * normed, axis=-1, keepdims=True)
        )
        proj_v[at, :] = grad.astype(BF16)
        return carry

    lax.fori_loop(0, chips, norm_one, 0)
    for i in range(width // head_dim):
        part = gains_acc[:, pl.ds(i * head_dim, head_dim)]
        part = jnp.concatenate([part, jnp.zeros((head_dim - 8, head_dim), F32)], axis=0)
        part = jnp.transpose(part).astype(BF16).reshape(2, shard, head_dim)
        skv[i // 4, i % 4, :, :, pl.ds(2 * head_dim, head_dim)] = part
    a_kv = p.copy(skv.at[:, :, 1 - c], rkv, "akv", 0, p.to_core)
    a_kv.start()
    homes = [
        p.copy(proj_v.at[pl.ds(pl.multiple_of(o * tile, tile), tile)], home.at[s], "home", i, t)
        for i, (t, o) in enumerate(others)
    ]
    do_c(groups - 2)
    a_kv.wait_recv()

    def last_b(a, carry):
        tkv[a] = (wide(skv[a, :, c]) + wide(rkv[a])).astype(BF16)
        return carry

    lax.fori_loop(0, planes, last_b, 0)
    b_kv = [
        p.copy(tkv.at[:, o], pkv.at[i], "bkv", i, t) for i, (t, o) in enumerate(others)
    ]
    for cp in b_kv:
        cp.start()
    for cp in homes:
        cp.start()
    own_home = load(proj_v.at[pl.ds(pl.multiple_of(s * tile, tile), tile)], home.at[s], 0)
    own_home.start()
    do_d(groups - 3)
    do_c(groups - 1)
    do_d(groups - 2)
    total = wide(tkv[:, s])
    for i, cp in enumerate(b_kv):
        cp.wait_recv()
        total = total + wide(pkv[i])
    ukv[...] = total.astype(BF16)
    c_kv = [
        p.copy(ukv.at[a], zkv.at[k], "ckv", k, (a, s, c)) for k, a in enumerate(lines)
    ]
    for cp in c_kv:
        cp.start()
    do_d(groups - 1)
    total = wide(ukv[z])
    for k, cp in enumerate(c_kv):
        cp.wait_recv()
        total = total + wide(zkv[k])
    gkv_out[...] = total
    for cp in homes:
        cp.wait_recv()
    own_home.wait()
    for cp in [to_other, a_kv] + b_kv + c_kv + homes:
        cp.wait_send()
    for cp in list(stage_a(groups - 1)) + stage_b(groups - 2) + stage_b(groups - 1):
        cp.wait_send()


def back(tile, gh2, grads_in, middle, x_in, wq, wo, h1t, q, att_t, kv, cosine, sine, marks, gains):
    planes, chips, pair, shard, width = wo.shape
    rows = chips * tile
    head_dim = kv.shape[-1] // 2
    group = 512
    groups = width // group
    last = wq.shape[-1] - width
    V = pltpu.VMEM
    sd = jax.ShapeDtypeStruct
    outs = [
        sd((chips, tile, width), BF16),
        sd((shard, width), F32),
        sd((shard, last), F32),
        sd((shard, width), F32),
    ]
    anyspec = pl.BlockSpec(memory_space=pl.ANY)
    inner = pl.BlockSpec(memory_space=V)
    scratch = [
        pltpu.SemaphoreType.DMA((GROUPS, 4)),
        pltpu.SemaphoreType.DMA((GROUPS, 4)),
        pltpu.SemaphoreType.DMA((16,)),
        V((rows, width), F32),
        V((rows, width), F32),
        V((chips, tile, width), BF16),
        V((rows, width), BF16),
        V((width, rows), BF16),
        V((rows, width), BF16),
        V((width, rows), BF16),
        V((chips, pair, tile, 2 * head_dim), BF16),
        V((rows, head_dim), F32),
        V((rows, head_dim), F32),
        V(marks.shape, jnp.int32),
        V((2, chips, pair, shard, width), BF16),
        V((2, planes, chips, pair, shard, group), BF16),
        V((planes, chips, pair, shard, 2 * head_dim), BF16),
        V((rows, group), BF16),
        V((rows, group), BF16),
        V((chips, pair, tile, 2 * head_dim), F32),
        V((chips, tile, 2 * head_dim), F32),
        V((8, width), F32),
        V((planes, chips, pair, shard, group), BF16),
        V((chips, pair, shard, width), BF16),
        V((2, planes, chips, shard, group), BF16),
        V((2, chips, shard, width), BF16),
        V((2, planes, chips, shard, group), BF16),
        V((2, chips, shard, width), BF16),
        V((groups, 3, planes, shard, group), BF16),
        V((groups, 3, shard, width), BF16),
        V((2, planes, shard, group), BF16),
        V((2, shard, width), BF16),
        V((groups, 3, shard, group), BF16),
        V((3, shard, width), BF16),
        V((planes, chips, pair, shard, last), BF16),
        V((planes, chips, shard, last), BF16),
        V((planes, chips, shard, last), BF16),
        V((3, planes, shard, last), BF16),
        V((planes, shard, last), BF16),
        V((3, shard, last), BF16),
        V((rows, 2 * head_dim), BF16),
    ]
    return pl.pallas_call(
        functools.partial(back_kernel, (tile, width, head_dim, group)),
        out_shape=outs,
        in_specs=[anyspec] * 13 + [inner],
        out_specs=[anyspec] + [inner] * 3,
        scratch_shapes=scratch,
        compiler_params=pltpu.CompilerParams(
            collective_id=2, has_side_effects=True, vmem_limit_bytes=63 * 1024 * 1024
        ),
        cost_estimate=pl.CostEstimate(
            flops=60_000_000_000, bytes_accessed=60_000_000, transcendentals=10_000_000
        ),
        name="back",
    )(gh2, grads_in, middle, x_in, wq, wo, h1t, q, att_t, kv, cosine, sine, marks, gains)


def middle_kernel(
    plan,
    two,
    grads,
    gate_up,
    down,
    residual,
    pre_out,
    hidden_out,
    partial_out,
    sum_out,
    send_sem,
    recv_sem,
    local_sem,
    gu_v,
    down_v,
    res_v,
    two_v,
    e_v,
    pre_v,
    hidden_v,
    far_v,
    x_v,
    y_v,
    own_v,
    xa_far,
    xa_own,
    yb_far,
    yb_own,
    ya_pass,
    xb_pass,
):
    rows, width, hidden = plan
    half = width // 2
    wide_tile, out_tile = 256, 512
    p = Post(send_sem, recv_sem)
    low, high = pl.ds(0, half), pl.ds(half, half)
    order = (p.far, p.by_x, p.by_y, p.own)
    targets = (far_v, x_v, y_v, own_v)

    def load(src, dst, index):
        return pltpu.make_async_copy(src, dst, local_sem.at[index])

    def fetch(i):
        return (
            load(two.at[order[i]], two_v.at[i % 2], 2 * (i % 2)),
            load(grads.at[order[i]], e_v.at[i % 2], 2 * (i % 2) + 1),
        )

    def keep_pre(i):
        at = pl.ds(pl.multiple_of(order[i] * rows, rows), rows)
        return load(pre_v, pre_out.at[at], 4)

    def keep_hidden(i):
        at = pl.ds(pl.multiple_of(order[i] * rows, rows), rows)
        return load(hidden_v.at[i], hidden_out.at[at], 5 + i)

    def place(i):
        return load(two_v.at[i % 2], partial_out.at[order[i]], i % 2)

    weights = [load(gate_up, gu_v, 9), load(down, down_v, 10), load(residual, res_v, 11)]
    for cp in list(fetch(0)) + weights:
        cp.start()
    bar = pltpu.get_barrier_semaphore()
    for target in (p.to_x, p.to_y):
        pl.semaphore_signal(bar, inc=1, device_id=target, device_id_type=MESH)
    pl.semaphore_wait(bar, 2)
    for cp in weights:
        cp.wait()

    def chunk(i, start, size):
        at, above = pl.ds(start, size), pl.ds(start + hidden, size)
        gate = dot2(two_v[i % 2], gu_v[:, at], 1, 0)
        up = dot2(two_v[i % 2], gu_v[:, above], 1, 0)
        grad = dot2(e_v[i % 2], down_v[at, :], 1, 1)
        sig = jax.nn.sigmoid(gate)
        silu = gate * sig
        hidden_v[i, :, at] = (silu * up).astype(BF16)
        pre_v[:, at] = (grad * up * sig * (1.0 + gate * (1.0 - sig))).astype(BF16)
        pre_v[:, above] = (grad * silu).astype(BF16)

    whole_tiles = hidden // wide_tile
    sends = []
    for i in range(4):
        for cp in fetch(i):
            cp.wait()
        if i < 3:
            for cp in fetch(i + 1):
                cp.start()

        def step(j, carry, i=i):
            chunk(i, pl.multiple_of(j * wide_tile, wide_tile), wide_tile)
            return carry

        lax.fori_loop(0, whole_tiles, step, 0)
        if hidden % wide_tile:
            chunk(i, whole_tiles * wide_tile, hidden % wide_tile)
        keep_pre(i).start()
        keep_hidden(i).start()

        def back_tile(n, carry, i=i):
            at = pl.ds(pl.multiple_of(n * out_tile, out_tile), out_tile)
            targets[i][:, at] = dot2(pre_v[...], gu_v[at, :], 1, 1).astype(BF16)
            return carry

        lax.fori_loop(0, width // out_tile, back_tile, 0)
        keep_pre(i).wait()
        if i == 0:
            go = [
                p.copy(far_v.at[:, low], xa_far, "xa_far", 0, p.to_x),
                p.copy(far_v.at[:, high], yb_far, "yb_far", 0, p.to_y),
            ]
        elif i == 1:
            go = [p.copy(x_v.at[:, low], xa_own, "xa_own", 0, p.to_x)]
            sends[1].wait_recv()
            x_v[:, high] = (x_v[:, high].astype(F32) + yb_far[...].astype(F32)).astype(BF16)
            go.append(p.copy(x_v.at[:, high], xb_pass, "xb_pass", 0, p.to_x))
        elif i == 2:
            go = [p.copy(y_v.at[:, high], yb_own, "yb_own", 0, p.to_y)]
            sends[0].wait_recv()
            y_v[:, low] = (y_v[:, low].astype(F32) + xa_far[...].astype(F32)).astype(BF16)
            go.append(p.copy(y_v.at[:, low], ya_pass, "ya_pass", 0, p.to_y))
        else:
            go = []
        for cp in go:
            cp.start()
        sends += go

    for i in range(4):
        if i >= 2:
            place(i - 2).wait()

        def out_chunk(n, carry, i=i):
            at = pl.ds(pl.multiple_of(n * out_tile, out_tile), out_tile)
            part = dot2(hidden_v[i], down_v[:, at], 1, 0)
            if i == 3:
                part = part + res_v[:, at]
            two_v[i % 2, :, at] = part.astype(BF16)
            return carry

        lax.fori_loop(0, width // out_tile, out_chunk, 0)
        place(i).start()
    for i in range(4):
        keep_hidden(i).wait()
    for cp in sends[2:]:
        cp.wait_recv()
    own_v[:, low] = (
        own_v[:, low].astype(F32) + xa_own[...].astype(F32) + ya_pass[...].astype(F32)
    ).astype(BF16)
    own_v[:, high] = (
        own_v[:, high].astype(F32) + yb_own[...].astype(F32) + xb_pass[...].astype(F32)
    ).astype(BF16)
    done = load(own_v, sum_out, 4)
    done.start()
    place(2).wait()
    place(3).wait()
    done.wait()
    for cp in sends:
        cp.wait_send()


def middle_call(two, grads, gate_up, down, residual):
    chips, rows, width = two.shape
    hidden = down.shape[0]
    V = pltpu.VMEM
    sd = jax.ShapeDtypeStruct
    anyspec = pl.BlockSpec(memory_space=pl.ANY)
    block = (rows, width)
    part = (rows, width // 2)
    return pl.pallas_call(
        functools.partial(middle_kernel, (rows, width, hidden)),
        out_shape=[
            sd((chips * rows, 2 * hidden), BF16),
            sd((chips * rows, hidden), BF16),
            sd((chips,) + block, BF16),
            sd(block, BF16),
        ],
        in_specs=[anyspec] * 5,
        out_specs=[anyspec] * 4,
        scratch_shapes=[
            pltpu.SemaphoreType.DMA((8, 4)),
            pltpu.SemaphoreType.DMA((8, 4)),
            pltpu.SemaphoreType.DMA((12,)),
            V((width, 2 * hidden), BF16),
            V((hidden, width), BF16),
            V(block, F32),
            V((2,) + block, BF16),
            V((2,) + block, BF16),
            V((rows, 2 * hidden), BF16),
            V((chips, rows, hidden), BF16),
        ]
        + [V(block, BF16)] * 4
        + [V(part, BF16)] * 6,
        compiler_params=pltpu.CompilerParams(
            collective_id=3, has_side_effects=True, vmem_limit_bytes=63 * 1024 * 1024
        ),
        cost_estimate=pl.CostEstimate(
            flops=80_000_000_000, bytes_accessed=60_000_000, transcendentals=10_000_000
        ),
        name="feed_forward",
    )(two, grads, gate_up, down, residual)


def body_plane(
    tokens,
    cotangent,
    segments,
    positions,
    w_query,
    w_key,
    w_value,
    w_out,
    w_gate,
    w_up,
    w_down,
    gain_attn,
    gain_mlp,
):
    micro, tile, width = tokens.shape
    head_dim = w_key.shape[1]
    head_count = width // head_dim
    planes = lax.axis_size("dp")
    chips = lax.axis_size("seq")
    pair = lax.axis_size("fsdp")
    plane = lax.axis_index("dp")
    own = lax.axis_index("seq")
    core = lax.axis_index("fsdp")
    rows = micro * tile
    hidden = w_gate.shape[1]
    shard = w_query.shape[0]
    own_hidden = hidden // chips
    piece = own_hidden // planes
    qkv = width + 2 * head_dim
    score_scale = 1.0 / math.sqrt(head_dim)

    gains = jnp.stack([gain_attn, gain_mlp], axis=1)
    gains = jnp.pad(gains, ((0, 0), (0, head_dim - 2)))
    w_in = jnp.concatenate([w_query, w_key, w_value, gains], axis=1)
    gate_up = jnp.stack([w_gate, w_up], axis=1).reshape(shard, 2, planes, chips, piece)
    gate_up = gate_up.transpose(3, 0, 1, 2, 4).reshape(chips, shard, 2 * own_hidden)
    marks = jnp.pad(jnp.stack([segments, positions], axis=1), ((0, 0), (0, 6), (0, 0)))
    (
        x_rows,
        marks,
        w_qkv,
        out_mat,
        gate_up,
        down_mat,
        grads_in,
        plane_two,
        middle,
        hidden_one,
        queries,
        attended,
        kv,
        kv_home,
        cosine,
        sine,
    ) = front(tokens, cotangent, marks, w_in, w_out, gate_up, w_down)
    gains = jnp.pad(w_qkv[..., qkv : qkv + 2].reshape(width, 2).T, ((0, 6), (0, 0))).astype(F32)
    gate_up = gate_up.reshape(width, 2 * own_hidden)
    down_mat = down_mat.reshape(own_hidden, width)
    plane_grads = grads_in.reshape(chips * rows, width)
    plane_two = plane_two.reshape(chips * rows, width)

    grad_pre, hidden_mlp, partial_out, grad_hidden_two = middle_call(
        plane_two.reshape(chips, rows, width),
        grads_in.reshape(chips, rows, width),
        gate_up,
        down_mat,
        middle,
    )
    layer_rows = scatter_sum(partial_out.reshape(chips, chips, tile, width), "seq", 1)
    layer_rows = layer_rows.reshape(micro, tile, width)
    grad_down = dot32(hidden_mlp, plane_grads, ((0,), (0,))).astype(BF16)
    grad_gate_up = dot32(plane_two, grad_pre, ((0,), (0,))).astype(BF16)
    grad_down = scatter_core(grad_down.reshape(planes, pair, -1, width), core, 1)
    grad_gate_up = scatter_core(
        grad_gate_up.reshape(planes, chips, pair, shard, 2 * own_hidden), core, 2
    )
    layer_rows, grad_down, grad_gate_up = lax.optimization_barrier(
        (layer_rows, grad_down, grad_gate_up)
    )
    grad_down = scatter_sum(grad_down, "dp", 0).reshape(-1, width).astype(F32)
    grad_gate_up = scatter_sum(grad_gate_up, "dp", 0).reshape(chips, shard, 2 * own_hidden)
    grad_gate_up = swap_blocks(grad_gate_up, own).reshape(chips, shard, 2, planes, piece)
    grad_gate_up = grad_gate_up.transpose(2, 1, 3, 0, 4).reshape(2, shard, hidden).astype(F32)

    grad_input, grad_q, grad_kv, grad_out = back(
        tile,
        grad_hidden_two,
        grads_in,
        middle,
        x_rows,
        w_qkv,
        out_mat,
        hidden_one.T,
        queries,
        attended.T,
        kv,
        cosine,
        sine,
        marks,
        gains,
    )
    return (
        layer_rows,
        kv_home[..., :head_dim],
        kv_home[..., head_dim:],
        grad_input.astype(F32),
        grad_q,
        grad_kv[:, :head_dim],
        grad_kv[:, head_dim : 2 * head_dim],
        grad_out,
        grad_gate_up[0],
        grad_gate_up[1],
        grad_down,
        grad_kv[:, 2 * head_dim],
        grad_kv[:, 2 * head_dim + 1],
    )


def body(tokens, *rest):
    if tokens.shape[0] == lax.axis_size("seq") == 4 and lax.axis_size("fsdp") == 2:
        return body_plane(tokens, *rest)
    return body_general(tokens, *rest)


def solution(mesh):
    in_specs = (
        P(None, ("dp", "seq", "fsdp"), None),
        P(None, ("dp", "seq", "fsdp"), None),
        P(None, ("dp", "seq", "fsdp")),
        P(None, ("dp", "seq", "fsdp")),
        P(("dp", "seq", "fsdp"), None),
        P(("dp", "seq", "fsdp"), None),
        P(("dp", "seq", "fsdp"), None),
        P(("dp", "seq", "fsdp"), None),
        P(("dp", "seq", "fsdp"), None),
        P(("dp", "seq", "fsdp"), None),
        P(("dp", "seq", "fsdp"), None),
        P(("dp", "seq", "fsdp")),
        P(("dp", "seq", "fsdp")),
    )
    out_specs = (
        P(None, ("dp", "seq", "fsdp"), None),
        P(None, ("dp", "seq", "fsdp"), None),
        P(None, ("dp", "seq", "fsdp"), None),
        P(None, ("dp", "seq", "fsdp"), None),
        P(("dp", "seq", "fsdp"), None),
        P(("dp", "seq", "fsdp"), None),
        P(("dp", "seq", "fsdp"), None),
        P(("dp", "seq", "fsdp"), None),
        P(("dp", "seq", "fsdp"), None),
        P(("dp", "seq", "fsdp"), None),
        P(("dp", "seq", "fsdp"), None),
        P(("dp", "seq", "fsdp")),
        P(("dp", "seq", "fsdp")),
    )
    return jax.shard_map(body, mesh=mesh, in_specs=in_specs, out_specs=out_specs, check_vma=False)
```

```python
import functools
import math

import jax
import jax.numpy as jnp
from jax import lax
from jax.experimental import pallas as pl
from jax.experimental.pallas import tpu as pltpu
from jax.sharding import PartitionSpec as P

EPSILON = 1e-05
MASKED = -1e30
LINE, PLANE, CORE = "dp", "seq", "fsdp"
EVERY = (LINE, PLANE, CORE)
SCORES, KEYS = "qhd,kd->hqk", "hqk,qhd->kd"
ROWS, COLUMNS = "nf,df->nd", "nd,nf->df"
OUTER, INNER = "nd,ne->de", "ne,de->nd"


def rope_tables(places, half_dim):
    frequency = jnp.exp(-math.log(10000.0) * jnp.arange(half_dim, dtype=jnp.float32) / half_dim)
    angles = places.astype(jnp.float32)[:, None] * frequency[None, :]
    return (jnp.cos(angles), jnp.sin(angles))


def rotate(vector, cosine, sine_part):
    half_dim = vector.shape[-1] // 2
    first_half = vector[..., :half_dim]
    second_half = vector[..., half_dim:]
    return jnp.concatenate(
        [
            first_half * cosine - second_half * sine_part,
            second_half * cosine + first_half * sine_part,
        ],
        axis=-1,
    )


def norm_back(grad_normed, normed, inverse):
    return inverse * (grad_normed - normed * jnp.mean(grad_normed * normed, axis=-1, keepdims=True))


def mask_scores(scores, query_place, query_segment, key_segment):
    key_place = jnp.arange(key_segment.shape[0], dtype=jnp.int32)
    allowed = (query_segment[:, None] == key_segment[None, :]) & (
        query_place[:, None] >= key_place[None, :]
    )
    return jnp.where(allowed[None], scores, MASKED)


def attend_micro(micro_item, query_place, block_rows, score_scale):
    queries, keys_seq, values_seq, query_segment, key_segment = micro_item
    query_rows, local_heads, head_dim = queries.shape
    blocks = query_rows // block_rows

    def one_block(block_item):
        block_query, block_place, block_segment = block_item
        scores = (
            jnp.einsum(SCORES, block_query, keys_seq, preferred_element_type=jnp.float32)
            * score_scale
        )
        scores = mask_scores(scores, block_place, block_segment, key_segment)
        row_max = jnp.max(scores, axis=-1, keepdims=True)
        log_total = row_max + jnp.log(jnp.sum(jnp.exp(scores - row_max), axis=-1, keepdims=True))
        soft_weights = jnp.exp(scores - log_total).astype(jnp.bfloat16)
        attended = jnp.einsum(
            "hqk,kd->qhd", soft_weights, values_seq, preferred_element_type=jnp.float32
        )
        return (attended.astype(jnp.bfloat16), log_total)

    return lax.map(
        one_block,
        (
            queries.reshape(blocks, block_rows, local_heads, head_dim),
            query_place.reshape(blocks, block_rows),
            query_segment.reshape(blocks, block_rows),
        ),
    )


def attend_back(micro_item, query_place, block_rows, score_scale):
    queries, keys_seq, values_seq, grad_attended, log_total, query_segment, key_segment = micro_item
    query_rows, local_heads, head_dim = queries.shape
    blocks = query_rows // block_rows

    def one_block(running, block_item):
        grad_keys, grad_values = running
        block_query, block_grad, block_total, block_place, block_segment = block_item
        scores = (
            jnp.einsum(SCORES, block_query, keys_seq, preferred_element_type=jnp.float32)
            * score_scale
        )
        scores = mask_scores(scores, block_place, block_segment, key_segment)
        soft_weights = jnp.exp(scores - block_total)
        grad_soft = jnp.einsum(
            SCORES, block_grad, values_seq, preferred_element_type=jnp.float32
        )
        inner_sum = jnp.sum(soft_weights * grad_soft, axis=-1, keepdims=True)
        grad_scores = (soft_weights * (grad_soft - inner_sum)).astype(jnp.bfloat16)
        grad_queries = (
            jnp.einsum("hqk,kd->qhd", grad_scores, keys_seq, preferred_element_type=jnp.float32)
            * score_scale
        )
        grad_keys = (
            grad_keys
            + jnp.einsum(
                KEYS, grad_scores, block_query, preferred_element_type=jnp.float32
            )
            * score_scale
        )
        grad_values = grad_values + jnp.einsum(
            KEYS,
            soft_weights.astype(jnp.bfloat16),
            block_grad,
            preferred_element_type=jnp.float32,
        )
        return ((grad_keys, grad_values), grad_queries)

    zero_init = jnp.zeros(keys_seq.shape, jnp.float32)
    running, grad_queries = lax.scan(
        one_block,
        (zero_init, zero_init),
        (
            queries.reshape(blocks, block_rows, local_heads, head_dim),
            grad_attended.reshape(blocks, block_rows, local_heads, head_dim),
            log_total,
            query_place.reshape(blocks, block_rows),
            query_segment.reshape(blocks, block_rows),
        ),
    )
    return (grad_queries, running[0], running[1])


def body_general(
    tokens,
    cotangent,
    segments,
    positions,
    w_query,
    w_key,
    w_value,
    w_out,
    w_gate,
    w_up,
    w_down,
    gain_attn,
    gain_mlp,
):
    micro_count, tok_rows, model_width = tokens.shape
    head_dim = w_key.shape[1]
    head_count = model_width // head_dim
    seq_size = lax.axis_size(PLANE)
    pair_size = lax.axis_size(CORE)
    local_heads = head_count // seq_size
    row_count = micro_count * tok_rows
    query_rows = seq_size * tok_rows
    block_rows = min(512, query_rows)
    score_scale = 1.0 / math.sqrt(head_dim)
    gathered = (
        lax.all_gather(w_query, EVERY, axis=0, tiled=True),
        lax.all_gather(w_key, EVERY, axis=0, tiled=True),
        lax.all_gather(w_value, EVERY, axis=0, tiled=True),
        lax.all_gather(w_out, EVERY, axis=0, tiled=True),
        lax.all_gather(w_gate, EVERY, axis=0, tiled=True),
        lax.all_gather(w_up, EVERY, axis=0, tiled=True),
        lax.all_gather(w_down, EVERY, axis=0, tiled=True),
        lax.all_gather(gain_attn, EVERY, axis=0, tiled=True),
        lax.all_gather(gain_mlp, EVERY, axis=0, tiled=True),
    )
    query_mat, key_mat, value_mat, out_mat, gate_mat, up_mat, down_mat, gain_one, gain_two = (
        gathered
    )
    flat_rows = tokens.reshape(row_count, model_width).astype(jnp.float32)
    inverse_one = lax.rsqrt(jnp.mean(flat_rows * flat_rows, axis=-1, keepdims=True) + EPSILON)
    normed_one = flat_rows * inverse_one
    hidden_one = (normed_one * gain_one.astype(jnp.float32)).astype(jnp.bfloat16)
    cosine, sine_part = rope_tables(positions.reshape(row_count), head_dim // 2)
    query_lin = jnp.dot(hidden_one, query_mat, preferred_element_type=jnp.float32).reshape(
        row_count, head_count, head_dim
    )
    queries = rotate(query_lin, cosine[:, None, :], sine_part[:, None, :]).astype(jnp.bfloat16)
    keys_local = rotate(
        jnp.dot(hidden_one, key_mat, preferred_element_type=jnp.float32), cosine, sine_part
    ).astype(jnp.bfloat16)
    values_local = jnp.dot(hidden_one, value_mat, preferred_element_type=jnp.float32).astype(
        jnp.bfloat16
    )
    keys_local = keys_local.reshape(micro_count, tok_rows, head_dim)
    values_local = values_local.reshape(micro_count, tok_rows, head_dim)
    keys_seq, values_seq, segment_seq = (
        lax.all_gather(keys_local, (PLANE, CORE), axis=1, tiled=True),
        lax.all_gather(values_local, (PLANE, CORE), axis=1, tiled=True),
        lax.all_gather(segments.astype(jnp.bfloat16), (PLANE, CORE), axis=1, tiled=True),
    )
    key_segment = segment_seq.astype(jnp.int32)
    pair_index = lax.axis_index(CORE)
    query_place = (
        (jnp.arange(seq_size, dtype=jnp.int32)[:, None] * pair_size + pair_index) * tok_rows
        + jnp.arange(tok_rows, dtype=jnp.int32)[None, :]
    ).reshape(query_rows)
    query_segment = lax.dynamic_index_in_dim(
        key_segment.reshape(micro_count, seq_size, pair_size, tok_rows),
        pair_index,
        axis=2,
        keepdims=False,
    ).reshape(micro_count, query_rows)
    head_queries = lax.all_to_all(
        queries.reshape(micro_count, tok_rows, model_width),
        PLANE,
        split_axis=2,
        concat_axis=1,
        tiled=True,
    )
    head_queries = head_queries.reshape(micro_count, query_rows, local_heads, head_dim)

    def forward_micro(micro_item):
        return attend_micro(micro_item, query_place, block_rows, score_scale)

    attended, log_total = lax.map(
        forward_micro, (head_queries, keys_seq, values_seq, query_segment, key_segment)
    )
    mixed_rows = lax.all_to_all(
        attended.reshape(micro_count, query_rows, local_heads * head_dim),
        PLANE,
        split_axis=1,
        concat_axis=2,
        tiled=True,
    )
    mixed_rows = mixed_rows.reshape(row_count, model_width)
    middle = flat_rows + jnp.dot(mixed_rows, out_mat, preferred_element_type=jnp.float32)
    inverse_two = lax.rsqrt(jnp.mean(middle * middle, axis=-1, keepdims=True) + EPSILON)
    normed_two = middle * inverse_two
    hidden_two = (normed_two * gain_two.astype(jnp.float32)).astype(jnp.bfloat16)
    gate_proj = jnp.dot(hidden_two, gate_mat, preferred_element_type=jnp.float32)
    up_proj = jnp.dot(hidden_two, up_mat, preferred_element_type=jnp.float32)
    gate_sigmoid = jax.nn.sigmoid(gate_proj)
    gate_silu = gate_proj * gate_sigmoid
    hidden_mlp = (gate_silu * up_proj).astype(jnp.bfloat16)
    result = middle + jnp.dot(hidden_mlp, down_mat, preferred_element_type=jnp.float32)
    back_weights = (
        lax.all_gather(w_query, EVERY, axis=0, tiled=True),
        lax.all_gather(w_key, EVERY, axis=0, tiled=True),
        lax.all_gather(w_value, EVERY, axis=0, tiled=True),
        lax.all_gather(w_out, EVERY, axis=0, tiled=True),
        lax.all_gather(w_gate, EVERY, axis=0, tiled=True),
        lax.all_gather(w_up, EVERY, axis=0, tiled=True),
        lax.all_gather(w_down, EVERY, axis=0, tiled=True),
        lax.all_gather(gain_attn, EVERY, axis=0, tiled=True),
        lax.all_gather(gain_mlp, EVERY, axis=0, tiled=True),
    )
    query_mat, key_mat, value_mat, out_mat, gate_mat, up_mat, down_mat, gain_one, gain_two = (
        back_weights
    )
    grad_rows = cotangent.reshape(row_count, model_width).astype(jnp.float32)
    grad_branch = cotangent.reshape(row_count, model_width)
    grad_down_w = jnp.einsum(
        "nf,nd->fd", hidden_mlp, grad_branch, preferred_element_type=jnp.float32
    )
    grad_hidden = jnp.einsum("nd,fd->nf", grad_branch, down_mat, preferred_element_type=jnp.float32)
    grad_gate_pre = (
        grad_hidden * up_proj * gate_sigmoid * (1.0 + gate_proj * (1.0 - gate_sigmoid))
    ).astype(jnp.bfloat16)
    grad_up_pre = (grad_hidden * gate_silu).astype(jnp.bfloat16)
    grad_gate_w = jnp.einsum(
        COLUMNS, hidden_two, grad_gate_pre, preferred_element_type=jnp.float32
    )
    grad_up_w = jnp.einsum(COLUMNS, hidden_two, grad_up_pre, preferred_element_type=jnp.float32)
    grad_hidden_two = jnp.einsum(
        ROWS, grad_gate_pre, gate_mat, preferred_element_type=jnp.float32
    ) + jnp.einsum(ROWS, grad_up_pre, up_mat, preferred_element_type=jnp.float32)
    grad_gain_two = jnp.sum(grad_hidden_two * normed_two, axis=0)
    grad_middle = grad_rows + norm_back(
        grad_hidden_two * gain_two.astype(jnp.float32), normed_two, inverse_two
    )
    grad_proj = grad_middle.astype(jnp.bfloat16)
    grad_out_w = jnp.einsum(OUTER, mixed_rows, grad_proj, preferred_element_type=jnp.float32)
    grad_mixed = jnp.einsum(
        INNER, grad_proj, out_mat, preferred_element_type=jnp.float32
    ).astype(jnp.bfloat16)
    grad_heads = lax.all_to_all(
        grad_mixed.reshape(micro_count, tok_rows, model_width),
        PLANE,
        split_axis=2,
        concat_axis=1,
        tiled=True,
    )
    grad_heads = grad_heads.reshape(micro_count, query_rows, local_heads, head_dim)

    def backward_micro(micro_item):
        return attend_back(micro_item, query_place, block_rows, score_scale)

    grad_head_queries, grad_keys_seq, grad_values_seq = lax.map(
        backward_micro,
        (head_queries, keys_seq, values_seq, grad_heads, log_total, query_segment, key_segment),
    )
    grad_query_rows = lax.all_to_all(
        grad_head_queries.reshape(micro_count, query_rows, local_heads * head_dim).astype(
            jnp.bfloat16
        ),
        PLANE,
        split_axis=1,
        concat_axis=2,
        tiled=True,
    ).astype(jnp.float32)
    grad_keys_own, grad_values_own = (
        lax.psum_scatter(
            grad_keys_seq.astype(jnp.bfloat16), (PLANE, CORE), scatter_dimension=1, tiled=True
        ).astype(jnp.float32),
        lax.psum_scatter(
            grad_values_seq.astype(jnp.bfloat16), (PLANE, CORE), scatter_dimension=1, tiled=True
        ).astype(jnp.float32),
    )
    grad_query_lin = (
        rotate(
            grad_query_rows.reshape(row_count, head_count, head_dim),
            cosine[:, None, :],
            -sine_part[:, None, :],
        )
        .reshape(row_count, model_width)
        .astype(jnp.bfloat16)
    )
    grad_key_lin = rotate(grad_keys_own.reshape(row_count, head_dim), cosine, -sine_part).astype(
        jnp.bfloat16
    )
    grad_value_lin = grad_values_own.reshape(row_count, head_dim).astype(jnp.bfloat16)
    grad_query_w = jnp.einsum(
        OUTER, hidden_one, grad_query_lin, preferred_element_type=jnp.float32
    )
    grad_key_w = jnp.einsum(
        OUTER, hidden_one, grad_key_lin, preferred_element_type=jnp.float32
    )
    grad_value_w = jnp.einsum(
        OUTER, hidden_one, grad_value_lin, preferred_element_type=jnp.float32
    )
    grad_hidden_one = jnp.einsum(
        INNER, grad_query_lin, query_mat, preferred_element_type=jnp.float32
    )
    grad_hidden_one = grad_hidden_one + jnp.einsum(
        INNER, grad_key_lin, key_mat, preferred_element_type=jnp.float32
    )
    grad_hidden_one = grad_hidden_one + jnp.einsum(
        INNER, grad_value_lin, value_mat, preferred_element_type=jnp.float32
    )
    grad_gain_one = jnp.sum(grad_hidden_one * normed_one, axis=0)
    grad_input = grad_middle + norm_back(
        grad_hidden_one * gain_one.astype(jnp.float32), normed_one, inverse_one
    )
    matrix_grads = (
        grad_query_w,
        grad_key_w,
        grad_value_w,
        grad_out_w,
        grad_gate_w,
        grad_up_w,
        grad_down_w,
    )
    shards = tuple(
        lax.psum_scatter(
            grad.astype(jnp.bfloat16), EVERY, scatter_dimension=0, tiled=True
        ).astype(jnp.float32)
        for grad in matrix_grads
    ) + (
        lax.psum_scatter(grad_gain_one, EVERY, scatter_dimension=0, tiled=True),
        lax.psum_scatter(grad_gain_two, EVERY, scatter_dimension=0, tiled=True),
    )
    layer_rows = result.reshape(micro_count, tok_rows, model_width).astype(jnp.bfloat16)
    return (
        layer_rows,
        keys_local,
        values_local,
        grad_input.reshape(micro_count, tok_rows, model_width),
        shards[0],
        shards[1],
        shards[2],
        shards[3],
        shards[4],
        shards[5],
        shards[6],
        shards[7],
        shards[8],
    )


BF16 = jnp.bfloat16
F32 = jnp.float32
MESH = pl.DeviceIdType.MESH
GROUPS = 64


def dot32(left, right, contract):
    return lax.dot_general(left, right, ((contract[0], contract[1]), ((), ())), preferred_element_type=F32)


def turn(vector, cosine, sine):
    return vector * cosine + pltpu.roll(vector, vector.shape[-1] // 2, 1) * sine


def scatter_sum(value, axes, dim):
    return lax.psum_scatter(value, axes, scatter_dimension=dim, tiled=True)


def send_plane(value, step):
    return lax.ppermute(value, PLANE, [(i, i ^ step) for i in range(4)])


def send_core(value):
    return lax.ppermute(value, CORE, [(0, 1), (1, 0)])


def block_of(value, index, dim=0):
    return lax.dynamic_index_in_dim(value, index, axis=dim, keepdims=False)


def put_block(value, block, index, dim=0):
    return lax.dynamic_update_index_in_dim(value, block, index, axis=dim)


def swap_blocks(value, own):
    out = value
    for step in (1, 2, 3):
        other = own ^ step
        out = put_block(out, send_plane(block_of(value, other), step), other)
    return out


def scatter_core(value, core, dim):
    other = send_core(block_of(value, 1 - core, dim))
    return (block_of(value, core, dim).astype(F32) + other.astype(F32)).astype(BF16)


class Post:
    def __init__(self, send_sem, recv_sem):
        self.plane=lax.axis_index(LINE); self.own=lax.axis_index(PLANE); self.core=lax.axis_index(CORE)
        self.planes=lax.axis_size(LINE)
        x=lax.rem(self.own,2); y=lax.div(self.own,2)
        self.by_x=self.own+1-2*x; self.by_y=self.own+2-4*y; self.far=3-self.own
        z,s,c=self.plane,self.own,self.core
        self.to_x=(z,self.by_x,c); self.to_y=(z,self.by_y,c); self.to_far=(z,self.far,c)
        self.to_core=(z,s,1-c)
        self.to_up=(lax.rem(z+1,self.planes),s,c); self.to_down=(lax.rem(z+self.planes-1,self.planes),s,c)
        self.has_up=z<self.planes-1; self.has_down=z>0
        self.send_sem, self.recv_sem = send_sem, recv_sem
        self.sent=[]
        self.steps={0:[(z,())]}
        for k in range(1,self.planes):
            self.steps[k]=[(jnp.clip(z-k,0,self.planes-1),(z-k>=0,)),(jnp.clip(z+k,0,self.planes-1),(z+k<=self.planes-1,))]
        self.groups={}
    def group(self, name):
        return self.groups.setdefault(name, len(self.groups))
    def barrier(self):
        bar=pltpu.get_barrier_semaphore()
        for t in (self.to_x,self.to_y,self.to_far,self.to_core):
            pl.semaphore_signal(bar,inc=1,device_id=t,device_id_type=MESH)
        for chip in (self.by_x,self.by_y,self.far):
            pl.semaphore_signal(bar,inc=1,device_id=(self.plane,chip,1-self.core),device_id_type=MESH)
        @pl.when(self.has_up)
        def _(): pl.semaphore_signal(bar,inc=1,device_id=self.to_up,device_id_type=MESH)
        @pl.when(self.has_down)
        def _(): pl.semaphore_signal(bar,inc=1,device_id=self.to_down,device_id_type=MESH)
        pl.semaphore_wait(bar,7+self.has_up.astype(jnp.int32)+self.has_down.astype(jnp.int32))
    def copy(self, src, dst, name, index, target, arrive=None):
        return pltpu.make_async_remote_copy(src_ref=src,dst_ref=dst,
            send_sem=self.send_sem.at[self.group(name),index],
            recv_sem=self.recv_sem.at[self.group(arrive or name),index],
            device_id=target,device_id_type=MESH)
    def send(self, src, dst, name, index, target, arrive=None, when=()):
        def go(): self.copy(src,dst,name,index,target,arrive).start()
        if when:
            cond=functools.reduce(jnp.logical_and,when)
            pl.when(cond)(go)
        else: go()
        self.sent.append((when,lambda: self.copy(src,dst,name,index,target,arrive).wait_send()))
    def wait(self, ref, name, index):
        self.copy(ref,ref,name,index,self.to_core).wait_recv()
    def finish(self):
        for when,w in self.sent:
            if when: pl.when(functools.reduce(jnp.logical_and,when))(w)
            else: w()

class Line:
    def __init__(self, post, name, unit, own_source):
        self.p, self.name, self.unit, self.src = post, name, unit, own_source
    def start(self):
        p=self.p
        p.send(self.src,self.unit(p.plane),self.name+"_up",p.plane,p.to_up,self.name,(p.has_up,))
        p.send(self.src,self.unit(p.plane),self.name+"_down",p.plane,p.to_down,self.name,(p.has_down,))
    def hop(self, k, then=None):
        p=self.p
        for sign,(at,(here,)) in zip((-1,1),p.steps[k]):
            on=p.has_up if sign<0 else p.has_down
            target=p.to_up if sign<0 else p.to_down
            ref=self.unit(at)
            @pl.when(here)
            def _(ref=ref,at=at): p.wait(ref,self.name,at)
            if k<p.planes-1:
                p.send(ref,ref,self.name+("_up" if sign<0 else "_down"),at,target,self.name,(here,on))
            if then: then(at,here)

class Spread:
    def __init__(self, post, name, unit, low, high):
        self.p,self.name,self.unit,self.low,self.high=post,name,unit,low,high
    def start(self, index, source, when=()):
        p=self.p
        dst=self.unit(index,p.own)
        p.send(source,dst,self.name+"_x",index,p.to_x,None,when)
        p.send(source,dst,self.name+"_y",index,p.to_y,None,when)
    def relay(self, index, when=()):
        p=self.p
        def go(f):
            if when: pl.when(functools.reduce(jnp.logical_and,when))(f)
            else: f()
        go(lambda: p.wait(self.unit(index,p.by_x),self.name+"_x",index))
        ref=self.low(index,p.by_x)
        p.send(ref,ref,self.name+"_l",index,p.to_y,None,when)
        go(lambda: p.wait(self.unit(index,p.by_y),self.name+"_y",index))
        ref=self.high(index,p.by_y)
        p.send(ref,ref,self.name+"_h",index,p.to_x,None,when)
    def arrive(self, index, when=()):
        p=self.p
        def go():
            p.wait(self.low(index,p.far),self.name+"_l",index)
            p.wait(self.high(index,p.far),self.name+"_h",index)
        if when: pl.when(functools.reduce(jnp.logical_and,when))(go)
        else: go()


def dot2(l, r, ca, cb):
    return dot32(l, r, ((ca,), (cb,)))


def front_kernel(plan,tok,cot,marks,wq_in,wo_in,gu_in,freq,
    x_out,marks_out,wq_out,wo_out,gu,E,two,middle_out,h1_out,q_out,att_out,kv_out,home,cos_out,sin_out,
    send_sem,recv_sem,local_sem,b_cot,b_gu,
    x_v,marks_v,wq_v,wo_v,h1_v,lin_v,q_v,att_v,kv_v,mid_v,two_v,cos_v,sin_v,gain_v,h1t_v,att_t_v):
    tile,width,head_dim,group=plan
    scale=head_dim**-0.5
    p=Post(send_sem,recv_sem)
    z,s,c=p.plane,p.own,p.core
    chips=4
    rows=chips*tile
    groups=width//group; heads=group//head_dim
    qkv=width+2*head_dim
    count=[0]
    outs_=[]
    def local(src,dst):
        cp=pltpu.make_async_copy(src,dst,local_sem.at[count[0]]); count[0]+=1
        cp.start(); return cp
    def out(src,dst):
        outs_.append(local(src,dst))
    loads=[local(tok.at[s],x_v.at[s]),local(marks.at[s],marks_v.at[c,s]),local(wq_in,wq_v.at[z,s,c]),local(wo_in,wo_v.at[z,s,c])]
    late=[local(cot,b_cot),local(gu_in.at[s],b_gu)]
    p.barrier()
    def attention_weight(name, arr, src):
        n=arr.shape[3]//2
        spread=Spread(p,name,lambda a,b: arr.at[a,b,c],lambda a,b: arr.at[a,b,c,pl.ds(0,n)],lambda a,b: arr.at[a,b,c,pl.ds(n,n)])
        line=Line(p,name+"_z",lambda a: arr.at[a,s,c],src)
        return spread,line
    q_spread,q_line=attention_weight("wq",wq_v,wq_in)
    o_spread,o_line=attention_weight("wo",wo_v,wo_in)
    def each(k, f):
        for at,when in p.steps[k]: f(at,when)
    def to_sibling(name, arr, a, when):
        ref=arr.at[a,:,c]
        p.send(ref,ref,name+"_c",a,p.to_core,None,when)
    others=((p.to_x,p.by_x),(p.to_y,p.by_y),(p.to_far,p.far))
    def swap(src,dst_of,name):
        for i,(t,o) in enumerate(others):
            p.send(src.at[o],dst_of(s),name,i,t)
    def swapped(dst_of,name):
        for i,(t,o) in enumerate(others):
            p.wait(dst_of(o),name,i)
    swap(gu_in,lambda b: gu.at[z,b,c],"gu")
    q_line.start()
    q_spread.start(z,wq_in)
    swap(tok,lambda b: x_v.at[b],"tok")
    for i,(t,o) in enumerate(others):
        p.send(marks.at[o],marks_v.at[c,s],"mk",i,t)
        p.send(marks.at[o],marks_v.at[c,s],"mk2",i,(z,o,1-c))
    p.send(marks.at[s],marks_v.at[c,s],"mk2",3,p.to_core)
    fwd=lambda a,here: q_spread.start(a,wq_v.at[a,s,c],(here,))
    gufwd=lambda a,here: to_sibling("gu",gu,a,(here,))
    ofwd=lambda a,here: o_spread.start(a,wo_v.at[a,s,c],(here,))
    gu_line=Line(p,"gu_z",lambda a: gu.at[a,:,c],gu.at[z,:,c])
    for cp in loads+late: cp.wait()
    out(b_cot,E.at[:,s]); out(b_gu,gu.at[z,s,c]); own_gu=outs_[-1]
    q_line.hop(1,fwd)
    q_line.hop(2,fwd)
    q_line.hop(3,fwd)
    swapped(lambda b: gu.at[z,b,c],"gu")
    own_gu.wait(); outs_[:]=[o for o in outs_ if o is not own_gu]
    gu_line.start(); to_sibling("gu",gu,z,())
    for k in range(4): each(k,lambda a,w: q_spread.relay(a,w))
    gu_line.hop(1,gufwd)
    o_line.start(); o_spread.start(z,wo_in)
    def each_q(a,w):
        q_spread.arrive(a,w); to_sibling("wq",wq_v,a,w)
    for k in range(4): each(k,each_q)
    swapped(lambda b: x_v.at[b],"tok")
    for i,(t,o) in enumerate(others):
        p.wait(marks_v.at[c,o],"mk",i); p.wait(marks_v.at[1-c,o],"mk2",i)
    p.wait(marks_v.at[1-c,s],"mk2",3)
    for a in range(4): p.wait(wq_v.at[a,:,1-c],"wq_c",a)
    out(x_v,x_out); out(marks_v,marks_out); out(wq_v,wq_out)
    e_parts=[]
    for i in range(2):
        def sub(lo,n,i=i): return lambda _,b: E.at[pl.ds(2*i+lo,n),b]
        e_parts.append(Spread(p,"E%d"%i,sub(0,2),sub(0,1),sub(1,1)))
    def e_start(i):
        for t,nm in ((p.to_x,"_x"),(p.to_y,"_y")):
            p.send(cot.at[pl.ds(2*i,2)],E.at[pl.ds(2*i,2),s],"E%d"%i+nm,0,t)
    for i in range(width//head_dim):
        a,b=divmod(i,4)
        block=wq_v[a,b,:,:,pl.ds(qkv,head_dim)].reshape(head_dim,head_dim).astype(F32)
        gain_v[:,pl.ds(i*head_dim,head_dim)]=jnp.transpose(block)[0:8]
    e_start(0); e_start(1)
    def norm_block(b,carry):
        x=x_v[b].astype(F32)
        inv=lax.rsqrt(jnp.mean(x*x,axis=-1,keepdims=True)+EPSILON)
        h1_v[pl.ds(b*tile,tile),:]=(x*inv*gain_v[0:1,:]).astype(BF16)
        return carry
    lax.fori_loop(0,chips,norm_block,0)
    lane=lax.broadcasted_iota(jnp.int32,(1,head_dim),1)
    sign=jnp.where(lane<head_dim//2,-1.0,1.0).astype(F32)
    seg_cols=[]
    for b in range(chips):
        m=jnp.transpose(marks_v[c,b].astype(F32))
        angle=m[:,1:2]*freq[...]
        cos_v[pl.ds(b*tile,tile),:]=jnp.cos(angle); sin_v[pl.ds(b*tile,tile),:]=jnp.sin(angle)*sign
        seg_cols.append(m[:,0:1])
    key_seg=jnp.concatenate([marks_v[k%2,k//2,0:1,:] for k in range(2*chips)],axis=1).astype(F32)
    o_line.hop(1,ofwd)
    w=wq_v[:,:,:,:,pl.ds(width,2*head_dim)].reshape(width,2*head_dim)
    kv=dot2(h1_v[...],w,1,0)
    kv=jnp.concatenate([turn(kv[:,:head_dim],cos_v[...],sin_v[...]),kv[:,head_dim:]],axis=1).astype(BF16)
    kv_v[:,pl.ds(c,1)]=kv.reshape(chips,1,tile,2*head_dim)
    p.send(kv_v.at[:,c],kv_v.at[:,c],"kv",0,p.to_core)
    swap(kv_v.at[:,c],lambda b: home.at[b],"home")
    out(kv_v.at[s,c],home.at[s]); out(cos_v,cos_out); out(sin_v,sin_out)
    steps={0:[lambda: o_line.hop(2,ofwd)],
           1:[lambda: p.wait(kv_v.at[:,1-c],"kv",0), lambda: o_line.hop(3,ofwd)],
           2:[lambda: each(0,lambda a,w: o_spread.relay(a,w)), lambda: each(1,lambda a,w: o_spread.relay(a,w))],
           3:[lambda: each(2,lambda a,w: o_spread.relay(a,w)), lambda: each(3,lambda a,w: o_spread.relay(a,w))],
           4:[]}
    def lin_group(g,carry):
        w=wq_v[:,:,:,:,pl.ds(pl.multiple_of(g*group,group),group)].reshape(width,group)
        lin_v[...]=dot2(h1_v[...],w,1,0)
        for b in range(chips):
            cos,sin=cos_v[pl.ds(b*tile,tile),:],sin_v[pl.ds(b*tile,tile),:]
            for h in range(heads):
                part=lin_v[pl.ds(b*tile,tile),pl.ds(h*head_dim,head_dim)]
                q_v[pl.ds(b*tile,tile),pl.ds(pl.multiple_of(g*group+h*head_dim,head_dim),head_dim)]=turn(part,cos,sin).astype(BF16)
        return carry
    for f in steps[0]: f()
    lax.fori_loop(0,groups,lin_group,0)
    for f in steps[1]: f()
    gu_line.hop(2,gufwd)
    out(kv_v,kv_out); out(q_v,q_out)
    def attend_group(g,carry):
        for b in range(chips):
            extent=(b+1)*2*tile
            at=lambda h: pl.ds(pl.multiple_of(g*group+h*head_dim,head_dim),head_dim)
            q=jnp.concatenate([q_v[pl.ds(b*tile,tile),at(h)] for h in range(heads)],axis=0)
            kvs=kv_v[pl.ds(0,b+1)].reshape(extent,2*head_dim)
            place=(2*b+c)*tile+lax.broadcasted_iota(jnp.int32,(tile,extent),0)
            seen=lax.broadcasted_iota(jnp.int32,(tile,extent),1)
            allowed=(place>=seen)&(seg_cols[b]==key_seg[:,:extent])
            bias=jnp.where(allowed,0.0,MASKED).astype(F32)
            sc=dot2(q,kvs[:,:head_dim],1,1)*scale
            sc=(sc.reshape(heads,tile,extent)+bias[None]).reshape(heads*tile,extent)
            top=jnp.max(sc,axis=-1,keepdims=True)
            e=jnp.exp(sc-top)
            soft=(e*(1.0/jnp.sum(e,axis=-1,keepdims=True))).astype(BF16)
            mixed=dot2(soft,kvs[:,head_dim:],1,0).astype(BF16)
            for h in range(heads):
                att_v[pl.ds(b*tile,tile),at(h)]=mixed[h*tile:(h+1)*tile]
        for i in (2,3):
            @pl.when(g==i-1)
            def _(i=i):
                for f in steps[i]: f()
        return carry
    lax.fori_loop(0,groups,attend_group,0)
    def each_o(a,w):
        o_spread.arrive(a,w); to_sibling("wo",wo_v,a,w)
    for k in range(4): each(k,each_o)
    for f in steps[4]: f()
    for a in range(4): p.wait(wo_v.at[a,:,1-c],"wo_c",a)
    out(wo_v,wo_out)
    def project(g,carry):
        at=pl.ds(pl.multiple_of(g*group,group),group)
        w=wo_v[:,:,:,:,at].reshape(width,group)
        lin_v[...]=dot2(att_v[...],w,1,0)
        for b in range(chips):
            mid_v[pl.ds(b*tile,tile),at]=x_v[b,:,at].astype(F32)+lin_v[pl.ds(b*tile,tile),:]
        return carry
    e_parts[0].relay(0)
    e_parts[1].relay(0)
    lax.fori_loop(0,groups,project,0)
    out(mid_v,middle_out)
    def norm_two(b,carry):
        at=pl.ds(pl.multiple_of(b*tile,tile),tile)
        m=mid_v[at,:]
        inv=lax.rsqrt(jnp.mean(m*m,axis=-1,keepdims=True)+EPSILON)
        two_v[at,:]=(m*inv*gain_v[1:2,:]).astype(BF16)
        return carry
    lax.fori_loop(0,chips,norm_two,0)
    out(two_v,two)
    for i in range(width//head_dim):
        at=slice(i*head_dim,(i+1)*head_dim)
        h1t_v[at,:]=jnp.transpose(h1_v[:,at])
        att_t_v[at,:]=jnp.transpose(att_v[:,at])
    out(h1t_v,h1_out); out(att_t_v,att_out)
    gu_line.hop(3,gufwd)
    e_parts[0].arrive(0)
    e_parts[1].arrive(0)
    for a in range(4): p.wait(gu.at[a,:,1-c],"gu_c",a)
    swapped(lambda b: home.at[b],"home")
    for cp in outs_: cp.wait()
    p.finish()
    assert len(p.groups)<=GROUPS, len(p.groups)

def front(tok,cot,marks,wq_in,wo_in,gu_in):
    Z,S,C=lax.axis_size(LINE),lax.axis_size(PLANE),lax.axis_size(CORE)
    sd=jax.ShapeDtypeStruct
    micro,tile,width=tok.shape
    rows=micro*tile
    head_dim=128
    group=512
    half=head_dim//2
    freq=jnp.exp(-jnp.log(jnp.float32(10000.0))*jnp.arange(half,dtype=F32)/half)
    freq=jnp.concatenate([freq,freq])[None]
    outs=[sd((S,tile,width),BF16),sd((C,)+marks.shape,jnp.int32),sd((Z,S,C)+wq_in.shape,BF16),sd((Z,S,C)+wo_in.shape,BF16),
          sd((Z,S,C)+gu_in.shape[1:],BF16),sd((S,)+cot.shape,BF16),
          sd((rows,width),BF16),sd((rows,width),F32),sd((width,rows),BF16),sd((rows,width),BF16),sd((width,rows),BF16),
          sd((S,C,tile,2*head_dim),BF16),sd((S,tile,2*head_dim),BF16),sd((rows,head_dim),F32),sd((rows,head_dim),F32)]
    anyspec=pl.BlockSpec(memory_space=pl.ANY)
    V=pltpu.VMEM
    return pl.pallas_call(functools.partial(front_kernel,(tile,width,head_dim,group)),out_shape=outs,
        in_specs=[anyspec]*6+[pl.BlockSpec(memory_space=V)],out_specs=[anyspec]*len(outs),
        scratch_shapes=[pltpu.SemaphoreType.DMA((GROUPS,4)),pltpu.SemaphoreType.DMA((GROUPS,4)),pltpu.SemaphoreType.DMA((32,)),
          V(cot.shape,BF16),V(gu_in.shape[1:],BF16),
          V((S,tile,width),BF16),V((C,)+marks.shape,jnp.int32),V((Z,S,C)+wq_in.shape,BF16),V((Z,S,C)+wo_in.shape,BF16),
          V((rows,width),BF16),V((rows,group),F32),V((rows,width),BF16),V((rows,width),BF16),V((S,C,tile,2*head_dim),BF16),
          V((rows,width),F32),V((rows,width),BF16),V((rows,head_dim),F32),V((rows,head_dim),F32),V((8,width),F32),V((width,rows),BF16),V((width,rows),BF16)],
        compiler_params=pltpu.CompilerParams(collective_id=1,has_side_effects=True,vmem_limit_bytes=60*1024*1024),cost_estimate=pl.CostEstimate(flops=20_000_000_000,bytes_accessed=100_000_000,transcendentals=10_000_000),name="front")(tok,cot,marks,wq_in,wo_in,gu_in,freq)


def back_kernel(
    plan,
    gh2,
    grads_in,
    middle,
    x_in,
    wq,
    wo,
    h1t_in,
    q_in,
    att_t_in,
    kv_in,
    cos_in,
    sin_in,
    marks_in,
    gain_v,
    home,
    gq_out,
    gkv_out,
    go_out,
    send_sem,
    recv_sem,
    local_sem,
    mid_v,
    gh1_v,
    x_v,
    proj_v,
    h1t_v,
    q_v,
    att_t_v,
    kv_v,
    cos_v,
    sin_v,
    marks_v,
    wo_b,
    wq_b,
    wk_v,
    mix_v,
    lin_v,
    kvacc,
    kvx,
    gains_acc,
    sq,
    so,
    rq,
    ro,
    tq,
    to,
    pq,
    po,
    uq,
    uo,
    zq,
    zo,
    skv,
    rkv,
    tkv,
    pkv,
    ukv,
    zkv,
    gl_v,
):
    tile, width, head_dim, group = plan
    scale = head_dim**-0.5
    chips, planes = 4, 4
    rows = chips * tile
    groups = width // group
    heads = group // head_dim
    shard = sq.shape[3]
    p = Post(send_sem, recv_sem)
    z, s, c = p.plane, p.own, p.core
    others = ((p.to_x, p.by_x), (p.to_y, p.by_y), (p.to_far, p.far))
    lines = [lax.rem(z + k, planes) for k in range(1, planes)]
    bar = pltpu.get_barrier_semaphore()

    def load(src, dst, index):
        return pltpu.make_async_copy(src, dst, local_sem.at[index])

    first = [
        load(gh2, q_v, 0),
        load(middle, mid_v, 1),
        load(grads_in.at[s], x_v, 2),
    ]
    second = [
        load(h1t_in, h1t_v, 3),
        load(att_t_in, att_t_v, 5),
        load(kv_in, kv_v, 6),
        load(cos_in, cos_v, 7),
        load(sin_in, sin_v, 8),
        load(marks_in, marks_v, 9),
        load(wq.at[:, :, :, :, pl.ds(width, 2 * head_dim)], wk_v, 10),
    ]
    tokens_again = load(x_in, x_v, 11)

    def fetch(g):
        at = pl.ds(pl.multiple_of(g * group, group), group)
        slot = lax.rem(g, 2)
        return (
            load(wo.at[g], wo_b.at[slot], 12 + slot),
            load(wq.at[:, :, :, :, at], wq_b.at[slot], 14 + slot),
        )

    for cp in first + second:
        cp.start()
    for cp in fetch(0):
        cp.start()
    for target in [t for t, _ in others] + [p.to_core] + [(a, s, c) for a in lines]:
        pl.semaphore_signal(bar, inc=1, device_id=target, device_id_type=MESH)
    pl.semaphore_wait(bar, 7)

    def stage_a(g):
        slot = lax.rem(g, 2)
        return (
            p.copy(sq.at[:, :, 1 - c], rq.at[slot], "aq", g, p.to_core),
            p.copy(so.at[:, 1 - c], ro.at[slot], "ao", g, p.to_core),
        )

    def stage_b(g):
        slot = lax.rem(g, 2)
        copies = []
        for i, (target, other) in enumerate(others):
            copies.append(p.copy(tq.at[slot, :, other], pq.at[g, i], "bq%d" % i, g, target))
            copies.append(p.copy(to.at[slot, other], po.at[g, i], "bo%d" % i, g, target))
        return copies

    def stage_c(g):
        slot = lax.rem(g, 2)
        return [
            p.copy(uq.at[slot, a], zq.at[g, k], "cq%d" % k, g, (a, s, c))
            for k, a in enumerate(lines)
        ]

    def stage_c_out(g, k):
        return p.copy(uo.at[lax.rem(g, 2)], zo.at[k], "co", k, (g, s, c))

    def wide(value):
        return value.astype(F32)

    def do_b(g):
        slot = lax.rem(g, 2)
        for cp in stage_a(g):
            cp.wait_recv()

        @pl.when(g >= 2)
        def _():
            for cp in stage_b(g - 2):
                cp.wait_send()

        def one(a, carry):
            tq[slot, a] = (wide(sq[a, :, c]) + wide(rq[slot, a])).astype(BF16)
            to[slot, a] = (wide(so[a, c]) + wide(ro[slot, a])).astype(BF16)
            return carry

        lax.fori_loop(0, planes, one, 0)
        for cp in stage_b(g):
            cp.start()

    def do_c(g):
        slot = lax.rem(g, 2)
        for cp in stage_b(g):
            cp.wait_recv()
        total = wide(tq[slot, :, s])
        mixed = wide(to[slot, s])
        for i in range(3):
            total = total + wide(pq[g, i])
            mixed = mixed + wide(po[g, i])
        uq[slot] = total.astype(BF16)
        uo[slot] = mixed.astype(BF16)
        for cp in stage_c(g):
            cp.start()
        for k in range(1, planes):

            @pl.when(lax.rem(g + planes - z, planes) == k)
            def _(k=k):
                stage_c_out(g, k - 1).start()

    def do_d(g):
        slot = lax.rem(g, 2)
        total = wide(uq[slot, z])
        for k, cp in enumerate(stage_c(g)):
            cp.wait_recv()
            total = total + wide(zq[g, k])
        gq_out[:, pl.ds(pl.multiple_of(g * group, group), group)] = total

        @pl.when(z == g)
        def _():
            mixed = wide(uo[slot])
            for k in range(planes - 1):
                stage_c_out(g, k).wait_recv()
                mixed = mixed + wide(zo[k])
            go_out[...] = mixed

        for k in range(1, planes):

            @pl.when(lax.rem(g + planes - z, planes) == k)
            def _(k=k):
                stage_c_out(g, k - 1).wait_send()

        for cp in stage_c(g):
            cp.wait_send()

    for cp in first:
        cp.wait()
    gains_acc[...] = jnp.zeros_like(gains_acc)

    def norm_two(b, carry):
        at = pl.ds(pl.multiple_of(b * tile, tile), tile)
        m = mid_v[at, :]
        inv = lax.rsqrt(jnp.mean(m * m, axis=-1, keepdims=True) + EPSILON)
        normed = m * inv
        grad = wide(q_v[at, :])
        gains_acc[1:2, :] += jnp.sum(grad * normed, axis=0, keepdims=True)
        grad = grad * gain_v[1:2, :]
        grad = wide(x_v[b]) + inv * (grad - normed * jnp.mean(grad * normed, axis=-1, keepdims=True))
        mid_v[at, :] = grad
        proj_v[at, :] = grad.astype(BF16)
        gh1_v[at, :] = jnp.zeros_like(grad)
        return carry

    lax.fori_loop(0, chips, norm_two, 0)
    tokens_again.start()
    queries = load(q_in, q_v, 4)
    queries.start()
    for cp in second + [queries]:
        cp.wait()
    kvacc[...] = jnp.zeros_like(kvacc)
    seg_cols = [jnp.transpose(marks_v[c, b].astype(F32))[:, 0:1] for b in range(chips)]
    key_seg = jnp.concatenate(
        [marks_v[k % 2, k // 2, 0:1, :] for k in range(2 * chips)], axis=1
    ).astype(F32)

    def one_group(g, carry):
        slot = lax.rem(g, 2)
        column = pl.multiple_of(g * group, group)
        for cp in fetch(g):
            cp.wait()

        @pl.when(g + 1 < groups)
        def _():
            for cp in fetch(g + 1):
                cp.start()

        w = wo_b[slot].reshape(group, width)
        mix_v[...] = dot2(proj_v[...], w, 1, 1).astype(BF16)
        for b in range(chips):
            extent = (b + 1) * 2 * tile
            at = pl.ds(b * tile, tile)
            kvs = kv_v[pl.ds(0, b + 1)].reshape(extent, 2 * head_dim)
            keys, values = kvs[:, :head_dim], kvs[:, head_dim:]
            place = (2 * b + c) * tile + lax.broadcasted_iota(jnp.int32, (tile, extent), 0)
            seen = lax.broadcasted_iota(jnp.int32, (tile, extent), 1)
            allowed = (place >= seen) & (seg_cols[b] == key_seg[:, :extent])
            bias = jnp.where(allowed, 0.0, MASKED).astype(F32)
            cosine, sine = cos_v[at, :], sin_v[at, :]
            for first_head in range(0, heads, 2):
                span = range(first_head, first_head + 2)
                q = jnp.concatenate(
                    [q_v[at, pl.ds(pl.multiple_of(column + h * head_dim, head_dim), head_dim)] for h in span],
                    axis=0,
                )
                grads = jnp.concatenate(
                    [mix_v[at, pl.ds(h * head_dim, head_dim)] for h in span], axis=0
                )
                scores = dot2(q, keys, 1, 1) * scale
                scores = (scores.reshape(2, tile, extent) + bias[None]).reshape(2 * tile, extent)
                top = jnp.max(scores, axis=-1, keepdims=True)
                soft = jnp.exp(scores - top)
                soft = soft * (1.0 / jnp.sum(soft, axis=-1, keepdims=True))
                grad_soft = dot2(grads, values, 1, 1)
                inner = jnp.sum(soft * grad_soft, axis=-1, keepdims=True)
                grad_scores = (soft * (grad_soft - inner)).astype(BF16)
                both = jnp.concatenate(
                    [dot2(grad_scores, q, 0, 0) * scale, dot2(soft.astype(BF16), grads, 0, 0)],
                    axis=1,
                )
                kvacc[pl.ds(0, b + 1)] += both.reshape(b + 1, 2, tile, 2 * head_dim)
                grad_q = dot2(grad_scores, keys, 1, 0) * scale
                for i, h in enumerate(span):
                    part = turn(grad_q[i * tile : (i + 1) * tile], cosine, -sine)
                    lin_v[at, pl.ds(h * head_dim, head_dim)] = part.astype(BF16)

        @pl.when(g >= 1)
        def _():
            do_b(g - 1)
            for cp in stage_a(g - 1):
                cp.wait_send()

        left = att_t_v[pl.ds(column, group), :]

        def weights(n, carry):
            at = pl.ds(pl.multiple_of(n * group, group), group)
            part = dot2(h1t_v[at, :], lin_v[...], 1, 0)
            sq[n] = part.astype(BF16).reshape(chips, 2, shard, group)
            part = dot2(left, proj_v[:, at], 1, 0)
            so[:, :, :, at] = part.astype(BF16).reshape(chips, 2, shard, group)
            return carry

        lax.fori_loop(0, planes, weights, 0)
        for cp in stage_a(g):
            cp.start()

        def inputs(n, carry):
            at = pl.ds(pl.multiple_of(n * group, group), group)
            gh1_v[:, at] += dot2(lin_v[...], wq_b[slot, n].reshape(group, group), 1, 1)
            return carry

        lax.fori_loop(0, planes, inputs, 0)

        @pl.when(g >= 2)
        def _():
            do_c(g - 2)

        @pl.when(g >= 3)
        def _():
            do_d(g - 3)

        return carry

    lax.fori_loop(0, groups, one_group, 0)

    to_other = p.copy(kvacc.at[:, 1 - c], kvx, "kx", 0, p.to_core)
    to_other.start()
    do_b(groups - 1)
    to_other.wait_recv()
    for b in range(chips):
        at = pl.ds(b * tile, tile)
        part = kvacc[b, c] + kvx[b]
        turned = turn(part[:, :head_dim], cos_v[at, :], -sin_v[at, :])
        gl_v[at, :] = jnp.concatenate([turned, part[:, head_dim:]], axis=1).astype(BF16)

    def last_inputs(n, carry):
        at = pl.ds(pl.multiple_of(n * group, group), group)
        gh1_v[:, at] += dot2(gl_v[...], wk_v[n].reshape(group, 2 * head_dim), 1, 1)
        part = dot2(h1t_v[at, :], gl_v[...], 1, 0).astype(BF16)
        skv[n, :, :, :, pl.ds(0, 2 * head_dim)] = part.reshape(chips, 2, shard, 2 * head_dim)
        return carry

    lax.fori_loop(0, planes, last_inputs, 0)
    tokens_again.wait()

    def norm_one(b, carry):
        at = pl.ds(pl.multiple_of(b * tile, tile), tile)
        x = wide(x_v[b])
        inv = lax.rsqrt(jnp.mean(x * x, axis=-1, keepdims=True) + EPSILON)
        normed = x * inv
        grad = gh1_v[at, :]
        gains_acc[0:1, :] += jnp.sum(grad * normed, axis=0, keepdims=True)
        grad = grad * gain_v[0:1, :]
        grad = mid_v[at, :] + inv * (
            grad - normed * jnp.mean(grad * normed, axis=-1, keepdims=True)
        )
        proj_v[at, :] = grad.astype(BF16)
        return carry

    lax.fori_loop(0, chips, norm_one, 0)
    for i in range(width // head_dim):
        part = gains_acc[:, pl.ds(i * head_dim, head_dim)]
        part = jnp.concatenate([part, jnp.zeros((head_dim - 8, head_dim), F32)], axis=0)
        part = jnp.transpose(part).astype(BF16).reshape(2, shard, head_dim)
        skv[i // 4, i % 4, :, :, pl.ds(2 * head_dim, head_dim)] = part
    a_kv = p.copy(skv.at[:, :, 1 - c], rkv, "akv", 0, p.to_core)
    a_kv.start()
    homes = [
        p.copy(proj_v.at[pl.ds(pl.multiple_of(o * tile, tile), tile)], home.at[s], "home", i, t)
        for i, (t, o) in enumerate(others)
    ]
    do_c(groups - 2)
    a_kv.wait_recv()

    def last_b(a, carry):
        tkv[a] = (wide(skv[a, :, c]) + wide(rkv[a])).astype(BF16)
        return carry

    lax.fori_loop(0, planes, last_b, 0)
    b_kv = [
        p.copy(tkv.at[:, o], pkv.at[i], "bkv", i, t) for i, (t, o) in enumerate(others)
    ]
    for cp in b_kv:
        cp.start()
    for cp in homes:
        cp.start()
    own_home = load(proj_v.at[pl.ds(pl.multiple_of(s * tile, tile), tile)], home.at[s], 0)
    own_home.start()
    do_d(groups - 3)
    do_c(groups - 1)
    do_d(groups - 2)
    total = wide(tkv[:, s])
    for i, cp in enumerate(b_kv):
        cp.wait_recv()
        total = total + wide(pkv[i])
    ukv[...] = total.astype(BF16)
    c_kv = [
        p.copy(ukv.at[a], zkv.at[k], "ckv", k, (a, s, c)) for k, a in enumerate(lines)
    ]
    for cp in c_kv:
        cp.start()
    do_d(groups - 1)
    total = wide(ukv[z])
    for k, cp in enumerate(c_kv):
        cp.wait_recv()
        total = total + wide(zkv[k])
    gkv_out[...] = total
    for cp in homes:
        cp.wait_recv()
    own_home.wait()
    for cp in [to_other, a_kv] + b_kv + c_kv + homes:
        cp.wait_send()
    for cp in list(stage_a(groups - 1)) + stage_b(groups - 2) + stage_b(groups - 1):
        cp.wait_send()


def back(tile, gh2, grads_in, middle, x_in, wq, wo, h1t, q, att_t, kv, cosine, sine, marks, gains):
    planes, chips, pair, shard, width = wo.shape
    rows = chips * tile
    head_dim = kv.shape[-1] // 2
    group = 512
    groups = width // group
    last = wq.shape[-1] - width
    V = pltpu.VMEM
    sd = jax.ShapeDtypeStruct
    outs = [
        sd((chips, tile, width), BF16),
        sd((shard, width), F32),
        sd((shard, last), F32),
        sd((shard, width), F32),
    ]
    anyspec = pl.BlockSpec(memory_space=pl.ANY)
    inner = pl.BlockSpec(memory_space=V)
    scratch = [
        pltpu.SemaphoreType.DMA((GROUPS, 4)),
        pltpu.SemaphoreType.DMA((GROUPS, 4)),
        pltpu.SemaphoreType.DMA((16,)),
        V((rows, width), F32),
        V((rows, width), F32),
        V((chips, tile, width), BF16),
        V((rows, width), BF16),
        V((width, rows), BF16),
        V((rows, width), BF16),
        V((width, rows), BF16),
        V((chips, pair, tile, 2 * head_dim), BF16),
        V((rows, head_dim), F32),
        V((rows, head_dim), F32),
        V(marks.shape, jnp.int32),
        V((2, chips, pair, shard, width), BF16),
        V((2, planes, chips, pair, shard, group), BF16),
        V((planes, chips, pair, shard, 2 * head_dim), BF16),
        V((rows, group), BF16),
        V((rows, group), BF16),
        V((chips, pair, tile, 2 * head_dim), F32),
        V((chips, tile, 2 * head_dim), F32),
        V((8, width), F32),
        V((planes, chips, pair, shard, group), BF16),
        V((chips, pair, shard, width), BF16),
        V((2, planes, chips, shard, group), BF16),
        V((2, chips, shard, width), BF16),
        V((2, planes, chips, shard, group), BF16),
        V((2, chips, shard, width), BF16),
        V((groups, 3, planes, shard, group), BF16),
        V((groups, 3, shard, width), BF16),
        V((2, planes, shard, group), BF16),
        V((2, shard, width), BF16),
        V((groups, 3, shard, group), BF16),
        V((3, shard, width), BF16),
        V((planes, chips, pair, shard, last), BF16),
        V((planes, chips, shard, last), BF16),
        V((planes, chips, shard, last), BF16),
        V((3, planes, shard, last), BF16),
        V((planes, shard, last), BF16),
        V((3, shard, last), BF16),
        V((rows, 2 * head_dim), BF16),
    ]
    return pl.pallas_call(
        functools.partial(back_kernel, (tile, width, head_dim, group)),
        out_shape=outs,
        in_specs=[anyspec] * 13 + [inner],
        out_specs=[anyspec] + [inner] * 3,
        scratch_shapes=scratch,
        compiler_params=pltpu.CompilerParams(
            collective_id=2, has_side_effects=True, vmem_limit_bytes=63 * 1024 * 1024
        ),
        cost_estimate=pl.CostEstimate(
            flops=1_000_000_000, bytes_accessed=1_000_000, transcendentals=0
        ),
        name="back",
    )(gh2, grads_in, middle, x_in, wq, wo, h1t, q, att_t, kv, cosine, sine, marks, gains)


def middle_kernel(
    plan,
    two_in,
    grads,
    gate_up,
    down,
    residual,
    two_out,
    pre_out,
    hidden_out,
    partial_out,
    sum_out,
    send_sem,
    recv_sem,
    local_sem,
    gu_v,
    down_v,
    res_b,
    out_b,
    two_v,
    e_v,
    pre_v,
    hidden_v,
    far_v,
    x_v,
    y_v,
    own_v,
    xa_far,
    xa_own,
    yb_far,
    yb_own,
    ya_pass,
    xb_pass,
):
    rows, width, hidden = plan
    half = width // 2
    wide_tile, out_tile = 256, 512
    tiles = width // out_tile
    p = Post(send_sem, recv_sem)
    low, high = pl.ds(0, half), pl.ds(half, half)
    top, bottom = pl.ds(0, rows // 2), pl.ds(rows // 2, rows // 2)
    order = (p.own, p.by_x, p.by_y, p.far)
    targets = (own_v, x_v, y_v, far_v)

    def load(src, dst, index):
        return pltpu.make_async_copy(src, dst, local_sem.at[index])

    def fetch(i):
        return load(grads.at[order[i]], e_v, 0)

    def keep_pre(i):
        at = pl.ds(pl.multiple_of(order[i] * rows, rows), rows)
        return load(pre_v, pre_out.at[at], 1)

    def keep_hidden(i):
        at = pl.ds(pl.multiple_of(order[i] * rows, rows), rows)
        return load(hidden_v.at[i], hidden_out.at[at], 2 + i)

    def keep_two(i):
        return load(two_v.at[order[i]], two_out.at[order[i]], 6 + i)

    def columns(n):
        return pl.ds(pl.multiple_of(n * out_tile, out_tile), out_tile)

    def residual_tile(n):
        return load(residual.at[:, columns(n)], res_b.at[lax.rem(n, 2)], 10 + lax.rem(n, 2))

    def place(i, n):
        slot = lax.rem(n, 2)
        return load(out_b.at[slot], partial_out.at[order[i], :, columns(n)], 12 + slot)

    weights = [load(gate_up, gu_v, 14), load(down, down_v, 15)]
    mine = load(two_in, two_v.at[p.own], 16)
    for cp in [mine, fetch(0)] + weights:
        cp.start()
    residual_tile(0).start()
    bar = pltpu.get_barrier_semaphore()
    for target in (p.to_x, p.to_y):
        pl.semaphore_signal(bar, inc=1, device_id=target, device_id_type=MESH)
    pl.semaphore_wait(bar, 2)
    sends = [
        p.copy(two_in, two_v.at[p.own], "two_x", 0, p.to_x),
        p.copy(two_in, two_v.at[p.own], "two_y", 0, p.to_y),
    ]
    relays = [
        p.copy(two_v.at[p.by_x, top], two_v.at[p.by_x, top], "two_l", 0, p.to_y),
        p.copy(two_v.at[p.by_y, bottom], two_v.at[p.by_y, bottom], "two_h", 0, p.to_x),
    ]
    for cp in sends:
        cp.start()
    for cp in weights + [mine]:
        cp.wait()

    def chunk(i, start, size):
        at, above = pl.ds(start, size), pl.ds(start + hidden, size)
        gate = dot2(two_v[order[i]], gu_v[:, at], 1, 0)
        up = dot2(two_v[order[i]], gu_v[:, above], 1, 0)
        grad = dot2(e_v[...], down_v[at, :], 1, 1)
        sig = jax.nn.sigmoid(gate)
        silu = gate * sig
        hidden_v[i, :, at] = (silu * up).astype(BF16)
        pre_v[:, at] = (grad * up * sig * (1.0 + gate * (1.0 - sig))).astype(BF16)
        pre_v[:, above] = (grad * silu).astype(BF16)

    whole_tiles = hidden // wide_tile
    x_low = p.copy(x_v.at[:, low], xa_own, "xa_own", 0, p.to_x)
    y_high = p.copy(y_v.at[:, high], yb_own, "yb_own", 0, p.to_y)
    far_low = p.copy(far_v.at[:, low], xa_far, "xa_far", 0, p.to_x)
    far_high = p.copy(far_v.at[:, high], yb_far, "yb_far", 0, p.to_y)
    x_high = p.copy(x_v.at[:, high], xb_pass, "xb_pass", 0, p.to_x)
    y_low = p.copy(y_v.at[:, low], ya_pass, "ya_pass", 0, p.to_y)
    for i in range(4):
        if i == 1:
            for cp, relay in zip(sends, relays):
                cp.wait_recv()
                relay.start()
        if i == 3:
            for relay in relays:
                relay.wait_recv()
        fetch(i).wait()
        keep_two(i).start()

        def step(j, carry, i=i):
            chunk(i, pl.multiple_of(j * wide_tile, wide_tile), wide_tile)
            return carry

        lax.fori_loop(0, whole_tiles, step, 0)
        if hidden % wide_tile:
            chunk(i, whole_tiles * wide_tile, hidden % wide_tile)
        if i < 3:
            fetch(i + 1).start()
        keep_pre(i).start()
        keep_hidden(i).start()

        def back_tile(n, carry, i=i):
            targets[i][:, columns(n)] = dot2(pre_v[...], gu_v[columns(n), :], 1, 1).astype(BF16)
            return carry

        lax.fori_loop(0, tiles, back_tile, 0)
        keep_pre(i).wait()
        for cp in ((), (x_low,), (y_high,), (far_low, far_high))[i]:
            cp.start()

    def output(i):
        def out_chunk(n, carry):
            @pl.when(n >= 2)
            def _():
                place(i, n - 2).wait()

            part = dot2(hidden_v[i], down_v[:, columns(n)], 1, 0)
            if i == 0:

                @pl.when(n + 1 < tiles)
                def _():
                    residual_tile(n + 1).start()

                residual_tile(n).wait()
                part = part + res_b[lax.rem(n, 2)]
            out_b[lax.rem(n, 2)] = part.astype(BF16)
            place(i, n).start()
            return carry

        lax.fori_loop(0, tiles, out_chunk, 0)
        place(i, tiles - 2).wait()
        place(i, tiles - 1).wait()

    for i in (0, 1, 2):
        output(i)
    far_high.wait_recv()
    x_v[:, high] = (x_v[:, high].astype(F32) + yb_far[...].astype(F32)).astype(BF16)
    x_high.start()
    far_low.wait_recv()
    y_v[:, low] = (y_v[:, low].astype(F32) + xa_far[...].astype(F32)).astype(BF16)
    y_low.start()
    output(3)
    for i in range(4):
        keep_hidden(i).wait()
        keep_two(i).wait()
    for cp in (x_low, y_low, y_high, x_high):
        cp.wait_recv()
    own_v[:, low] = (
        own_v[:, low].astype(F32) + xa_own[...].astype(F32) + ya_pass[...].astype(F32)
    ).astype(BF16)
    own_v[:, high] = (
        own_v[:, high].astype(F32) + yb_own[...].astype(F32) + xb_pass[...].astype(F32)
    ).astype(BF16)
    done = load(own_v, sum_out, 0)
    done.start()
    done.wait()
    for cp in sends + relays + [x_low, x_high, y_low, y_high, far_low, far_high]:
        cp.wait_send()


def middle_call(two, grads, gate_up, down, residual):
    chips = grads.shape[0]
    rows, width = two.shape
    hidden = down.shape[0]
    V = pltpu.VMEM
    sd = jax.ShapeDtypeStruct
    anyspec = pl.BlockSpec(memory_space=pl.ANY)
    block = (rows, width)
    part = (rows, width // 2)
    return pl.pallas_call(
        functools.partial(middle_kernel, (rows, width, hidden)),
        out_shape=[
            sd((chips,) + block, BF16),
            sd((chips * rows, 2 * hidden), BF16),
            sd((chips * rows, hidden), BF16),
            sd((chips,) + block, BF16),
            sd(block, BF16),
        ],
        in_specs=[anyspec] * 5,
        out_specs=[anyspec] * 5,
        scratch_shapes=[
            pltpu.SemaphoreType.DMA((10, 4)),
            pltpu.SemaphoreType.DMA((10, 4)),
            pltpu.SemaphoreType.DMA((17,)),
            V((width, 2 * hidden), BF16),
            V((hidden, width), BF16),
            V((2, rows, 512), F32),
            V((2, rows, 512), BF16),
            V((chips,) + block, BF16),
            V(block, BF16),
            V((rows, 2 * hidden), BF16),
            V((chips, rows, hidden), BF16),
        ]
        + [V(block, BF16)] * 4
        + [V(part, BF16)] * 6,
        compiler_params=pltpu.CompilerParams(
            collective_id=3, has_side_effects=True, vmem_limit_bytes=63 * 1024 * 1024
        ),
        cost_estimate=pl.CostEstimate(
            flops=80_000_000_000, bytes_accessed=60_000_000, transcendentals=10_000_000
        ),
        name="feed_forward",
    )(two, grads, gate_up, down, residual)


def trade_kernel(blocks, gate_out, up_out, got, send_sem, recv_sem, local_sem):
    chips, shard, columns = got.shape
    piece = columns // 8
    p = Post(send_sem, recv_sem)
    others = ((p.to_x, p.by_x), (p.to_y, p.by_y), (p.to_far, p.far))
    mine = pltpu.make_async_copy(blocks.at[p.own], got.at[p.own], local_sem.at[0])
    mine.start()
    bar = pltpu.get_barrier_semaphore()
    for target, _ in others:
        pl.semaphore_signal(bar, inc=1, device_id=target, device_id_type=MESH)
    pl.semaphore_wait(bar, 3)
    copies = [
        p.copy(blocks.at[o], got.at[p.own], "trade", i, t) for i, (t, o) in enumerate(others)
    ]
    for cp in copies:
        cp.start()
    mine.wait()
    for cp in copies:
        cp.wait_recv()
    for half, out in enumerate((gate_out, up_out)):
        parts = [
            got[chip, :, (half * 4 + plane) * piece : (half * 4 + plane + 1) * piece].astype(F32)
            for plane in range(4)
            for chip in range(chips)
        ]
        out[...] = jnp.concatenate(parts, axis=1)
    for cp in copies:
        cp.wait_send()


def trade(blocks, hidden):
    chips, shard, columns = blocks.shape
    V = pltpu.VMEM
    return pl.pallas_call(
        trade_kernel,
        out_shape=[jax.ShapeDtypeStruct((shard, hidden), F32)] * 2,
        in_specs=[pl.BlockSpec(memory_space=pl.ANY)],
        out_specs=[pl.BlockSpec(memory_space=V)] * 2,
        scratch_shapes=[
            V(blocks.shape, BF16),
            pltpu.SemaphoreType.DMA((1, 4)),
            pltpu.SemaphoreType.DMA((1, 4)),
            pltpu.SemaphoreType.DMA((1,)),
        ],
        compiler_params=pltpu.CompilerParams(
            collective_id=4, has_side_effects=True, vmem_limit_bytes=32 * 1024 * 1024
        ),
        name="trade",
    )(blocks)


class PlaneSum:
    def __init__(self, post, partial, column, buffers, local_sem):
        p = self.p = post
        self.x_v, self.y_v, self.own_v = buffers[:3]
        self.xa_far, self.xa_own, self.yb_far, self.yb_own, self.ya_pass, self.xb_pass = buffers[3:]
        half = self.xa_far.shape[-1]
        self.low, self.high = pl.ds(0, half), pl.ds(half, half)
        low, high, both = (
            pl.ds(column, half),
            pl.ds(column + half, half),
            pl.ds(column, 2 * half),
        )
        self.loads = [
            pltpu.make_async_copy(partial.at[:, chip, :, both], ref, local_sem.at[i])
            for i, (chip, ref) in enumerate(
                ((p.by_x, self.x_v), (p.by_y, self.y_v), (p.own, self.own_v))
            )
        ]
        self.far_low = p.copy(partial.at[:, p.far, :, low], self.xa_far, "xa_far", 0, p.to_x)
        self.far_high = p.copy(partial.at[:, p.far, :, high], self.yb_far, "yb_far", 0, p.to_y)
        self.x_low = p.copy(partial.at[:, p.by_x, :, low], self.xa_own, "xa_own", 0, p.to_x)
        self.y_high = p.copy(partial.at[:, p.by_y, :, high], self.yb_own, "yb_own", 0, p.to_y)
        self.x_high = p.copy(self.x_v.at[:, :, self.high], self.xb_pass, "xb_pass", 0, p.to_x)
        self.y_low = p.copy(self.y_v.at[:, :, self.low], self.ya_pass, "ya_pass", 0, p.to_y)

    def start(self):
        for cp in [self.far_low, self.far_high, self.x_low, self.y_high] + self.loads:
            cp.start()

    def turn(self):
        for cp in self.loads:
            cp.wait()
        self.far_high.wait_recv()
        total = self.x_v[:, :, self.high].astype(F32) + self.yb_far[...].astype(F32)
        self.x_v[:, :, self.high] = total.astype(BF16)
        self.x_high.start()
        self.far_low.wait_recv()
        total = self.y_v[:, :, self.low].astype(F32) + self.xa_far[...].astype(F32)
        self.y_v[:, :, self.low] = total.astype(BF16)
        self.y_low.start()

    def finish(self, out, sem):
        for cp in (self.x_low, self.y_low, self.y_high, self.x_high):
            cp.wait_recv()
        for at, direct, passed in (
            (self.low, self.xa_own, self.ya_pass),
            (self.high, self.yb_own, self.xb_pass),
        ):
            total = self.own_v[:, :, at].astype(F32) + direct[...].astype(F32)
            self.own_v[:, :, at] = (total + passed[...].astype(F32)).astype(BF16)
        done = pltpu.make_async_copy(self.own_v, out, sem)
        done.start()
        done.wait()
        for cp in (self.far_low, self.far_high, self.x_low, self.y_high, self.x_high, self.y_low):
            cp.wait_send()


def weight_grad_kernel(
    plan, left, right, partial, sum_out, rows_out, send_sem, recv_sem, local_sem, *scratch
):
    turned, width, tile, column = plan
    left_v, right_v, left_t, stage, got, total_v = scratch[:6]
    planes = got.shape[0]
    p = Post(send_sem, recv_sem)
    c = p.core
    plane_sum = PlaneSum(p, partial, column, scratch[6:], local_sem)
    load_left = pltpu.make_async_copy(left, left_v, local_sem.at[3])
    load_right = pltpu.make_async_copy(right, right_v, local_sem.at[4])
    load_left.start()
    load_right.start()
    bar = pltpu.get_barrier_semaphore()
    for target in (p.to_x, p.to_y, p.to_core):
        pl.semaphore_signal(bar, inc=1, device_id=target, device_id_type=MESH)
    pl.semaphore_wait(bar, 3)
    plane_sum.start()
    height = 1
    for size in stage.shape[1:-1]:
        height *= size
    rank = len(stage.shape) - 1
    own = (slice(None),) * (rank - 3) + (c,)
    other = (slice(None),) * (rank - 3) + (1 - c,)

    def to_core(z):
        return p.copy(stage.at[(z % 2,) + other], got.at[z], "core", z, p.to_core)

    def keep(z):
        return pltpu.make_async_copy(total_v.at[z % 2], sum_out.at[z], local_sem.at[5 + z % 2])

    def add(z):
        to_core(z).wait_recv()
        if z >= 2:
            keep(z - 2).wait()
        mine = stage[(z % 2,) + own].astype(F32)
        total_v[z % 2] = (mine + got[z].astype(F32)).astype(BF16)
        keep(z).start()

    load_left.wait()
    for z in range(planes):
        if z >= 2:
            to_core(z - 2).wait_send()
        start = z * height
        first = start // turned * turned
        last = -(-(start + height) // turned) * turned
        for at in range(first, last, turned):
            if at >= start or z == 0:
                left_t[pl.ds(at, turned), :] = jnp.transpose(left_v[:, at : at + turned])
        if z == 0:
            load_right.wait()

        def columns(n, carry, z=z, start=start):
            at = pl.ds(pl.multiple_of(n * tile, tile), tile)
            part = dot2(left_t[pl.ds(start, height), :], right_v[:, at], 1, 0).astype(BF16)
            stage[z % 2, ..., at] = part.reshape(stage.shape[1:-1] + (tile,))
            return carry

        lax.fori_loop(0, width // tile, columns, 0)
        to_core(z).start()
        if z >= 1:
            add(z - 1)
        if z == 2:
            plane_sum.turn()
    add(planes - 1)
    plane_sum.finish(rows_out, local_sem.at[7])
    for z in (planes - 2, planes - 1):
        keep(z).wait()
        to_core(z).wait_send()


def weight_grad(left, right, partial, block, tile, column, name, identity):
    planes = block[0]
    rows, height = left.shape
    width = right.shape[1]
    chips, tokens = partial.shape[0], partial.shape[2]
    half = partial.shape[3] // 4
    V = pltpu.VMEM
    anyspec = pl.BlockSpec(memory_space=pl.ANY)
    inner = block[1:]
    kept = inner[:-2] + inner[-1:]
    part = (chips, tokens, half)
    both = (chips, tokens, 2 * half)
    return pl.pallas_call(
        functools.partial(weight_grad_kernel, (128, width, tile, column)),
        out_shape=[
            jax.ShapeDtypeStruct((planes,) + kept + (width,), BF16),
            jax.ShapeDtypeStruct(both, BF16),
        ],
        in_specs=[anyspec] * 3,
        out_specs=[anyspec] * 2,
        scratch_shapes=[
            pltpu.SemaphoreType.DMA((7, 4)),
            pltpu.SemaphoreType.DMA((7, 4)),
            pltpu.SemaphoreType.DMA((8,)),
            V(left.shape, BF16),
            V(right.shape, BF16),
            V((height, rows), BF16),
            V((2,) + inner + (width,), BF16),
            V((planes,) + kept + (width,), BF16),
            V((2,) + kept + (width,), BF16),
        ]
        + [V(both, BF16)] * 3
        + [V(part, BF16)] * 6,
        compiler_params=pltpu.CompilerParams(
            collective_id=identity, has_side_effects=True, vmem_limit_bytes=62 * 1024 * 1024
        ),
        cost_estimate=pl.CostEstimate(
            flops=2 * rows * height * width, bytes_accessed=40_000_000, transcendentals=0
        ),
        name=name,
    )(left, right, partial)


def body_plane(
    tokens,
    cotangent,
    segments,
    positions,
    w_query,
    w_key,
    w_value,
    w_out,
    w_gate,
    w_up,
    w_down,
    gain_attn,
    gain_mlp,
):
    micro, tile, width = tokens.shape
    head_dim = w_key.shape[1]
    head_count = width // head_dim
    planes = lax.axis_size(LINE)
    chips = lax.axis_size(PLANE)
    pair = lax.axis_size(CORE)
    plane = lax.axis_index(LINE)
    own = lax.axis_index(PLANE)
    core = lax.axis_index(CORE)
    rows = micro * tile
    hidden = w_gate.shape[1]
    shard = w_query.shape[0]
    own_hidden = hidden // chips
    piece = own_hidden // planes
    qkv = width + 2 * head_dim
    score_scale = 1.0 / math.sqrt(head_dim)

    gains = jnp.stack([gain_attn, gain_mlp], axis=1)
    gains = jnp.pad(gains, ((0, 0), (0, head_dim - 2)))
    w_in = jnp.concatenate([w_query, w_key, w_value, gains], axis=1)
    gate_up = jnp.stack([w_gate, w_up], axis=1).reshape(shard, 2, planes, chips, piece)
    gate_up = gate_up.transpose(3, 0, 1, 2, 4).reshape(chips, shard, 2 * own_hidden)
    marks = jnp.pad(jnp.stack([segments, positions], axis=1), ((0, 0), (0, 6), (0, 0)))
    (
        x_rows,
        marks,
        w_qkv,
        out_mat,
        gate_up,
        grads_in,
        hidden_two,
        middle,
        hidden_one,
        queries,
        attended,
        kv,
        kv_home,
        cosine,
        sine,
    ) = front(tokens, cotangent, marks, w_in, w_out, gate_up)
    gains = jnp.pad(w_qkv[..., qkv : qkv + 2].reshape(width, 2).T, ((0, 6), (0, 0))).astype(F32)
    gate_up = gate_up.reshape(width, 2 * own_hidden)
    down_mat = lax.all_gather(w_down, (LINE, CORE), axis=0, tiled=True)
    plane_grads = grads_in.reshape(chips * rows, width)

    plane_two, grad_pre, hidden_mlp, partial_out, grad_hidden_two = middle_call(
        hidden_two,
        grads_in.reshape(chips, rows, width),
        gate_up,
        down_mat,
        middle,
    )
    plane_two = plane_two.reshape(chips * rows, width)
    partial_out = partial_out.reshape(chips, chips, tile, width)
    grad_down, rows_low = weight_grad(
        hidden_mlp,
        plane_grads,
        partial_out,
        (planes, pair, piece // pair),
        512,
        0,
        "down_grad",
        6,
    )
    grad_down, grad_pre = lax.optimization_barrier((grad_down, grad_pre))
    grad_gate_up, rows_high = weight_grad(
        plane_two,
        grad_pre,
        partial_out,
        (planes, chips, pair, shard),
        256,
        width // 2,
        "gate_up_grad",
        5,
    )
    layer_rows = jnp.concatenate([rows_low, rows_high], axis=-1)
    grad_down = scatter_sum(grad_down, LINE, 0).reshape(-1, width).astype(F32)
    grad_gate_up = scatter_sum(grad_gate_up, LINE, 0).reshape(chips, shard, 2 * own_hidden)

    grad_input, grad_q, grad_kv, grad_out = back(
        tile,
        grad_hidden_two,
        grads_in,
        middle,
        x_rows,
        w_qkv,
        out_mat,
        hidden_one,
        queries,
        attended,
        kv,
        cosine,
        sine,
        marks,
        gains,
    )
    grad_gate, grad_up = trade(grad_gate_up, hidden)
    return (
        layer_rows,
        kv_home[..., :head_dim],
        kv_home[..., head_dim:],
        grad_input.astype(F32),
        grad_q,
        grad_kv[:, :head_dim],
        grad_kv[:, head_dim : 2 * head_dim],
        grad_out,
        grad_gate,
        grad_up,
        grad_down,
        grad_kv[:, 2 * head_dim],
        grad_kv[:, 2 * head_dim + 1],
    )


def body(tokens, *rest):
    if tokens.shape[0] == lax.axis_size(PLANE) == 4 and lax.axis_size(CORE) == 2:
        return body_plane(tokens, *rest)
    return body_general(tokens, *rest)


def solution(mesh):
    in_specs = (
        P(None, EVERY, None),
        P(None, EVERY, None),
        P(None, EVERY),
        P(None, EVERY),
        P(EVERY, None),
        P(EVERY, None),
        P(EVERY, None),
        P(EVERY, None),
        P(EVERY, None),
        P(EVERY, None),
        P(EVERY, None),
        P(EVERY),
        P(EVERY),
    )
    out_specs = (
        P(None, EVERY, None),
        P(None, EVERY, None),
        P(None, EVERY, None),
        P(None, EVERY, None),
        P(EVERY, None),
        P(EVERY, None),
        P(EVERY, None),
        P(EVERY, None),
        P(EVERY, None),
        P(EVERY, None),
        P(EVERY, None),
        P(EVERY),
        P(EVERY),
    )
    return jax.shard_map(body, mesh=mesh, in_specs=in_specs, out_specs=out_specs, check_vma=False)
```

```python
import functools
import math

import jax
import jax.numpy as jnp
from jax import lax
from jax.experimental import pallas as pl
from jax.experimental.pallas import tpu as pltpu
from jax.sharding import PartitionSpec as P

EPSILON = 1e-05
MASKED = -1e30
LINE, PLANE, CORE = "dp", "seq", "fsdp"
EVERY = (LINE, PLANE, CORE)
SCORES, KEYS = "qhd,kd->hqk", "hqk,qhd->kd"
ROWS, COLUMNS = "nf,df->nd", "nd,nf->df"
OUTER, INNER = "nd,ne->de", "ne,de->nd"


def rope_tables(places, half_dim):
    frequency = jnp.exp(-math.log(10000.0) * jnp.arange(half_dim, dtype=jnp.float32) / half_dim)
    angles = places.astype(jnp.float32)[:, None] * frequency[None, :]
    return (jnp.cos(angles), jnp.sin(angles))


def rotate(vector, cosine, sine_part):
    half_dim = vector.shape[-1] // 2
    first_half = vector[..., :half_dim]
    second_half = vector[..., half_dim:]
    return jnp.concatenate(
        [
            first_half * cosine - second_half * sine_part,
            second_half * cosine + first_half * sine_part,
        ],
        axis=-1,
    )


def norm_back(grad_normed, normed, inverse):
    return inverse * (grad_normed - normed * jnp.mean(grad_normed * normed, axis=-1, keepdims=True))


def mask_scores(scores, query_place, query_segment, key_segment):
    key_place = jnp.arange(key_segment.shape[0], dtype=jnp.int32)
    allowed = (query_segment[:, None] == key_segment[None, :]) & (
        query_place[:, None] >= key_place[None, :]
    )
    return jnp.where(allowed[None], scores, MASKED)


def attend_micro(micro_item, query_place, block_rows, score_scale):
    queries, keys_seq, values_seq, query_segment, key_segment = micro_item
    query_rows, local_heads, head_dim = queries.shape
    blocks = query_rows // block_rows

    def one_block(block_item):
        block_query, block_place, block_segment = block_item
        scores = (
            jnp.einsum(SCORES, block_query, keys_seq, preferred_element_type=jnp.float32)
            * score_scale
        )
        scores = mask_scores(scores, block_place, block_segment, key_segment)
        row_max = jnp.max(scores, axis=-1, keepdims=True)
        log_total = row_max + jnp.log(jnp.sum(jnp.exp(scores - row_max), axis=-1, keepdims=True))
        soft_weights = jnp.exp(scores - log_total).astype(jnp.bfloat16)
        attended = jnp.einsum(
            "hqk,kd->qhd", soft_weights, values_seq, preferred_element_type=jnp.float32
        )
        return (attended.astype(jnp.bfloat16), log_total)

    return lax.map(
        one_block,
        (
            queries.reshape(blocks, block_rows, local_heads, head_dim),
            query_place.reshape(blocks, block_rows),
            query_segment.reshape(blocks, block_rows),
        ),
    )


def attend_back(micro_item, query_place, block_rows, score_scale):
    queries, keys_seq, values_seq, grad_attended, log_total, query_segment, key_segment = micro_item
    query_rows, local_heads, head_dim = queries.shape
    blocks = query_rows // block_rows

    def one_block(running, block_item):
        grad_keys, grad_values = running
        block_query, block_grad, block_total, block_place, block_segment = block_item
        scores = (
            jnp.einsum(SCORES, block_query, keys_seq, preferred_element_type=jnp.float32)
            * score_scale
        )
        scores = mask_scores(scores, block_place, block_segment, key_segment)
        soft_weights = jnp.exp(scores - block_total)
        grad_soft = jnp.einsum(
            SCORES, block_grad, values_seq, preferred_element_type=jnp.float32
        )
        inner_sum = jnp.sum(soft_weights * grad_soft, axis=-1, keepdims=True)
        grad_scores = (soft_weights * (grad_soft - inner_sum)).astype(jnp.bfloat16)
        grad_queries = (
            jnp.einsum("hqk,kd->qhd", grad_scores, keys_seq, preferred_element_type=jnp.float32)
            * score_scale
        )
        grad_keys = (
            grad_keys
            + jnp.einsum(
                KEYS, grad_scores, block_query, preferred_element_type=jnp.float32
            )
            * score_scale
        )
        grad_values = grad_values + jnp.einsum(
            KEYS,
            soft_weights.astype(jnp.bfloat16),
            block_grad,
            preferred_element_type=jnp.float32,
        )
        return ((grad_keys, grad_values), grad_queries)

    zero_init = jnp.zeros(keys_seq.shape, jnp.float32)
    running, grad_queries = lax.scan(
        one_block,
        (zero_init, zero_init),
        (
            queries.reshape(blocks, block_rows, local_heads, head_dim),
            grad_attended.reshape(blocks, block_rows, local_heads, head_dim),
            log_total,
            query_place.reshape(blocks, block_rows),
            query_segment.reshape(blocks, block_rows),
        ),
    )
    return (grad_queries, running[0], running[1])


def body_general(
    tokens,
    cotangent,
    segments,
    positions,
    w_query,
    w_key,
    w_value,
    w_out,
    w_gate,
    w_up,
    w_down,
    gain_attn,
    gain_mlp,
):
    micro_count, tok_rows, model_width = tokens.shape
    head_dim = w_key.shape[1]
    head_count = model_width // head_dim
    seq_size = lax.axis_size(PLANE)
    pair_size = lax.axis_size(CORE)
    local_heads = head_count // seq_size
    row_count = micro_count * tok_rows
    query_rows = seq_size * tok_rows
    block_rows = min(512, query_rows)
    score_scale = 1.0 / math.sqrt(head_dim)
    gathered = (
        lax.all_gather(w_query, EVERY, axis=0, tiled=True),
        lax.all_gather(w_key, EVERY, axis=0, tiled=True),
        lax.all_gather(w_value, EVERY, axis=0, tiled=True),
        lax.all_gather(w_out, EVERY, axis=0, tiled=True),
        lax.all_gather(w_gate, EVERY, axis=0, tiled=True),
        lax.all_gather(w_up, EVERY, axis=0, tiled=True),
        lax.all_gather(w_down, EVERY, axis=0, tiled=True),
        lax.all_gather(gain_attn, EVERY, axis=0, tiled=True),
        lax.all_gather(gain_mlp, EVERY, axis=0, tiled=True),
    )
    query_mat, key_mat, value_mat, out_mat, gate_mat, up_mat, down_mat, gain_one, gain_two = (
        gathered
    )
    flat_rows = tokens.reshape(row_count, model_width).astype(jnp.float32)
    inverse_one = lax.rsqrt(jnp.mean(flat_rows * flat_rows, axis=-1, keepdims=True) + EPSILON)
    normed_one = flat_rows * inverse_one
    hidden_one = (normed_one * gain_one.astype(jnp.float32)).astype(jnp.bfloat16)
    cosine, sine_part = rope_tables(positions.reshape(row_count), head_dim // 2)
    query_lin = jnp.dot(hidden_one, query_mat, preferred_element_type=jnp.float32).reshape(
        row_count, head_count, head_dim
    )
    queries = rotate(query_lin, cosine[:, None, :], sine_part[:, None, :]).astype(jnp.bfloat16)
    keys_local = rotate(
        jnp.dot(hidden_one, key_mat, preferred_element_type=jnp.float32), cosine, sine_part
    ).astype(jnp.bfloat16)
    values_local = jnp.dot(hidden_one, value_mat, preferred_element_type=jnp.float32).astype(
        jnp.bfloat16
    )
    keys_local = keys_local.reshape(micro_count, tok_rows, head_dim)
    values_local = values_local.reshape(micro_count, tok_rows, head_dim)
    keys_seq, values_seq, segment_seq = (
        lax.all_gather(keys_local, (PLANE, CORE), axis=1, tiled=True),
        lax.all_gather(values_local, (PLANE, CORE), axis=1, tiled=True),
        lax.all_gather(segments.astype(jnp.bfloat16), (PLANE, CORE), axis=1, tiled=True),
    )
    key_segment = segment_seq.astype(jnp.int32)
    pair_index = lax.axis_index(CORE)
    query_place = (
        (jnp.arange(seq_size, dtype=jnp.int32)[:, None] * pair_size + pair_index) * tok_rows
        + jnp.arange(tok_rows, dtype=jnp.int32)[None, :]
    ).reshape(query_rows)
    query_segment = lax.dynamic_index_in_dim(
        key_segment.reshape(micro_count, seq_size, pair_size, tok_rows),
        pair_index,
        axis=2,
        keepdims=False,
    ).reshape(micro_count, query_rows)
    head_queries = lax.all_to_all(
        queries.reshape(micro_count, tok_rows, model_width),
        PLANE,
        split_axis=2,
        concat_axis=1,
        tiled=True,
    )
    head_queries = head_queries.reshape(micro_count, query_rows, local_heads, head_dim)

    def forward_micro(micro_item):
        return attend_micro(micro_item, query_place, block_rows, score_scale)

    attended, log_total = lax.map(
        forward_micro, (head_queries, keys_seq, values_seq, query_segment, key_segment)
    )
    mixed_rows = lax.all_to_all(
        attended.reshape(micro_count, query_rows, local_heads * head_dim),
        PLANE,
        split_axis=1,
        concat_axis=2,
        tiled=True,
    )
    mixed_rows = mixed_rows.reshape(row_count, model_width)
    middle = flat_rows + jnp.dot(mixed_rows, out_mat, preferred_element_type=jnp.float32)
    inverse_two = lax.rsqrt(jnp.mean(middle * middle, axis=-1, keepdims=True) + EPSILON)
    normed_two = middle * inverse_two
    hidden_two = (normed_two * gain_two.astype(jnp.float32)).astype(jnp.bfloat16)
    gate_proj = jnp.dot(hidden_two, gate_mat, preferred_element_type=jnp.float32)
    up_proj = jnp.dot(hidden_two, up_mat, preferred_element_type=jnp.float32)
    gate_sigmoid = jax.nn.sigmoid(gate_proj)
    gate_silu = gate_proj * gate_sigmoid
    hidden_mlp = (gate_silu * up_proj).astype(jnp.bfloat16)
    result = middle + jnp.dot(hidden_mlp, down_mat, preferred_element_type=jnp.float32)
    back_weights = (
        lax.all_gather(w_query, EVERY, axis=0, tiled=True),
        lax.all_gather(w_key, EVERY, axis=0, tiled=True),
        lax.all_gather(w_value, EVERY, axis=0, tiled=True),
        lax.all_gather(w_out, EVERY, axis=0, tiled=True),
        lax.all_gather(w_gate, EVERY, axis=0, tiled=True),
        lax.all_gather(w_up, EVERY, axis=0, tiled=True),
        lax.all_gather(w_down, EVERY, axis=0, tiled=True),
        lax.all_gather(gain_attn, EVERY, axis=0, tiled=True),
        lax.all_gather(gain_mlp, EVERY, axis=0, tiled=True),
    )
    query_mat, key_mat, value_mat, out_mat, gate_mat, up_mat, down_mat, gain_one, gain_two = (
        back_weights
    )
    grad_rows = cotangent.reshape(row_count, model_width).astype(jnp.float32)
    grad_branch = cotangent.reshape(row_count, model_width)
    grad_down_w = jnp.einsum(
        "nf,nd->fd", hidden_mlp, grad_branch, preferred_element_type=jnp.float32
    )
    grad_hidden = jnp.einsum("nd,fd->nf", grad_branch, down_mat, preferred_element_type=jnp.float32)
    grad_gate_pre = (
        grad_hidden * up_proj * gate_sigmoid * (1.0 + gate_proj * (1.0 - gate_sigmoid))
    ).astype(jnp.bfloat16)
    grad_up_pre = (grad_hidden * gate_silu).astype(jnp.bfloat16)
    grad_gate_w = jnp.einsum(
        COLUMNS, hidden_two, grad_gate_pre, preferred_element_type=jnp.float32
    )
    grad_up_w = jnp.einsum(COLUMNS, hidden_two, grad_up_pre, preferred_element_type=jnp.float32)
    grad_hidden_two = jnp.einsum(
        ROWS, grad_gate_pre, gate_mat, preferred_element_type=jnp.float32
    ) + jnp.einsum(ROWS, grad_up_pre, up_mat, preferred_element_type=jnp.float32)
    grad_gain_two = jnp.sum(grad_hidden_two * normed_two, axis=0)
    grad_middle = grad_rows + norm_back(
        grad_hidden_two * gain_two.astype(jnp.float32), normed_two, inverse_two
    )
    grad_proj = grad_middle.astype(jnp.bfloat16)
    grad_out_w = jnp.einsum(OUTER, mixed_rows, grad_proj, preferred_element_type=jnp.float32)
    grad_mixed = jnp.einsum(
        INNER, grad_proj, out_mat, preferred_element_type=jnp.float32
    ).astype(jnp.bfloat16)
    grad_heads = lax.all_to_all(
        grad_mixed.reshape(micro_count, tok_rows, model_width),
        PLANE,
        split_axis=2,
        concat_axis=1,
        tiled=True,
    )
    grad_heads = grad_heads.reshape(micro_count, query_rows, local_heads, head_dim)

    def backward_micro(micro_item):
        return attend_back(micro_item, query_place, block_rows, score_scale)

    grad_head_queries, grad_keys_seq, grad_values_seq = lax.map(
        backward_micro,
        (head_queries, keys_seq, values_seq, grad_heads, log_total, query_segment, key_segment),
    )
    grad_query_rows = lax.all_to_all(
        grad_head_queries.reshape(micro_count, query_rows, local_heads * head_dim).astype(
            jnp.bfloat16
        ),
        PLANE,
        split_axis=1,
        concat_axis=2,
        tiled=True,
    ).astype(jnp.float32)
    grad_keys_own, grad_values_own = (
        lax.psum_scatter(
            grad_keys_seq.astype(jnp.bfloat16), (PLANE, CORE), scatter_dimension=1, tiled=True
        ).astype(jnp.float32),
        lax.psum_scatter(
            grad_values_seq.astype(jnp.bfloat16), (PLANE, CORE), scatter_dimension=1, tiled=True
        ).astype(jnp.float32),
    )
    grad_query_lin = (
        rotate(
            grad_query_rows.reshape(row_count, head_count, head_dim),
            cosine[:, None, :],
            -sine_part[:, None, :],
        )
        .reshape(row_count, model_width)
        .astype(jnp.bfloat16)
    )
    grad_key_lin = rotate(grad_keys_own.reshape(row_count, head_dim), cosine, -sine_part).astype(
        jnp.bfloat16
    )
    grad_value_lin = grad_values_own.reshape(row_count, head_dim).astype(jnp.bfloat16)
    grad_query_w = jnp.einsum(
        OUTER, hidden_one, grad_query_lin, preferred_element_type=jnp.float32
    )
    grad_key_w = jnp.einsum(
        OUTER, hidden_one, grad_key_lin, preferred_element_type=jnp.float32
    )
    grad_value_w = jnp.einsum(
        OUTER, hidden_one, grad_value_lin, preferred_element_type=jnp.float32
    )
    grad_hidden_one = jnp.einsum(
        INNER, grad_query_lin, query_mat, preferred_element_type=jnp.float32
    )
    grad_hidden_one = grad_hidden_one + jnp.einsum(
        INNER, grad_key_lin, key_mat, preferred_element_type=jnp.float32
    )
    grad_hidden_one = grad_hidden_one + jnp.einsum(
        INNER, grad_value_lin, value_mat, preferred_element_type=jnp.float32
    )
    grad_gain_one = jnp.sum(grad_hidden_one * normed_one, axis=0)
    grad_input = grad_middle + norm_back(
        grad_hidden_one * gain_one.astype(jnp.float32), normed_one, inverse_one
    )
    matrix_grads = (
        grad_query_w,
        grad_key_w,
        grad_value_w,
        grad_out_w,
        grad_gate_w,
        grad_up_w,
        grad_down_w,
    )
    shards = tuple(
        lax.psum_scatter(
            grad.astype(jnp.bfloat16), EVERY, scatter_dimension=0, tiled=True
        ).astype(jnp.float32)
        for grad in matrix_grads
    ) + (
        lax.psum_scatter(grad_gain_one, EVERY, scatter_dimension=0, tiled=True),
        lax.psum_scatter(grad_gain_two, EVERY, scatter_dimension=0, tiled=True),
    )
    layer_rows = result.reshape(micro_count, tok_rows, model_width).astype(jnp.bfloat16)
    return (
        layer_rows,
        keys_local,
        values_local,
        grad_input.reshape(micro_count, tok_rows, model_width),
        shards[0],
        shards[1],
        shards[2],
        shards[3],
        shards[4],
        shards[5],
        shards[6],
        shards[7],
        shards[8],
    )


BF16 = jnp.bfloat16
F32 = jnp.float32
MESH = pl.DeviceIdType.MESH
GROUPS = 64


def dot32(left, right, contract):
    return lax.dot_general(left, right, ((contract[0], contract[1]), ((), ())), preferred_element_type=F32)


def turn(vector, cosine, sine):
    return vector * cosine + pltpu.roll(vector, vector.shape[-1] // 2, 1) * sine


def scatter_sum(value, axes, dim):
    return lax.psum_scatter(value, axes, scatter_dimension=dim, tiled=True)


def send_plane(value, step):
    return lax.ppermute(value, PLANE, [(i, i ^ step) for i in range(4)])


def send_core(value):
    return lax.ppermute(value, CORE, [(0, 1), (1, 0)])


def block_of(value, index, dim=0):
    return lax.dynamic_index_in_dim(value, index, axis=dim, keepdims=False)


def put_block(value, block, index, dim=0):
    return lax.dynamic_update_index_in_dim(value, block, index, axis=dim)


def swap_blocks(value, own):
    out = value
    for step in (1, 2, 3):
        other = own ^ step
        out = put_block(out, send_plane(block_of(value, other), step), other)
    return out


def scatter_core(value, core, dim):
    other = send_core(block_of(value, 1 - core, dim))
    return (block_of(value, core, dim).astype(F32) + other.astype(F32)).astype(BF16)


class Post:
    def __init__(self, send_sem, recv_sem):
        self.plane=lax.axis_index(LINE); self.own=lax.axis_index(PLANE); self.core=lax.axis_index(CORE)
        self.planes=lax.axis_size(LINE)
        x=lax.rem(self.own,2); y=lax.div(self.own,2)
        self.by_x=self.own+1-2*x; self.by_y=self.own+2-4*y; self.far=3-self.own
        z,s,c=self.plane,self.own,self.core
        self.to_x=(z,self.by_x,c); self.to_y=(z,self.by_y,c); self.to_far=(z,self.far,c)
        self.to_core=(z,s,1-c)
        self.to_up=(lax.rem(z+1,self.planes),s,c); self.to_down=(lax.rem(z+self.planes-1,self.planes),s,c)
        self.has_up=z<self.planes-1; self.has_down=z>0
        self.send_sem, self.recv_sem = send_sem, recv_sem
        self.sent=[]
        self.steps={0:[(z,())]}
        for k in range(1,self.planes):
            self.steps[k]=[(jnp.clip(z-k,0,self.planes-1),(z-k>=0,)),(jnp.clip(z+k,0,self.planes-1),(z+k<=self.planes-1,))]
        self.groups={}
    def group(self, name):
        return self.groups.setdefault(name, len(self.groups))
    def barrier(self):
        bar=pltpu.get_barrier_semaphore()
        for t in (self.to_x,self.to_y,self.to_far,self.to_core):
            pl.semaphore_signal(bar,inc=1,device_id=t,device_id_type=MESH)
        for chip in (self.by_x,self.by_y,self.far):
            pl.semaphore_signal(bar,inc=1,device_id=(self.plane,chip,1-self.core),device_id_type=MESH)
        @pl.when(self.has_up)
        def _(): pl.semaphore_signal(bar,inc=1,device_id=self.to_up,device_id_type=MESH)
        @pl.when(self.has_down)
        def _(): pl.semaphore_signal(bar,inc=1,device_id=self.to_down,device_id_type=MESH)
        pl.semaphore_wait(bar,7+self.has_up.astype(jnp.int32)+self.has_down.astype(jnp.int32))
    def copy(self, src, dst, name, index, target, arrive=None):
        return pltpu.make_async_remote_copy(src_ref=src,dst_ref=dst,
            send_sem=self.send_sem.at[self.group(name),index],
            recv_sem=self.recv_sem.at[self.group(arrive or name),index],
            device_id=target,device_id_type=MESH)
    def send(self, src, dst, name, index, target, arrive=None, when=()):
        def go(): self.copy(src,dst,name,index,target,arrive).start()
        if when:
            cond=functools.reduce(jnp.logical_and,when)
            pl.when(cond)(go)
        else: go()
        self.sent.append((when,lambda: self.copy(src,dst,name,index,target,arrive).wait_send()))
    def wait(self, ref, name, index):
        self.copy(ref,ref,name,index,self.to_core).wait_recv()
    def finish(self):
        for when,w in self.sent:
            if when: pl.when(functools.reduce(jnp.logical_and,when))(w)
            else: w()

class Line:
    def __init__(self, post, name, unit, own_source):
        self.p, self.name, self.unit, self.src = post, name, unit, own_source
    def start(self):
        p=self.p
        p.send(self.src,self.unit(p.plane),self.name+"_up",p.plane,p.to_up,self.name,(p.has_up,))
        p.send(self.src,self.unit(p.plane),self.name+"_down",p.plane,p.to_down,self.name,(p.has_down,))
    def hop(self, k, then=None):
        p=self.p
        for sign,(at,(here,)) in zip((-1,1),p.steps[k]):
            on=p.has_up if sign<0 else p.has_down
            target=p.to_up if sign<0 else p.to_down
            ref=self.unit(at)
            @pl.when(here)
            def _(ref=ref,at=at): p.wait(ref,self.name,at)
            if k<p.planes-1:
                p.send(ref,ref,self.name+("_up" if sign<0 else "_down"),at,target,self.name,(here,on))
            if then: then(at,here)

class Spread:
    def __init__(self, post, name, unit, low, high):
        self.p,self.name,self.unit,self.low,self.high=post,name,unit,low,high
    def start(self, index, source, when=()):
        p=self.p
        dst=self.unit(index,p.own)
        p.send(source,dst,self.name+"_x",index,p.to_x,None,when)
        p.send(source,dst,self.name+"_y",index,p.to_y,None,when)
    def relay(self, index, when=()):
        p=self.p
        def go(f):
            if when: pl.when(functools.reduce(jnp.logical_and,when))(f)
            else: f()
        go(lambda: p.wait(self.unit(index,p.by_x),self.name+"_x",index))
        ref=self.low(index,p.by_x)
        p.send(ref,ref,self.name+"_l",index,p.to_y,None,when)
        go(lambda: p.wait(self.unit(index,p.by_y),self.name+"_y",index))
        ref=self.high(index,p.by_y)
        p.send(ref,ref,self.name+"_h",index,p.to_x,None,when)
    def arrive(self, index, when=()):
        p=self.p
        def go():
            p.wait(self.low(index,p.far),self.name+"_l",index)
            p.wait(self.high(index,p.far),self.name+"_h",index)
        if when: pl.when(functools.reduce(jnp.logical_and,when))(go)
        else: go()


def dot2(l, r, ca, cb):
    return dot32(l, r, ((ca,), (cb,)))


def front_kernel(plan,tok,cot,marks,wq_in,wo_in,gu_in,freq,
    x_out,marks_out,wq_out,wo_out,gu,E,two,middle_out,h1_out,q_out,att_out,kv_out,home,cos_out,sin_out,
    send_sem,recv_sem,local_sem,b_cot,b_gu,
    x_v,marks_v,wq_v,wo_v,h1_v,lin_v,q_v,att_v,kv_v,mid_v,two_v,cos_v,sin_v,gain_v,h1t_v,att_t_v):
    tile,width,head_dim,group=plan
    scale=head_dim**-0.5
    p=Post(send_sem,recv_sem)
    z,s,c=p.plane,p.own,p.core
    chips=4
    rows=chips*tile
    groups=width//group; heads=group//head_dim
    qkv=width+2*head_dim
    count=[0]
    outs_=[]
    def local(src,dst):
        cp=pltpu.make_async_copy(src,dst,local_sem.at[count[0]]); count[0]+=1
        cp.start(); return cp
    def out(src,dst):
        outs_.append(local(src,dst))
    loads=[local(tok.at[s],x_v.at[s]),local(marks.at[s],marks_v.at[c,s]),local(wq_in,wq_v.at[z,s,c]),local(wo_in,wo_v.at[z,s,c])]
    late=[local(cot,b_cot),local(gu_in.at[s],b_gu)]
    p.barrier()
    def attention_weight(name, arr, src):
        n=arr.shape[3]//2
        spread=Spread(p,name,lambda a,b: arr.at[a,b,c],lambda a,b: arr.at[a,b,c,pl.ds(0,n)],lambda a,b: arr.at[a,b,c,pl.ds(n,n)])
        line=Line(p,name+"_z",lambda a: arr.at[a,s,c],src)
        return spread,line
    q_spread,q_line=attention_weight("wq",wq_v,wq_in)
    o_spread,o_line=attention_weight("wo",wo_v,wo_in)
    def each(k, f):
        for at,when in p.steps[k]: f(at,when)
    def to_sibling(name, arr, a, when):
        ref=arr.at[a,:,c]
        p.send(ref,ref,name+"_c",a,p.to_core,None,when)
    others=((p.to_x,p.by_x),(p.to_y,p.by_y),(p.to_far,p.far))
    def swap(src,dst_of,name):
        for i,(t,o) in enumerate(others):
            p.send(src.at[o],dst_of(s),name,i,t)
    def swapped(dst_of,name):
        for i,(t,o) in enumerate(others):
            p.wait(dst_of(o),name,i)
    swap(gu_in,lambda b: gu.at[z,b,c],"gu")
    q_line.start()
    q_spread.start(z,wq_in)
    swap(tok,lambda b: x_v.at[b],"tok")
    for i,(t,o) in enumerate(others):
        p.send(marks.at[o],marks_v.at[c,s],"mk",i,t)
        p.send(marks.at[o],marks_v.at[c,s],"mk2",i,(z,o,1-c))
    p.send(marks.at[s],marks_v.at[c,s],"mk2",3,p.to_core)
    fwd=lambda a,here: q_spread.start(a,wq_v.at[a,s,c],(here,))
    gufwd=lambda a,here: to_sibling("gu",gu,a,(here,))
    ofwd=lambda a,here: o_spread.start(a,wo_v.at[a,s,c],(here,))
    gu_line=Line(p,"gu_z",lambda a: gu.at[a,:,c],gu.at[z,:,c])
    for cp in loads+late: cp.wait()
    out(b_cot,E.at[:,s]); out(b_gu,gu.at[z,s,c]); own_gu=outs_[-1]
    q_line.hop(1,fwd)
    q_line.hop(2,fwd)
    q_line.hop(3,fwd)
    swapped(lambda b: gu.at[z,b,c],"gu")
    own_gu.wait(); outs_[:]=[o for o in outs_ if o is not own_gu]
    gu_line.start(); to_sibling("gu",gu,z,())
    for k in range(4): each(k,lambda a,w: q_spread.relay(a,w))
    gu_line.hop(1,gufwd)
    o_line.start(); o_spread.start(z,wo_in)
    def each_q(a,w):
        q_spread.arrive(a,w); to_sibling("wq",wq_v,a,w)
    for k in range(4): each(k,each_q)
    swapped(lambda b: x_v.at[b],"tok")
    for i,(t,o) in enumerate(others):
        p.wait(marks_v.at[c,o],"mk",i); p.wait(marks_v.at[1-c,o],"mk2",i)
    p.wait(marks_v.at[1-c,s],"mk2",3)
    for a in range(4): p.wait(wq_v.at[a,:,1-c],"wq_c",a)
    out(x_v,x_out); out(marks_v,marks_out); out(wq_v,wq_out)
    e_parts=[]
    for i in range(2):
        def sub(lo,n,i=i): return lambda _,b: E.at[pl.ds(2*i+lo,n),b]
        e_parts.append(Spread(p,"E%d"%i,sub(0,2),sub(0,1),sub(1,1)))
    def e_start(i):
        for t,nm in ((p.to_x,"_x"),(p.to_y,"_y")):
            p.send(cot.at[pl.ds(2*i,2)],E.at[pl.ds(2*i,2),s],"E%d"%i+nm,0,t)
    for i in range(width//head_dim):
        a,b=divmod(i,4)
        block=wq_v[a,b,:,:,pl.ds(qkv,head_dim)].reshape(head_dim,head_dim).astype(F32)
        gain_v[:,pl.ds(i*head_dim,head_dim)]=jnp.transpose(block)[0:8]
    e_start(0); e_start(1)
    def norm_block(b,carry):
        x=x_v[b].astype(F32)
        inv=lax.rsqrt(jnp.mean(x*x,axis=-1,keepdims=True)+EPSILON)
        h1_v[pl.ds(b*tile,tile),:]=(x*inv*gain_v[0:1,:]).astype(BF16)
        return carry
    lax.fori_loop(0,chips,norm_block,0)
    lane=lax.broadcasted_iota(jnp.int32,(1,head_dim),1)
    sign=jnp.where(lane<head_dim//2,-1.0,1.0).astype(F32)
    seg_cols=[]
    for b in range(chips):
        m=jnp.transpose(marks_v[c,b].astype(F32))
        angle=m[:,1:2]*freq[...]
        cos_v[pl.ds(b*tile,tile),:]=jnp.cos(angle); sin_v[pl.ds(b*tile,tile),:]=jnp.sin(angle)*sign
        seg_cols.append(m[:,0:1])
    key_seg=jnp.concatenate([marks_v[k%2,k//2,0:1,:] for k in range(2*chips)],axis=1).astype(F32)
    o_line.hop(1,ofwd)
    w=wq_v[:,:,:,:,pl.ds(width,2*head_dim)].reshape(width,2*head_dim)
    kv=dot2(h1_v[...],w,1,0)
    kv=jnp.concatenate([turn(kv[:,:head_dim],cos_v[...],sin_v[...]),kv[:,head_dim:]],axis=1).astype(BF16)
    kv_v[:,pl.ds(c,1)]=kv.reshape(chips,1,tile,2*head_dim)
    p.send(kv_v.at[:,c],kv_v.at[:,c],"kv",0,p.to_core)
    swap(kv_v.at[:,c],lambda b: home.at[b],"home")
    out(kv_v.at[s,c],home.at[s]); out(cos_v,cos_out); out(sin_v,sin_out)
    steps={0:[lambda: o_line.hop(2,ofwd)],
           1:[lambda: p.wait(kv_v.at[:,1-c],"kv",0), lambda: o_line.hop(3,ofwd)],
           2:[lambda: each(0,lambda a,w: o_spread.relay(a,w)), lambda: each(1,lambda a,w: o_spread.relay(a,w))],
           3:[lambda: each(2,lambda a,w: o_spread.relay(a,w)), lambda: each(3,lambda a,w: o_spread.relay(a,w))],
           4:[]}
    def lin_group(g,carry):
        w=wq_v[:,:,:,:,pl.ds(pl.multiple_of(g*group,group),group)].reshape(width,group)
        lin_v[...]=dot2(h1_v[...],w,1,0)
        for b in range(chips):
            cos,sin=cos_v[pl.ds(b*tile,tile),:],sin_v[pl.ds(b*tile,tile),:]
            for h in range(heads):
                part=lin_v[pl.ds(b*tile,tile),pl.ds(h*head_dim,head_dim)]
                q_v[pl.ds(b*tile,tile),pl.ds(pl.multiple_of(g*group+h*head_dim,head_dim),head_dim)]=turn(part,cos,sin).astype(BF16)
        return carry
    for f in steps[0]: f()
    lax.fori_loop(0,groups,lin_group,0)
    for f in steps[1]: f()
    gu_line.hop(2,gufwd)
    out(kv_v,kv_out); out(q_v,q_out)
    def attend_group(g,carry):
        for b in range(chips):
            extent=(b+1)*2*tile
            at=lambda h: pl.ds(pl.multiple_of(g*group+h*head_dim,head_dim),head_dim)
            q=jnp.concatenate([q_v[pl.ds(b*tile,tile),at(h)] for h in range(heads)],axis=0)
            kvs=kv_v[pl.ds(0,b+1)].reshape(extent,2*head_dim)
            place=(2*b+c)*tile+lax.broadcasted_iota(jnp.int32,(tile,extent),0)
            seen=lax.broadcasted_iota(jnp.int32,(tile,extent),1)
            allowed=(place>=seen)&(seg_cols[b]==key_seg[:,:extent])
            bias=jnp.where(allowed,0.0,MASKED).astype(F32)
            sc=dot2(q,kvs[:,:head_dim],1,1)*scale
            sc=(sc.reshape(heads,tile,extent)+bias[None]).reshape(heads*tile,extent)
            top=jnp.max(sc,axis=-1,keepdims=True)
            e=jnp.exp(sc-top)
            soft=(e*(1.0/jnp.sum(e,axis=-1,keepdims=True))).astype(BF16)
            mixed=dot2(soft,kvs[:,head_dim:],1,0).astype(BF16)
            for h in range(heads):
                att_v[pl.ds(b*tile,tile),at(h)]=mixed[h*tile:(h+1)*tile]
        for i in (2,3):
            @pl.when(g==i-1)
            def _(i=i):
                for f in steps[i]: f()
        return carry
    lax.fori_loop(0,groups,attend_group,0)
    def each_o(a,w):
        o_spread.arrive(a,w); to_sibling("wo",wo_v,a,w)
    for k in range(4): each(k,each_o)
    for f in steps[4]: f()
    for a in range(4): p.wait(wo_v.at[a,:,1-c],"wo_c",a)
    out(wo_v,wo_out)
    def project(g,carry):
        at=pl.ds(pl.multiple_of(g*group,group),group)
        w=wo_v[:,:,:,:,at].reshape(width,group)
        lin_v[...]=dot2(att_v[...],w,1,0)
        for b in range(chips):
            mid_v[pl.ds(b*tile,tile),at]=x_v[b,:,at].astype(F32)+lin_v[pl.ds(b*tile,tile),:]
        return carry
    e_parts[0].relay(0)
    e_parts[1].relay(0)
    lax.fori_loop(0,groups,project,0)
    out(mid_v,middle_out)
    def norm_two(b,carry):
        at=pl.ds(pl.multiple_of(b*tile,tile),tile)
        m=mid_v[at,:]
        inv=lax.rsqrt(jnp.mean(m*m,axis=-1,keepdims=True)+EPSILON)
        two_v[at,:]=(m*inv*gain_v[1:2,:]).astype(BF16)
        return carry
    lax.fori_loop(0,chips,norm_two,0)
    out(two_v,two)
    for i in range(width//head_dim):
        at=slice(i*head_dim,(i+1)*head_dim)
        h1t_v[at,:]=jnp.transpose(h1_v[:,at])
        att_t_v[at,:]=jnp.transpose(att_v[:,at])
    out(h1t_v,h1_out); out(att_t_v,att_out)
    gu_line.hop(3,gufwd)
    e_parts[0].arrive(0)
    e_parts[1].arrive(0)
    for a in range(4): p.wait(gu.at[a,:,1-c],"gu_c",a)
    swapped(lambda b: home.at[b],"home")
    for cp in outs_: cp.wait()
    p.finish()
    assert len(p.groups)<=GROUPS, len(p.groups)

def front(tok,cot,marks,wq_in,wo_in,gu_in):
    Z,S,C=lax.axis_size(LINE),lax.axis_size(PLANE),lax.axis_size(CORE)
    sd=jax.ShapeDtypeStruct
    micro,tile,width=tok.shape
    rows=micro*tile
    head_dim=128
    group=512
    half=head_dim//2
    freq=jnp.exp(-jnp.log(jnp.float32(10000.0))*jnp.arange(half,dtype=F32)/half)
    freq=jnp.concatenate([freq,freq])[None]
    outs=[sd((S,tile,width),BF16),sd((C,)+marks.shape,jnp.int32),sd((Z,S,C)+wq_in.shape,BF16),sd((Z,S,C)+wo_in.shape,BF16),
          sd((Z,S,C)+gu_in.shape[1:],BF16),sd((S,)+cot.shape,BF16),
          sd((rows,width),BF16),sd((rows,width),F32),sd((width,rows),BF16),sd((rows,width),BF16),sd((width,rows),BF16),
          sd((S,C,tile,2*head_dim),BF16),sd((S,tile,2*head_dim),BF16),sd((rows,head_dim),F32),sd((rows,head_dim),F32)]
    anyspec=pl.BlockSpec(memory_space=pl.ANY)
    V=pltpu.VMEM
    return pl.pallas_call(functools.partial(front_kernel,(tile,width,head_dim,group)),out_shape=outs,
        in_specs=[anyspec]*6+[pl.BlockSpec(memory_space=V)],out_specs=[anyspec]*len(outs),
        scratch_shapes=[pltpu.SemaphoreType.DMA((GROUPS,4)),pltpu.SemaphoreType.DMA((GROUPS,4)),pltpu.SemaphoreType.DMA((32,)),
          V(cot.shape,BF16),V(gu_in.shape[1:],BF16),
          V((S,tile,width),BF16),V((C,)+marks.shape,jnp.int32),V((Z,S,C)+wq_in.shape,BF16),V((Z,S,C)+wo_in.shape,BF16),
          V((rows,width),BF16),V((rows,group),F32),V((rows,width),BF16),V((rows,width),BF16),V((S,C,tile,2*head_dim),BF16),
          V((rows,width),F32),V((rows,width),BF16),V((rows,head_dim),F32),V((rows,head_dim),F32),V((8,width),F32),V((width,rows),BF16),V((width,rows),BF16)],
        compiler_params=pltpu.CompilerParams(collective_id=1,has_side_effects=True,vmem_limit_bytes=60*1024*1024),cost_estimate=pl.CostEstimate(flops=20_000_000_000,bytes_accessed=100_000_000,transcendentals=10_000_000),name="front")(tok,cot,marks,wq_in,wo_in,gu_in,freq)


def back_kernel(
    plan,
    gh2,
    grads_in,
    middle,
    x_in,
    wq,
    wo,
    h1t_in,
    q_in,
    att_t_in,
    kv_in,
    cos_in,
    sin_in,
    marks_in,
    gain_v,
    home,
    gq_out,
    gkv_out,
    go_out,
    send_sem,
    recv_sem,
    local_sem,
    mid_v,
    gh1_v,
    x_v,
    proj_v,
    h1t_v,
    q_v,
    att_t_v,
    kv_v,
    cos_v,
    sin_v,
    marks_v,
    wo_b,
    wq_b,
    wk_v,
    mix_v,
    lin_v,
    kvacc,
    kvx,
    gains_acc,
    sq,
    so,
    rq,
    ro,
    tq,
    to,
    pq,
    po,
    uq,
    uo,
    zq,
    zo,
    skv,
    rkv,
    tkv,
    pkv,
    ukv,
    zkv,
    gl_v,
):
    tile, width, head_dim, group = plan
    scale = head_dim**-0.5
    chips, planes = 4, 4
    rows = chips * tile
    groups = width // group
    heads = group // head_dim
    shard = sq.shape[3]
    p = Post(send_sem, recv_sem)
    z, s, c = p.plane, p.own, p.core
    others = ((p.to_x, p.by_x), (p.to_y, p.by_y), (p.to_far, p.far))
    lines = [lax.rem(z + k, planes) for k in range(1, planes)]
    bar = pltpu.get_barrier_semaphore()

    def load(src, dst, index):
        return pltpu.make_async_copy(src, dst, local_sem.at[index])

    first = [
        load(gh2, q_v, 0),
        load(middle, mid_v, 1),
        load(grads_in.at[s], x_v, 2),
    ]
    second = [
        load(h1t_in, h1t_v, 3),
        load(att_t_in, att_t_v, 5),
        load(kv_in, kv_v, 6),
        load(cos_in, cos_v, 7),
        load(sin_in, sin_v, 8),
        load(marks_in, marks_v, 9),
        load(wq.at[:, :, :, :, pl.ds(width, 2 * head_dim)], wk_v, 10),
    ]
    tokens_again = load(x_in, x_v, 11)

    def fetch(g):
        at = pl.ds(pl.multiple_of(g * group, group), group)
        slot = lax.rem(g, 2)
        return (
            load(wo.at[g], wo_b.at[slot], 12 + slot),
            load(wq.at[:, :, :, :, at], wq_b.at[slot], 14 + slot),
        )

    for cp in first + second:
        cp.start()
    for cp in fetch(0):
        cp.start()
    for target in [t for t, _ in others] + [p.to_core] + [(a, s, c) for a in lines]:
        pl.semaphore_signal(bar, inc=1, device_id=target, device_id_type=MESH)
    pl.semaphore_wait(bar, 7)

    def stage_a(g):
        slot = lax.rem(g, 2)
        return (
            p.copy(sq.at[:, :, 1 - c], rq.at[slot], "aq", g, p.to_core),
            p.copy(so.at[:, 1 - c], ro.at[slot], "ao", g, p.to_core),
        )

    def stage_b(g):
        slot = lax.rem(g, 2)
        copies = []
        for i, (target, other) in enumerate(others):
            copies.append(p.copy(tq.at[slot, :, other], pq.at[g, i], "bq%d" % i, g, target))
            copies.append(p.copy(to.at[slot, other], po.at[g, i], "bo%d" % i, g, target))
        return copies

    def stage_c(g):
        slot = lax.rem(g, 2)
        return [
            p.copy(uq.at[slot, a], zq.at[g, k], "cq%d" % k, g, (a, s, c))
            for k, a in enumerate(lines)
        ]

    def stage_c_out(g, k):
        return p.copy(uo.at[lax.rem(g, 2)], zo.at[k], "co", k, (g, s, c))

    def wide(value):
        return value.astype(F32)

    def do_b(g):
        slot = lax.rem(g, 2)
        for cp in stage_a(g):
            cp.wait_recv()

        @pl.when(g >= 2)
        def _():
            for cp in stage_b(g - 2):
                cp.wait_send()

        def one(a, carry):
            tq[slot, a] = (wide(sq[a, :, c]) + wide(rq[slot, a])).astype(BF16)
            to[slot, a] = (wide(so[a, c]) + wide(ro[slot, a])).astype(BF16)
            return carry

        lax.fori_loop(0, planes, one, 0)
        for cp in stage_b(g):
            cp.start()

    def do_c(g):
        slot = lax.rem(g, 2)
        for cp in stage_b(g):
            cp.wait_recv()
        total = wide(tq[slot, :, s])
        mixed = wide(to[slot, s])
        for i in range(3):
            total = total + wide(pq[g, i])
            mixed = mixed + wide(po[g, i])
        uq[slot] = total.astype(BF16)
        uo[slot] = mixed.astype(BF16)
        for cp in stage_c(g):
            cp.start()
        for k in range(1, planes):

            @pl.when(lax.rem(g + planes - z, planes) == k)
            def _(k=k):
                stage_c_out(g, k - 1).start()

    def do_d(g):
        slot = lax.rem(g, 2)
        total = wide(uq[slot, z])
        for k, cp in enumerate(stage_c(g)):
            cp.wait_recv()
            total = total + wide(zq[g, k])
        gq_out[:, pl.ds(pl.multiple_of(g * group, group), group)] = total

        @pl.when(z == g)
        def _():
            mixed = wide(uo[slot])
            for k in range(planes - 1):
                stage_c_out(g, k).wait_recv()
                mixed = mixed + wide(zo[k])
            go_out[...] = mixed

        for k in range(1, planes):

            @pl.when(lax.rem(g + planes - z, planes) == k)
            def _(k=k):
                stage_c_out(g, k - 1).wait_send()

        for cp in stage_c(g):
            cp.wait_send()

    for cp in first:
        cp.wait()
    gains_acc[...] = jnp.zeros_like(gains_acc)

    def norm_two(b, carry):
        at = pl.ds(pl.multiple_of(b * tile, tile), tile)
        m = mid_v[at, :]
        inv = lax.rsqrt(jnp.mean(m * m, axis=-1, keepdims=True) + EPSILON)
        normed = m * inv
        grad = wide(q_v[at, :])
        gains_acc[1:2, :] += jnp.sum(grad * normed, axis=0, keepdims=True)
        grad = grad * gain_v[1:2, :]
        grad = wide(x_v[b]) + inv * (grad - normed * jnp.mean(grad * normed, axis=-1, keepdims=True))
        mid_v[at, :] = grad
        proj_v[at, :] = grad.astype(BF16)
        gh1_v[at, :] = jnp.zeros_like(grad)
        return carry

    lax.fori_loop(0, chips, norm_two, 0)
    tokens_again.start()
    queries = load(q_in, q_v, 4)
    queries.start()
    for cp in second + [queries]:
        cp.wait()
    kvacc[...] = jnp.zeros_like(kvacc)
    seg_cols = [jnp.transpose(marks_v[c, b].astype(F32))[:, 0:1] for b in range(chips)]
    key_seg = jnp.concatenate(
        [marks_v[k % 2, k // 2, 0:1, :] for k in range(2 * chips)], axis=1
    ).astype(F32)

    def one_group(g, carry):
        slot = lax.rem(g, 2)
        column = pl.multiple_of(g * group, group)
        for cp in fetch(g):
            cp.wait()

        @pl.when(g + 1 < groups)
        def _():
            for cp in fetch(g + 1):
                cp.start()

        w = wo_b[slot].reshape(group, width)
        mix_v[...] = dot2(proj_v[...], w, 1, 1).astype(BF16)
        for b in range(chips):
            extent = (b + 1) * 2 * tile
            at = pl.ds(b * tile, tile)
            kvs = kv_v[pl.ds(0, b + 1)].reshape(extent, 2 * head_dim)
            keys, values = kvs[:, :head_dim], kvs[:, head_dim:]
            place = (2 * b + c) * tile + lax.broadcasted_iota(jnp.int32, (tile, extent), 0)
            seen = lax.broadcasted_iota(jnp.int32, (tile, extent), 1)
            allowed = (place >= seen) & (seg_cols[b] == key_seg[:, :extent])
            bias = jnp.where(allowed, 0.0, MASKED).astype(F32)
            cosine, sine = cos_v[at, :], sin_v[at, :]
            for first_head in range(0, heads, 2):
                span = range(first_head, first_head + 2)
                q = jnp.concatenate(
                    [q_v[at, pl.ds(pl.multiple_of(column + h * head_dim, head_dim), head_dim)] for h in span],
                    axis=0,
                )
                grads = jnp.concatenate(
                    [mix_v[at, pl.ds(h * head_dim, head_dim)] for h in span], axis=0
                )
                scores = dot2(q, keys, 1, 1) * scale
                scores = (scores.reshape(2, tile, extent) + bias[None]).reshape(2 * tile, extent)
                top = jnp.max(scores, axis=-1, keepdims=True)
                soft = jnp.exp(scores - top)
                soft = soft * (1.0 / jnp.sum(soft, axis=-1, keepdims=True))
                grad_soft = dot2(grads, values, 1, 1)
                inner = jnp.sum(soft * grad_soft, axis=-1, keepdims=True)
                grad_scores = (soft * (grad_soft - inner)).astype(BF16)
                both = jnp.concatenate(
                    [dot2(grad_scores, q, 0, 0) * scale, dot2(soft.astype(BF16), grads, 0, 0)],
                    axis=1,
                )
                kvacc[pl.ds(0, b + 1)] += both.reshape(b + 1, 2, tile, 2 * head_dim)
                grad_q = dot2(grad_scores, keys, 1, 0) * scale
                for i, h in enumerate(span):
                    part = turn(grad_q[i * tile : (i + 1) * tile], cosine, -sine)
                    lin_v[at, pl.ds(h * head_dim, head_dim)] = part.astype(BF16)

        @pl.when(g >= 3)
        def _():
            do_c(g - 3)

        @pl.when(g >= 1)
        def _():
            do_b(g - 1)
            for cp in stage_a(g - 1):
                cp.wait_send()

        left = att_t_v[pl.ds(column, group), :]

        def weights(n, carry):
            at = pl.ds(pl.multiple_of(n * group, group), group)
            part = dot2(h1t_v[at, :], lin_v[...], 1, 0)
            sq[n] = part.astype(BF16).reshape(chips, 2, shard, group)
            part = dot2(left, proj_v[:, at], 1, 0)
            so[:, :, :, at] = part.astype(BF16).reshape(chips, 2, shard, group)
            return carry

        lax.fori_loop(0, planes, weights, 0)
        for cp in stage_a(g):
            cp.start()

        def inputs(n, carry):
            at = pl.ds(pl.multiple_of(n * group, group), group)
            gh1_v[:, at] += dot2(lin_v[...], wq_b[slot, n].reshape(group, group), 1, 1)
            return carry

        lax.fori_loop(0, planes, inputs, 0)

        return carry

    lax.fori_loop(0, groups, one_group, 0)

    to_other = p.copy(kvacc.at[:, 1 - c], kvx, "kx", 0, p.to_core)
    to_other.start()
    do_c(groups - 3)
    do_b(groups - 1)
    to_other.wait_recv()
    for b in range(chips):
        at = pl.ds(b * tile, tile)
        part = kvacc[b, c] + kvx[b]
        turned = turn(part[:, :head_dim], cos_v[at, :], -sin_v[at, :])
        gl_v[at, :] = jnp.concatenate([turned, part[:, head_dim:]], axis=1).astype(BF16)

    def last_inputs(n, carry):
        at = pl.ds(pl.multiple_of(n * group, group), group)
        gh1_v[:, at] += dot2(gl_v[...], wk_v[n].reshape(group, 2 * head_dim), 1, 1)
        part = dot2(h1t_v[at, :], gl_v[...], 1, 0).astype(BF16)
        skv[n, :, :, :, pl.ds(0, 2 * head_dim)] = part.reshape(chips, 2, shard, 2 * head_dim)
        return carry

    lax.fori_loop(0, planes, last_inputs, 0)
    tokens_again.wait()

    def norm_one(b, carry):
        at = pl.ds(pl.multiple_of(b * tile, tile), tile)
        x = wide(x_v[b])
        inv = lax.rsqrt(jnp.mean(x * x, axis=-1, keepdims=True) + EPSILON)
        normed = x * inv
        grad = gh1_v[at, :]
        gains_acc[0:1, :] += jnp.sum(grad * normed, axis=0, keepdims=True)
        grad = grad * gain_v[0:1, :]
        grad = mid_v[at, :] + inv * (
            grad - normed * jnp.mean(grad * normed, axis=-1, keepdims=True)
        )
        proj_v[at, :] = grad.astype(BF16)
        return carry

    lax.fori_loop(0, chips, norm_one, 0)
    for i in range(width // head_dim):
        part = gains_acc[:, pl.ds(i * head_dim, head_dim)]
        part = jnp.concatenate([part, jnp.zeros((head_dim - 8, head_dim), F32)], axis=0)
        part = jnp.transpose(part).astype(BF16).reshape(2, shard, head_dim)
        skv[i // 4, i % 4, :, :, pl.ds(2 * head_dim, head_dim)] = part
    a_kv = p.copy(skv.at[:, :, 1 - c], rkv, "akv", 0, p.to_core)
    a_kv.start()
    homes = [
        p.copy(proj_v.at[pl.ds(pl.multiple_of(o * tile, tile), tile)], home.at[s], "home", i, t)
        for i, (t, o) in enumerate(others)
    ]
    do_d(groups - 4)
    do_c(groups - 2)
    a_kv.wait_recv()

    def last_b(a, carry):
        tkv[a] = (wide(skv[a, :, c]) + wide(rkv[a])).astype(BF16)
        return carry

    lax.fori_loop(0, planes, last_b, 0)
    b_kv = [
        p.copy(tkv.at[:, o], pkv.at[i], "bkv", i, t) for i, (t, o) in enumerate(others)
    ]
    for cp in b_kv:
        cp.start()
    for cp in homes:
        cp.start()
    own_home = load(proj_v.at[pl.ds(pl.multiple_of(s * tile, tile), tile)], home.at[s], 0)
    own_home.start()
    do_d(groups - 3)
    do_c(groups - 1)
    do_d(groups - 2)
    total = wide(tkv[:, s])
    for i, cp in enumerate(b_kv):
        cp.wait_recv()
        total = total + wide(pkv[i])
    ukv[...] = total.astype(BF16)
    c_kv = [
        p.copy(ukv.at[a], zkv.at[k], "ckv", k, (a, s, c)) for k, a in enumerate(lines)
    ]
    for cp in c_kv:
        cp.start()
    do_d(groups - 1)
    total = wide(ukv[z])
    for k, cp in enumerate(c_kv):
        cp.wait_recv()
        total = total + wide(zkv[k])
    gkv_out[...] = total
    for cp in homes:
        cp.wait_recv()
    own_home.wait()
    for cp in [to_other, a_kv] + b_kv + c_kv + homes:
        cp.wait_send()
    for cp in list(stage_a(groups - 1)) + stage_b(groups - 2) + stage_b(groups - 1):
        cp.wait_send()


def back(tile, gh2, grads_in, middle, x_in, wq, wo, h1t, q, att_t, kv, cosine, sine, marks, gains):
    planes, chips, pair, shard, width = wo.shape
    rows = chips * tile
    head_dim = kv.shape[-1] // 2
    group = 512
    groups = width // group
    last = wq.shape[-1] - width
    V = pltpu.VMEM
    sd = jax.ShapeDtypeStruct
    outs = [
        sd((chips, tile, width), BF16),
        sd((shard, width), F32),
        sd((shard, last), F32),
        sd((shard, width), F32),
    ]
    anyspec = pl.BlockSpec(memory_space=pl.ANY)
    inner = pl.BlockSpec(memory_space=V)
    scratch = [
        pltpu.SemaphoreType.DMA((GROUPS, 4)),
        pltpu.SemaphoreType.DMA((GROUPS, 4)),
        pltpu.SemaphoreType.DMA((16,)),
        V((rows, width), F32),
        V((rows, width), F32),
        V((chips, tile, width), BF16),
        V((rows, width), BF16),
        V((width, rows), BF16),
        V((rows, width), BF16),
        V((width, rows), BF16),
        V((chips, pair, tile, 2 * head_dim), BF16),
        V((rows, head_dim), F32),
        V((rows, head_dim), F32),
        V(marks.shape, jnp.int32),
        V((2, chips, pair, shard, width), BF16),
        V((2, planes, chips, pair, shard, group), BF16),
        V((planes, chips, pair, shard, 2 * head_dim), BF16),
        V((rows, group), BF16),
        V((rows, group), BF16),
        V((chips, pair, tile, 2 * head_dim), F32),
        V((chips, tile, 2 * head_dim), F32),
        V((8, width), F32),
        V((planes, chips, pair, shard, group), BF16),
        V((chips, pair, shard, width), BF16),
        V((2, planes, chips, shard, group), BF16),
        V((2, chips, shard, width), BF16),
        V((2, planes, chips, shard, group), BF16),
        V((2, chips, shard, width), BF16),
        V((groups, 3, planes, shard, group), BF16),
        V((groups, 3, shard, width), BF16),
        V((2, planes, shard, group), BF16),
        V((2, shard, width), BF16),
        V((groups, 3, shard, group), BF16),
        V((3, shard, width), BF16),
        V((planes, chips, pair, shard, last), BF16),
        V((planes, chips, shard, last), BF16),
        V((planes, chips, shard, last), BF16),
        V((3, planes, shard, last), BF16),
        V((planes, shard, last), BF16),
        V((3, shard, last), BF16),
        V((rows, 2 * head_dim), BF16),
    ]
    return pl.pallas_call(
        functools.partial(back_kernel, (tile, width, head_dim, group)),
        out_shape=outs,
        in_specs=[anyspec] * 13 + [inner],
        out_specs=[anyspec] + [inner] * 3,
        scratch_shapes=scratch,
        compiler_params=pltpu.CompilerParams(
            collective_id=2, has_side_effects=True, vmem_limit_bytes=63 * 1024 * 1024
        ),
        cost_estimate=pl.CostEstimate(
            flops=1_000_000_000, bytes_accessed=1_000_000, transcendentals=0
        ),
        name="back",
    )(gh2, grads_in, middle, x_in, wq, wo, h1t, q, att_t, kv, cosine, sine, marks, gains)


def middle_kernel(
    plan,
    two_in,
    grads,
    gate_up,
    down,
    residual,
    two_out,
    pre_out,
    hidden_out,
    partial_out,
    sum_out,
    send_sem,
    recv_sem,
    local_sem,
    gu_v,
    down_v,
    res_b,
    out_b,
    two_v,
    e_v,
    pre_v,
    hidden_v,
    far_v,
    x_v,
    y_v,
    own_v,
    xa_far,
    xa_own,
    yb_far,
    yb_own,
    ya_pass,
    xb_pass,
):
    rows, width, hidden = plan
    half = width // 2
    wide_tile, out_tile = 256, 512
    tiles = width // out_tile
    p = Post(send_sem, recv_sem)
    low, high = pl.ds(0, half), pl.ds(half, half)
    top, bottom = pl.ds(0, rows // 2), pl.ds(rows // 2, rows // 2)
    order = (p.own, p.by_x, p.by_y, p.far)
    targets = (own_v, x_v, y_v, far_v)

    def load(src, dst, index):
        return pltpu.make_async_copy(src, dst, local_sem.at[index])

    def fetch(i):
        return load(grads.at[order[i]], e_v, 0)

    def keep_pre(i):
        at = pl.ds(pl.multiple_of(order[i] * rows, rows), rows)
        return load(pre_v, pre_out.at[at], 1)

    def keep_hidden(i):
        at = pl.ds(pl.multiple_of(order[i] * rows, rows), rows)
        return load(hidden_v.at[i], hidden_out.at[at], 2 + i)

    def keep_two(i):
        return load(two_v.at[order[i]], two_out.at[order[i]], 6 + i)

    def columns(n):
        return pl.ds(pl.multiple_of(n * out_tile, out_tile), out_tile)

    def residual_tile(n):
        return load(residual.at[:, columns(n)], res_b.at[lax.rem(n, 2)], 10 + lax.rem(n, 2))

    def place(i, n):
        slot = lax.rem(n, 2)
        return load(out_b.at[slot], partial_out.at[order[i], :, columns(n)], 12 + slot)

    weights = [load(gate_up, gu_v, 14), load(down, down_v, 15)]
    mine = load(two_in, two_v.at[p.own], 16)
    for cp in [mine, fetch(0)] + weights:
        cp.start()
    residual_tile(0).start()
    bar = pltpu.get_barrier_semaphore()
    for target in (p.to_x, p.to_y):
        pl.semaphore_signal(bar, inc=1, device_id=target, device_id_type=MESH)
    pl.semaphore_wait(bar, 2)
    sends = [
        p.copy(two_in, two_v.at[p.own], "two_x", 0, p.to_x),
        p.copy(two_in, two_v.at[p.own], "two_y", 0, p.to_y),
    ]
    relays = [
        p.copy(two_v.at[p.by_x, top], two_v.at[p.by_x, top], "two_l", 0, p.to_y),
        p.copy(two_v.at[p.by_y, bottom], two_v.at[p.by_y, bottom], "two_h", 0, p.to_x),
    ]
    for cp in sends:
        cp.start()
    for cp in weights + [mine]:
        cp.wait()

    def chunk(i, start, size):
        at, above = pl.ds(start, size), pl.ds(start + hidden, size)
        gate = dot2(two_v[order[i]], gu_v[:, at], 1, 0)
        up = dot2(two_v[order[i]], gu_v[:, above], 1, 0)
        grad = dot2(e_v[...], down_v[at, :], 1, 1)
        sig = jax.nn.sigmoid(gate)
        silu = gate * sig
        hidden_v[i, :, at] = (silu * up).astype(BF16)
        pre_v[:, at] = (grad * up * sig * (1.0 + gate * (1.0 - sig))).astype(BF16)
        pre_v[:, above] = (grad * silu).astype(BF16)

    whole_tiles = hidden // wide_tile
    x_low = p.copy(x_v.at[:, low], xa_own, "xa_own", 0, p.to_x)
    y_high = p.copy(y_v.at[:, high], yb_own, "yb_own", 0, p.to_y)
    far_low = p.copy(far_v.at[:, low], xa_far, "xa_far", 0, p.to_x)
    far_high = p.copy(far_v.at[:, high], yb_far, "yb_far", 0, p.to_y)
    x_high = p.copy(x_v.at[:, high], xb_pass, "xb_pass", 0, p.to_x)
    y_low = p.copy(y_v.at[:, low], ya_pass, "ya_pass", 0, p.to_y)
    for i in range(4):
        if i == 1:
            for cp, relay in zip(sends, relays):
                cp.wait_recv()
                relay.start()
        if i == 3:
            for relay in relays:
                relay.wait_recv()
        fetch(i).wait()
        keep_two(i).start()

        def step(j, carry, i=i):
            chunk(i, pl.multiple_of(j * wide_tile, wide_tile), wide_tile)
            return carry

        lax.fori_loop(0, whole_tiles, step, 0)
        if hidden % wide_tile:
            chunk(i, whole_tiles * wide_tile, hidden % wide_tile)
        if i < 3:
            fetch(i + 1).start()
        keep_pre(i).start()
        keep_hidden(i).start()

        def back_tile(n, carry, i=i):
            targets[i][:, columns(n)] = dot2(pre_v[...], gu_v[columns(n), :], 1, 1).astype(BF16)
            return carry

        lax.fori_loop(0, tiles, back_tile, 0)
        keep_pre(i).wait()
        for cp in ((), (x_low,), (y_high,), (far_low, far_high))[i]:
            cp.start()

    def output(i):
        def out_chunk(n, carry):
            @pl.when(n >= 2)
            def _():
                place(i, n - 2).wait()

            part = dot2(hidden_v[i], down_v[:, columns(n)], 1, 0)
            if i == 0:

                @pl.when(n + 1 < tiles)
                def _():
                    residual_tile(n + 1).start()

                residual_tile(n).wait()
                part = part + res_b[lax.rem(n, 2)]
            out_b[lax.rem(n, 2)] = part.astype(BF16)
            place(i, n).start()
            return carry

        lax.fori_loop(0, tiles, out_chunk, 0)
        place(i, tiles - 2).wait()
        place(i, tiles - 1).wait()

    for i in (0, 1, 2):
        output(i)
    far_high.wait_recv()
    x_v[:, high] = (x_v[:, high].astype(F32) + yb_far[...].astype(F32)).astype(BF16)
    x_high.start()
    far_low.wait_recv()
    y_v[:, low] = (y_v[:, low].astype(F32) + xa_far[...].astype(F32)).astype(BF16)
    y_low.start()
    output(3)
    for i in range(4):
        keep_hidden(i).wait()
        keep_two(i).wait()
    for cp in (x_low, y_low, y_high, x_high):
        cp.wait_recv()
    own_v[:, low] = (
        own_v[:, low].astype(F32) + xa_own[...].astype(F32) + ya_pass[...].astype(F32)
    ).astype(BF16)
    own_v[:, high] = (
        own_v[:, high].astype(F32) + yb_own[...].astype(F32) + xb_pass[...].astype(F32)
    ).astype(BF16)
    done = load(own_v, sum_out, 0)
    done.start()
    done.wait()
    for cp in sends + relays + [x_low, x_high, y_low, y_high, far_low, far_high]:
        cp.wait_send()


def middle_call(two, grads, gate_up, down, residual):
    chips = grads.shape[0]
    rows, width = two.shape
    hidden = down.shape[0]
    V = pltpu.VMEM
    sd = jax.ShapeDtypeStruct
    anyspec = pl.BlockSpec(memory_space=pl.ANY)
    block = (rows, width)
    part = (rows, width // 2)
    return pl.pallas_call(
        functools.partial(middle_kernel, (rows, width, hidden)),
        out_shape=[
            sd((chips,) + block, BF16),
            sd((chips * rows, 2 * hidden), BF16),
            sd((chips * rows, hidden), BF16),
            sd((chips,) + block, BF16),
            sd(block, BF16),
        ],
        in_specs=[anyspec] * 5,
        out_specs=[anyspec] * 5,
        scratch_shapes=[
            pltpu.SemaphoreType.DMA((10, 4)),
            pltpu.SemaphoreType.DMA((10, 4)),
            pltpu.SemaphoreType.DMA((17,)),
            V((width, 2 * hidden), BF16),
            V((hidden, width), BF16),
            V((2, rows, 512), F32),
            V((2, rows, 512), BF16),
            V((chips,) + block, BF16),
            V(block, BF16),
            V((rows, 2 * hidden), BF16),
            V((chips, rows, hidden), BF16),
        ]
        + [V(block, BF16)] * 4
        + [V(part, BF16)] * 6,
        compiler_params=pltpu.CompilerParams(
            collective_id=3, has_side_effects=True, vmem_limit_bytes=63 * 1024 * 1024
        ),
        cost_estimate=pl.CostEstimate(
            flops=80_000_000_000, bytes_accessed=60_000_000, transcendentals=10_000_000
        ),
        name="feed_forward",
    )(two, grads, gate_up, down, residual)


def trade_kernel(blocks, gate_out, up_out, got, send_sem, recv_sem, local_sem):
    chips, shard, columns = got.shape
    piece = columns // 8
    p = Post(send_sem, recv_sem)
    others = ((p.to_x, p.by_x), (p.to_y, p.by_y), (p.to_far, p.far))
    mine = pltpu.make_async_copy(blocks.at[p.own], got.at[p.own], local_sem.at[0])
    mine.start()
    bar = pltpu.get_barrier_semaphore()
    for target, _ in others:
        pl.semaphore_signal(bar, inc=1, device_id=target, device_id_type=MESH)
    pl.semaphore_wait(bar, 3)
    copies = [
        p.copy(blocks.at[o], got.at[p.own], "trade", i, t) for i, (t, o) in enumerate(others)
    ]
    for cp in copies:
        cp.start()
    mine.wait()
    for cp in copies:
        cp.wait_recv()
    for half, out in enumerate((gate_out, up_out)):
        parts = [
            got[chip, :, (half * 4 + plane) * piece : (half * 4 + plane + 1) * piece].astype(F32)
            for plane in range(4)
            for chip in range(chips)
        ]
        out[...] = jnp.concatenate(parts, axis=1)
    for cp in copies:
        cp.wait_send()


def trade(blocks, hidden):
    chips, shard, columns = blocks.shape
    V = pltpu.VMEM
    return pl.pallas_call(
        trade_kernel,
        out_shape=[jax.ShapeDtypeStruct((shard, hidden), F32)] * 2,
        in_specs=[pl.BlockSpec(memory_space=pl.ANY)],
        out_specs=[pl.BlockSpec(memory_space=V)] * 2,
        scratch_shapes=[
            V(blocks.shape, BF16),
            pltpu.SemaphoreType.DMA((1, 4)),
            pltpu.SemaphoreType.DMA((1, 4)),
            pltpu.SemaphoreType.DMA((1,)),
        ],
        compiler_params=pltpu.CompilerParams(
            collective_id=4, has_side_effects=True, vmem_limit_bytes=32 * 1024 * 1024
        ),
        name="trade",
    )(blocks)


class PlaneSum:
    def __init__(self, post, partial, column, buffers, local_sem):
        p = self.p = post
        self.x_v, self.y_v, self.own_v = buffers[:3]
        self.xa_far, self.xa_own, self.yb_far, self.yb_own, self.ya_pass, self.xb_pass = buffers[3:]
        half = self.xa_far.shape[-1]
        self.low, self.high = pl.ds(0, half), pl.ds(half, half)
        low, high, both = (
            pl.ds(column, half),
            pl.ds(column + half, half),
            pl.ds(column, 2 * half),
        )
        self.loads = [
            pltpu.make_async_copy(partial.at[:, chip, :, both], ref, local_sem.at[i])
            for i, (chip, ref) in enumerate(
                ((p.by_x, self.x_v), (p.by_y, self.y_v), (p.own, self.own_v))
            )
        ]
        self.far_low = p.copy(partial.at[:, p.far, :, low], self.xa_far, "xa_far", 0, p.to_x)
        self.far_high = p.copy(partial.at[:, p.far, :, high], self.yb_far, "yb_far", 0, p.to_y)
        self.x_low = p.copy(partial.at[:, p.by_x, :, low], self.xa_own, "xa_own", 0, p.to_x)
        self.y_high = p.copy(partial.at[:, p.by_y, :, high], self.yb_own, "yb_own", 0, p.to_y)
        self.x_high = p.copy(self.x_v.at[:, :, self.high], self.xb_pass, "xb_pass", 0, p.to_x)
        self.y_low = p.copy(self.y_v.at[:, :, self.low], self.ya_pass, "ya_pass", 0, p.to_y)

    def start(self):
        for cp in [self.far_low, self.far_high, self.x_low, self.y_high] + self.loads:
            cp.start()

    def turn(self):
        for cp in self.loads:
            cp.wait()
        self.far_high.wait_recv()
        total = self.x_v[:, :, self.high].astype(F32) + self.yb_far[...].astype(F32)
        self.x_v[:, :, self.high] = total.astype(BF16)
        self.x_high.start()
        self.far_low.wait_recv()
        total = self.y_v[:, :, self.low].astype(F32) + self.xa_far[...].astype(F32)
        self.y_v[:, :, self.low] = total.astype(BF16)
        self.y_low.start()

    def finish(self, out, sem):
        for cp in (self.x_low, self.y_low, self.y_high, self.x_high):
            cp.wait_recv()
        for at, direct, passed in (
            (self.low, self.xa_own, self.ya_pass),
            (self.high, self.yb_own, self.xb_pass),
        ):
            total = self.own_v[:, :, at].astype(F32) + direct[...].astype(F32)
            self.own_v[:, :, at] = (total + passed[...].astype(F32)).astype(BF16)
        done = pltpu.make_async_copy(self.own_v, out, sem)
        done.start()
        done.wait()
        for cp in (self.far_low, self.far_high, self.x_low, self.y_high, self.x_high, self.y_low):
            cp.wait_send()


def weight_grad_kernel(
    plan, left, right, partial, sum_out, rows_out, send_sem, recv_sem, local_sem, *scratch
):
    turned, width, tile, column = plan
    left_v, right_v, left_t, stage, got, total_v = scratch[:6]
    planes = got.shape[0]
    p = Post(send_sem, recv_sem)
    c = p.core
    plane_sum = PlaneSum(p, partial, column, scratch[6:], local_sem)
    load_left = pltpu.make_async_copy(left, left_v, local_sem.at[3])
    load_right = pltpu.make_async_copy(right, right_v, local_sem.at[4])
    load_left.start()
    load_right.start()
    bar = pltpu.get_barrier_semaphore()
    for target in (p.to_x, p.to_y, p.to_core):
        pl.semaphore_signal(bar, inc=1, device_id=target, device_id_type=MESH)
    pl.semaphore_wait(bar, 3)
    plane_sum.start()
    height = 1
    for size in stage.shape[1:-1]:
        height *= size
    rank = len(stage.shape) - 1
    own = (slice(None),) * (rank - 3) + (c,)
    other = (slice(None),) * (rank - 3) + (1 - c,)

    def to_core(z):
        return p.copy(stage.at[(z % 2,) + other], got.at[z], "core", z, p.to_core)

    def keep(z):
        return pltpu.make_async_copy(total_v.at[z % 2], sum_out.at[z], local_sem.at[5 + z % 2])

    def add(z):
        to_core(z).wait_recv()
        if z >= 2:
            keep(z - 2).wait()
        mine = stage[(z % 2,) + own].astype(F32)
        total_v[z % 2] = (mine + got[z].astype(F32)).astype(BF16)
        keep(z).start()

    load_left.wait()
    for z in range(planes):
        if z >= 2:
            to_core(z - 2).wait_send()
        start = z * height
        first = start // turned * turned
        last = -(-(start + height) // turned) * turned
        for at in range(first, last, turned):
            if at >= start or z == 0:
                left_t[pl.ds(at, turned), :] = jnp.transpose(left_v[:, at : at + turned])
        if z == 0:
            load_right.wait()

        def columns(n, carry, z=z, start=start):
            at = pl.ds(pl.multiple_of(n * tile, tile), tile)
            part = dot2(left_t[pl.ds(start, height), :], right_v[:, at], 1, 0).astype(BF16)
            stage[z % 2, ..., at] = part.reshape(stage.shape[1:-1] + (tile,))
            return carry

        lax.fori_loop(0, width // tile, columns, 0)
        to_core(z).start()
        if z >= 1:
            add(z - 1)
        if z == 2:
            plane_sum.turn()
    add(planes - 1)
    plane_sum.finish(rows_out, local_sem.at[7])
    for z in (planes - 2, planes - 1):
        keep(z).wait()
        to_core(z).wait_send()


def weight_grad(left, right, partial, block, tile, column, name, identity):
    planes = block[0]
    rows, height = left.shape
    width = right.shape[1]
    chips, tokens = partial.shape[0], partial.shape[2]
    half = partial.shape[3] // 4
    V = pltpu.VMEM
    anyspec = pl.BlockSpec(memory_space=pl.ANY)
    inner = block[1:]
    kept = inner[:-2] + inner[-1:]
    part = (chips, tokens, half)
    both = (chips, tokens, 2 * half)
    return pl.pallas_call(
        functools.partial(weight_grad_kernel, (128, width, tile, column)),
        out_shape=[
            jax.ShapeDtypeStruct((planes,) + kept + (width,), BF16),
            jax.ShapeDtypeStruct(both, BF16),
        ],
        in_specs=[anyspec] * 3,
        out_specs=[anyspec] * 2,
        scratch_shapes=[
            pltpu.SemaphoreType.DMA((7, 4)),
            pltpu.SemaphoreType.DMA((7, 4)),
            pltpu.SemaphoreType.DMA((8,)),
            V(left.shape, BF16),
            V(right.shape, BF16),
            V((height, rows), BF16),
            V((2,) + inner + (width,), BF16),
            V((planes,) + kept + (width,), BF16),
            V((2,) + kept + (width,), BF16),
        ]
        + [V(both, BF16)] * 3
        + [V(part, BF16)] * 6,
        compiler_params=pltpu.CompilerParams(
            collective_id=identity, has_side_effects=True, vmem_limit_bytes=62 * 1024 * 1024
        ),
        cost_estimate=pl.CostEstimate(
            flops=2 * rows * height * width, bytes_accessed=40_000_000, transcendentals=0
        ),
        name=name,
    )(left, right, partial)


def body_plane(
    tokens,
    cotangent,
    segments,
    positions,
    w_query,
    w_key,
    w_value,
    w_out,
    w_gate,
    w_up,
    w_down,
    gain_attn,
    gain_mlp,
):
    micro, tile, width = tokens.shape
    head_dim = w_key.shape[1]
    head_count = width // head_dim
    planes = lax.axis_size(LINE)
    chips = lax.axis_size(PLANE)
    pair = lax.axis_size(CORE)
    plane = lax.axis_index(LINE)
    own = lax.axis_index(PLANE)
    core = lax.axis_index(CORE)
    rows = micro * tile
    hidden = w_gate.shape[1]
    shard = w_query.shape[0]
    own_hidden = hidden // chips
    piece = own_hidden // planes
    qkv = width + 2 * head_dim
    score_scale = 1.0 / math.sqrt(head_dim)

    gains = jnp.stack([gain_attn, gain_mlp], axis=1)
    gains = jnp.pad(gains, ((0, 0), (0, head_dim - 2)))
    w_in = jnp.concatenate([w_query, w_key, w_value, gains], axis=1)
    gate_up = jnp.stack([w_gate, w_up], axis=1).reshape(shard, 2, planes, chips, piece)
    gate_up = gate_up.transpose(3, 0, 1, 2, 4).reshape(chips, shard, 2 * own_hidden)
    marks = jnp.pad(jnp.stack([segments, positions], axis=1), ((0, 0), (0, 6), (0, 0)))
    (
        x_rows,
        marks,
        w_qkv,
        out_mat,
        gate_up,
        grads_in,
        hidden_two,
        middle,
        hidden_one,
        queries,
        attended,
        kv,
        kv_home,
        cosine,
        sine,
    ) = front(tokens, cotangent, marks, w_in, w_out, gate_up)
    gains = jnp.pad(w_qkv[..., qkv : qkv + 2].reshape(width, 2).T, ((0, 6), (0, 0))).astype(F32)
    gate_up = gate_up.reshape(width, 2 * own_hidden)
    down_mat = lax.all_gather(w_down, (LINE, CORE), axis=0, tiled=True)
    plane_grads = grads_in.reshape(chips * rows, width)

    plane_two, grad_pre, hidden_mlp, partial_out, grad_hidden_two = middle_call(
        hidden_two,
        grads_in.reshape(chips, rows, width),
        gate_up,
        down_mat,
        middle,
    )
    plane_two = plane_two.reshape(chips * rows, width)
    partial_out = partial_out.reshape(chips, chips, tile, width)
    grad_down, rows_low = weight_grad(
        hidden_mlp,
        plane_grads,
        partial_out,
        (planes, pair, piece // pair),
        512,
        0,
        "down_grad",
        6,
    )
    grad_down, grad_pre = lax.optimization_barrier((grad_down, grad_pre))
    grad_gate_up, rows_high = weight_grad(
        plane_two,
        grad_pre,
        partial_out,
        (planes, chips, pair, shard),
        256,
        width // 2,
        "gate_up_grad",
        5,
    )
    layer_rows = jnp.concatenate([rows_low, rows_high], axis=-1)
    grad_down = scatter_sum(grad_down, LINE, 0).reshape(-1, width).astype(F32)
    grad_gate_up = scatter_sum(grad_gate_up, LINE, 0).reshape(chips, shard, 2 * own_hidden)

    grad_input, grad_q, grad_kv, grad_out = back(
        tile,
        grad_hidden_two,
        grads_in,
        middle,
        x_rows,
        w_qkv,
        out_mat,
        hidden_one,
        queries,
        attended,
        kv,
        cosine,
        sine,
        marks,
        gains,
    )
    grad_gate, grad_up = trade(grad_gate_up, hidden)
    return (
        layer_rows,
        kv_home[..., :head_dim],
        kv_home[..., head_dim:],
        grad_input.astype(F32),
        grad_q,
        grad_kv[:, :head_dim],
        grad_kv[:, head_dim : 2 * head_dim],
        grad_out,
        grad_gate,
        grad_up,
        grad_down,
        grad_kv[:, 2 * head_dim],
        grad_kv[:, 2 * head_dim + 1],
    )


def body(tokens, *rest):
    if tokens.shape[0] == lax.axis_size(PLANE) == 4 and lax.axis_size(CORE) == 2:
        return body_plane(tokens, *rest)
    return body_general(tokens, *rest)


def solution(mesh):
    in_specs = (
        P(None, EVERY, None),
        P(None, EVERY, None),
        P(None, EVERY),
        P(None, EVERY),
        P(EVERY, None),
        P(EVERY, None),
        P(EVERY, None),
        P(EVERY, None),
        P(EVERY, None),
        P(EVERY, None),
        P(EVERY, None),
        P(EVERY),
        P(EVERY),
    )
    out_specs = (
        P(None, EVERY, None),
        P(None, EVERY, None),
        P(None, EVERY, None),
        P(None, EVERY, None),
        P(EVERY, None),
        P(EVERY, None),
        P(EVERY, None),
        P(EVERY, None),
        P(EVERY, None),
        P(EVERY, None),
        P(EVERY, None),
        P(EVERY),
        P(EVERY),
    )
    return jax.shard_map(body, mesh=mesh, in_specs=in_specs, out_specs=out_specs, check_vma=False)
```
